128 devices in a mesh: lat: 8 (over y, core), lon: 16 (over x, z).
Axes of the slice: x: 4, y: 4, z: 4, core: 2. Of those that a mesh axis runs over, the one named last changes fastest.
Arguments:
- transport: float32 [4, 36, 256, 2048], P(None, None, 'lat', 'lon'), may hold values from 0.03 to 0.24
- mixing: float32 [35, 256, 2048], P(None, 'lat', 'lon'), may hold values from 0.05 to 5
- trajectory: bfloat16 [4, 3, 36, 256, 2048], P(None, None, None, 'lat', 'lon'), may hold values from -6 to 6
- kernel_table: float32 [64, 36], replicated, may hold values from 0 to 0.5
- track_tile: int32 [4, 65536, 1], P(None, ('lat', 'lon')), may hold values from 0 to 127; in each aligned block of 512 rows (0 to 511, 512 to 1023, ..., all dimensions but the last counted through in order) at most 8 rows name the same one
- sound_cell: int32 [4, 65536], P(None, ('lat', 'lon')), may hold values from 0 to 4095
- kernel_index: int32 [4, 65536], P(None, ('lat', 'lon')), may hold values from 0 to 63
- observed: float32 [4, 3, 65536], P(None, None, ('lat', 'lon')), may hold values from -8 to 8
- precision: float32 [4, 65536], P(None, ('lat', 'lon')), may hold values from 0.3 to 3
Outputs:
- adjoint_field: float32 [3, 36, 256, 2048], P(None, None, 'lat', 'lon')
- flux_grad: float32 [3, 256, 2048], P(None, 'lat', 'lon')
The draws below stay inside these ranges and needn't reach their ends.
Inputs may be any that keep to these rules, and one draw needn't show every extreme that they name: `track_tile`: within one step, the soundings held by one device name any one tile at most 8 times, and some device names some tile exactly 8 times.
All inputs are finite; a program needn't handle non-finite values.
Results may differ from the reference program's by a relative error of at most 0.0003.
Values may be sent and summed in bfloat16 or wider, within the bound.
No kernel may reach another device: no remote copies, remote signals or barrier semaphores. Data moves between devices by JAX's collectives and lax.ppermute only.
A program may use at most 128 MiB of HBM per device.

```python
import math
import jax
import jax.numpy as jnp
import numpy as np

TRACERS = 3
LEV = 36
NKER = 64
STEPS = 4
LATC = 32
LONC = 128
SND_DEV = 512
NTILES = 128
CAP = 8
NLAT = 256
NLON = 2048
SOUNDINGS = 65536
N_LON = 16


def place_ends(values, rng, smallest, largest):
    index_at = [jax.random.randint(jax.random.fold_in(rng, axis), (), 0, length) for axis, length in enumerate(values.shape)]
    widest = values.shape.index(max(values.shape))
    next_to = index_at[:widest] + [(index_at[widest] + 1) % values.shape[widest]] + index_at[widest + 1:]
    return values.at[tuple(index_at)].set(smallest).at[tuple(next_to)].set(largest)


def levels(stream_key, dims, shards, low, high):
    loudness, own = 1.0, jax.random.fold_in(stream_key, 6)
    for position, blocks in shards:
        draws = jnp.exp(jax.random.uniform(jax.random.fold_in(own, position), (blocks,), jnp.float32, low / len(shards), high / len(shards)))
        loudness = loudness * jnp.repeat(draws, dims[position] // blocks).reshape([-1 if axis == position else 1 for axis in range(len(dims))])
    return loudness


def routed_block(key, own, number, rows, count, top, limit, lean):
    order = jax.random.permutation(key, count)
    heavy_load, ordinary = shares(count, rows * top, limit, lean, True), shares(count, rows * top, limit, lean, False)
    places = jnp.arange(count)

    def named(sizes, rotation):
        used = int((sizes > 0).sum())
        fixed = max(1, used // 4)
        shifted = fixed + (places - fixed + rotation * (used - fixed)) % max(1, count - fixed)
        return jnp.zeros((count,), jnp.int32).at[order[jnp.where(places < fixed, places, shifted)]].set(jnp.asarray(sizes, jnp.int32))

    sizes = jnp.where(number % 4 == 0, named(heavy_load, number // 4), named(ordinary, number - number // 4 - 1))
    mixed = jax.random.permutation(jax.random.fold_in(own, 3), count)
    donor, taker = mixed[0:count // 2 * 2:2], mixed[1:count // 2 * 2:2]
    room = jnp.minimum(sizes[donor] - 1, limit - sizes[taker]) // 2
    room = jnp.where((donor == order[0]) | (taker == order[0]) | (sizes[taker] == 0), 0, jnp.maximum(room, 0))
    shifted = jax.random.randint(jax.random.fold_in(own, 4), (count // 2,), 0, 1 << 20) % (room + 1)
    sizes = sizes.at[donor].add(-shifted).at[taker].add(shifted)
    members = jnp.searchsorted(jnp.cumsum(sizes), jnp.arange(rows * top), side="right").astype(jnp.int32)
    table = members.reshape(top, rows).T
    table = table[jax.random.permutation(jax.random.fold_in(own, 1), rows)]
    rotation = jax.random.randint(jax.random.fold_in(own, 2), (rows, 1), 0, top)
    return jnp.take_along_axis(table, (jnp.arange(top)[None, :] + rotation) % top, axis=1)


def shares(amount, total, most, slope, full):
    loads = [(1 << 20) // math.isqrt(grade ** slope) + 1 for grade in range(1, amount + 1)]
    largest = most if full else min(most, max(-(-total // amount), total * loads[0] // sum(loads)))
    least = 1 if total - largest >= amount - 1 else 0
    holding, spare = [largest] + [least] * (amount - 1), total - largest - least * (amount - 1)
    while spare > 0:
        candidates = [i for i in range(1, amount) if holding[i] < largest] or [i for i in range(1, amount) if holding[i] < most]
        whole, remaining = sum([loads[i] for i in candidates]), spare
        for i in candidates:
            extra = min(most - holding[i], max(1, remaining * loads[i] // whole), spare)
            holding[i] = holding[i] + extra
            spare = spare - extra
    return np.array(holding)


def bell_draw(own_key, extent, width, reach, cuts=(), dtype=jnp.bfloat16):
    values = jax.random.normal(own_key, extent, jnp.float32) * width
    if len(cuts) > 0:
        values = levels(own_key, extent, cuts, -0.22, 0.18) * values
    return jnp.clip(values, min=-reach, max=reach).astype(dtype)


def setup_inputs(seed: int = 0) -> dict:
    keys = jax.random.split(jax.random.key(seed), 10)
    transport = jnp.clip(0.03 + 0.21 * jax.random.uniform(keys[0], (4, LEV, NLAT, NLON), jnp.float32) ** levels(keys[0], (4, LEV, NLAT, NLON), ((2, 8), (3, 16)), -0.2, 0.2), 0.03, 0.24)
    mixing = jnp.clip(jnp.exp(math.log(5.0) - 4.6051702 * jax.random.uniform(keys[1], (LEV - 1, NLAT, NLON), jnp.float32) ** levels(keys[1], (LEV - 1, NLAT, NLON), ((1, 8), (2, 16)), -0.2, 0.2)), 0.05, 5.0)
    trajectory = bell_draw(keys[2], (STEPS, TRACERS, LEV, NLAT, NLON), 1.0, 6.0, ((3, 8), (4, 16)))
    kernel_table = jnp.clip(jax.random.uniform(keys[3], (NKER, LEV), jnp.float32, 0.0, 0.5), 0.0, 0.5)
    track_tile_keys = jax.random.split(jax.random.fold_in(keys[4], 1), STEPS * SOUNDINGS // SND_DEV)
    track_tile_turns = jax.random.permutation(jax.random.fold_in(keys[4], 3), STEPS * SOUNDINGS // SND_DEV)
    track_tile = jax.vmap(lambda own, number: routed_block(jax.random.fold_in(keys[4], 2), own, number, SND_DEV, NTILES, 1, CAP, 2))(track_tile_keys, track_tile_turns).reshape((STEPS, SOUNDINGS, 1))
    sound_cell = place_ends(jax.random.randint(keys[5], (STEPS, SOUNDINGS), 0, LATC * LONC), jax.random.fold_in(keys[5], 1), 0, (LATC * LONC) - 1).astype(jnp.int32)
    kernel_index = place_ends(jax.random.randint(keys[6], (STEPS, SOUNDINGS), 0, NKER), jax.random.fold_in(keys[6], 1), 0, NKER - 1).astype(jnp.int32)
    observed = bell_draw(keys[7], (STEPS, TRACERS, SOUNDINGS), 2.0, 8.0, ((2, 128),), jnp.float32)
    precision = jnp.clip(jnp.exp(math.log(3.0) - 2.3025851 * jax.random.uniform(keys[8], (STEPS, SOUNDINGS), jnp.float32) ** levels(keys[8], (STEPS, SOUNDINGS), ((1, 128),), -0.2, 0.2)), 0.3, 3.0)
    return {"transport": transport, "mixing": mixing, "trajectory": trajectory, "kernel_table": kernel_table, "track_tile": track_tile, "sound_cell": sound_cell, "kernel_index": kernel_index, "observed": observed, "precision": precision}


def vertical_setup(mixing):
    layers = mixing.shape[0] + 1
    diag_list = []
    for height in range(layers):
        diag_entry = jnp.ones_like(mixing[0])
        if height > 0:
            diag_entry = diag_entry + mixing[height - 1]
        if height < layers - 1:
            diag_entry = diag_entry + mixing[height]
        diag_list.append(diag_entry)
    inverse = [1.0 / diag_list[0]]
    upper_terms = [-mixing[0] * inverse[0]]
    for height in range(1, layers):
        denom_val = diag_list[height] + mixing[height - 1] * upper_terms[height - 1]
        inverse.append(1.0 / denom_val)
        if height < layers - 1:
            upper_terms.append(-mixing[height] * inverse[height])
    return upper_terms, inverse


def vertical_solve(field, mixing, upper_terms, inverse):
    layers = field.shape[1]
    forward = [field[:, 0] * inverse[0]]
    for height in range(1, layers):
        forward.append((field[:, height] + mixing[height - 1] * forward[height - 1]) * inverse[height])
    result = [forward[layers - 1]]
    for height in range(layers - 2, -1, -1):
        result.append(forward[height] - upper_terms[height] * result[-1])
    return jnp.stack(result[::-1], axis=1)


def horizontal(field, transport):
    center = 1.0 - transport[0] - transport[1] - transport[2] - transport[3]
    east_term = jnp.roll(transport[0] * field, 1, axis=-1)
    west_term = jnp.roll(transport[1] * field, -1, axis=-1)
    north_val = transport[2] * field
    south_val = transport[3] * field
    zero_row = jnp.zeros_like(north_val[..., :1, :])
    north_term = jnp.concatenate([zero_row, north_val[..., :-1, :]], axis=-2)
    south_term = jnp.concatenate([south_val[..., 1:, :], zero_row], axis=-2)
    return center * field + east_term + west_term + north_term + south_term


def reference(transport, mixing, trajectory, kernel_table, track_tile, sound_cell, kernel_index, observed, precision):
    tiles = track_tile[..., 0]
    grid_row = (tiles // N_LON) * LATC + sound_cell // LONC
    grid_col = (tiles % N_LON) * LONC + sound_cell % LONC
    column_of = (grid_row * NLON + grid_col).astype(jnp.int32)
    upper_terms, inverse = vertical_setup(mixing)
    adjoint = jnp.zeros((TRACERS, LEV, NLAT, NLON), jnp.float32)
    flux = jnp.zeros((TRACERS, NLAT, NLON), jnp.float32)
    for step_no in range(STEPS - 1, -1, -1):
        flat_bg = trajectory[step_no].reshape(TRACERS, LEV, NLAT * NLON)
        sampled = jnp.take(flat_bg, column_of[step_no], axis=2).astype(jnp.float32)
        weights = kernel_table[kernel_index[step_no]].T
        model = jnp.sum(weights[None] * sampled, axis=1)
        scaled = (model - observed[step_no]) * precision[step_no][None, :]
        force = (weights[None] * scaled[:, None, :]).reshape(TRACERS * LEV, -1)
        forcing = jnp.zeros((TRACERS * LEV, NLAT * NLON), jnp.float32).at[:, column_of[step_no]].add(force)
        adjoint = adjoint + forcing.reshape(TRACERS, LEV, NLAT, NLON)
        adjoint = horizontal(vertical_solve(adjoint, mixing, upper_terms, inverse), transport)
        flux = flux + adjoint[:, 0]
    return adjoint, flux
```

```python
import functools

import jax
import jax.numpy as jnp
from jax import lax
from jax.experimental import pallas as pl
from jax.experimental.pallas import tpu as pltpu
from jax.sharding import PartitionSpec as P

CAP = 8
WORDS = 5
F32 = jnp.float32
BF16 = jnp.bfloat16


def split3(x):
    hi = x.astype(BF16)
    rest = x - hi.astype(F32)
    mid = rest.astype(BF16)
    return hi, mid, (rest - mid.astype(F32)).astype(BF16)


def split2(x):
    hi = x.astype(BF16)
    return hi, (x - hi.astype(F32)).astype(BF16)


def dot(a, b):
    return jnp.dot(a, b, preferred_element_type=F32)


def dot_t(a, b):
    return lax.dot_general(a, b, (((1,), (1,)), ((), ())), preferred_element_type=F32)


def call(kernel, outs, *args, scratch=(), vmem=24 << 20):
    return pl.pallas_call(
        kernel,
        out_shape=outs,
        in_specs=[pl.BlockSpec(memory_space=pltpu.VMEM)] * len(args),
        out_specs=jax.tree.map(lambda _: pl.BlockSpec(memory_space=pltpu.VMEM), outs),
        scratch_shapes=list(scratch),
        compiler_params=pltpu.CompilerParams(vmem_limit_bytes=vmem),
    )(*args)


def sds(*shape, dtype=F32):
    return jax.ShapeDtypeStruct(shape, dtype)


def route_kernel(tile_ref, cell_ref, index_ref, obs_ref, prec_ref, out_ref):
    steps, count = tile_ref.shape
    ntiles = out_ref.shape[0]
    tile_ids = lax.broadcasted_iota(jnp.int32, (ntiles, count), 0)
    before = (
        lax.broadcasted_iota(jnp.int32, (count, count), 0)
        < lax.broadcasted_iota(jnp.int32, (count, count), 1)
    ).astype(F32).astype(BF16)
    rank_ids = lax.broadcasted_iota(jnp.int32, (CAP, count), 0)
    pad = jnp.zeros((64 - CAP * WORDS, count), F32)
    half = jnp.zeros((64, count), F32)
    for pair in range(steps // 2):
        total = None
        for side in range(2):
            s = 2 * pair + side
            mine = tile_ids == tile_ref[s : s + 1, :]
            mine_f = mine.astype(F32)
            mine_b = mine_f.astype(BF16)
            seen = dot(mine_b, before)
            rank = jnp.sum(mine_f * seen, axis=0, keepdims=True).astype(jnp.int32)
            at_rank = rank_ids == rank
            code = (index_ref[s : s + 1, :] * 4096 + cell_ref[s : s + 1, :]).astype(F32)
            words = [code] + [obs_ref[s, t : t + 1, :] for t in range(3)] + [prec_ref[s : s + 1, :]]
            rows = [jnp.where(at_rank, w, 0.0) for w in words]
            block = jnp.concatenate(rows + [pad] + [half], axis=0)
            if side == 1:
                block = jnp.concatenate([half] + rows + [pad], axis=0)
            for part in split3(block):
                term = dot_t(mine_b, part)
                total = term if total is None else total + term
        out_ref[:, pair, :] = total


def unpack_kernel(got_ref, out_ref):
    ntiles = got_ref.shape[0]
    for pair in range(2):
        turned = got_ref[:, pair, :].T
        for side in range(2):
            s = 2 * pair + side
            base = 64 * side
            code = turned[base : base + CAP, :].astype(jnp.int32)
            kidx = code // 4096
            cell = code - kidx * 4096
            row = cell // 128
            col = cell - row * 128
            hi = row // 16
            fields = [hi * 128 + col, row - hi * 16, kidx]
            fields = [f.astype(F32) for f in fields]
            fields += [turned[base + CAP * w : base + CAP * (w + 1), :] for w in range(1, WORDS)]
            for f, value in enumerate(fields):
                for r in range(CAP):
                    out_ref[s, f : f + 1, r * ntiles : (r + 1) * ntiles] = value[r : r + 1, :]
            out_ref[s, 7:8, :] = jnp.zeros((1, CAP * ntiles), F32)


def forcing_kernel(s, chunk, snd_ref, traj_ref, table_ref, out_ref, pick, weight, scaled):
    tracers, layers = out_ref.shape[:2]
    slots = snd_ref.shape[2]
    nker = table_ref.shape[1]
    cell_ids = lax.broadcasted_iota(jnp.int32, (256, chunk), 0).astype(F32)
    low_ids = lax.broadcasted_iota(jnp.int32, (16, chunk), 0).astype(F32)
    ker_ids = lax.broadcasted_iota(jnp.int32, (nker, chunk), 0).astype(F32)
    table = split3(table_ref[...])
    for c in range(slots // chunk):
        at = pl.ds(c * chunk, chunk)
        pick[:, at] = jnp.where(cell_ids == snd_ref[s, 0:1, at], 1.0, 0.0).astype(BF16)
        low = jnp.where(low_ids == snd_ref[s, 1:2, at], 1.0, 0.0)
        ker = jnp.where(ker_ids == snd_ref[s, 2:3, at], 1.0, 0.0).astype(BF16)
        w = dot(table[0], ker) + dot(table[1], ker) + dot(table[2], ker)
        for k in range(layers):
            weight[k, :, at] = w[k : k + 1, :] * low

    def per_tracer(t, _):
        lhs = jnp.concatenate(
            [
                traj_ref[s, t, :, 0:16, :].reshape(layers * 16, 128),
                traj_ref[s, t, :, 16:32, :].reshape(layers * 16, 128),
            ],
            axis=1,
        )
        force = None
        for c in range(slots // chunk):
            at = pl.ds(c * chunk, chunk)
            sampled = dot(lhs, pick[:, at]).reshape(layers, 16, chunk)
            model = jnp.sum(jnp.sum(sampled * weight[:, :, at], axis=0), axis=0, keepdims=True)
            sc = (model - snd_ref[s, pl.ds(3 + t, 1), at]) * snd_ref[s, 6:7, at]
            hi, lo = split2((weight[:, :, at] * sc).reshape(layers * 16, chunk))
            term = dot_t(hi, pick[:, at]) + dot_t(lo, pick[:, at])
            force = term if force is None else force + term
        out_ref[t, :, 0:16, :] = force[:, 0:128].reshape(layers, 16, 128)
        out_ref[t, :, 16:32, :] = force[:, 128:256].reshape(layers, 16, 128)
        return 0

    lax.fori_loop(0, tracers, per_tracer, 0)


def setup_kernel(mix_ref, inv_ref, up_ref):
    layers = inv_ref.shape[0]
    for k in range(layers):
        diag = jnp.ones_like(mix_ref[0])
        if k > 0:
            diag = diag + mix_ref[k - 1]
        if k < layers - 1:
            diag = diag + mix_ref[k]
        if k > 0:
            diag = diag + mix_ref[k - 1] * up
        inv = 1.0 / diag
        inv_ref[k] = inv
        if k < layers - 1:
            up = -mix_ref[k] * inv
            up_ref[k] = up


def halo_add(value, t, k, layers, lon, north_ref, south_ref):
    lane = lax.broadcasted_iota(jnp.int32, value.shape, 1)
    turned = pltpu.roll(lon[t], lax.rem(255 - 2 * k, 128), axis=1)
    value = value + jnp.where((lane == 0) | (lane == 127), turned, 0.0)
    row = lax.broadcasted_iota(jnp.int32, (8, 128), 0)
    at = pl.ds(t * layers + k, 1)
    top = value[0:8] + jnp.where(row == 0, north_ref[at, :], 0.0)
    low = value[24:32] + jnp.where(row == 7, south_ref[at, :], 0.0)
    return jnp.concatenate([top, value[8:24], low], axis=0)


def lon_merge(east_ref, west_ref, lon):
    lane = lax.broadcasted_iota(jnp.int32, east_ref.shape, 2)
    lon[...] = jnp.where(lane % 2 == 0, east_ref[...], west_ref[...])


def step_body(base, force_ref, mix_ref, inv_ref, up_ref, tr_ref, mask_ref, outs, v):
    w_out, lon_out, north_out, south_out = outs
    tracers, layers = force_ref.shape[:2]
    d = tuple((force_ref[t, 0] + base(t, 0)) * inv_ref[0] for t in range(tracers))
    for t in range(tracers):
        v[t, 0] = d[t]

    def forward(k, d):
        m, inv = mix_ref[k - 1], inv_ref[k]
        d = tuple((force_ref[t, k] + base(t, k) + m * d[t]) * inv for t in range(tracers))
        for t in range(tracers):
            v[t, k] = d[t]
        return d

    d = lax.fori_loop(1, layers, forward, d, unroll=5)

    def backward(i, x):
        k = layers - 2 - i
        u = up_ref[k]
        x = tuple(v[t, k] - u * x[t] for t in range(tracers))
        for t in range(tracers):
            v[t, k] = x[t]
        return x

    lax.fori_loop(0, layers - 1, backward, d, unroll=5)

    lane = lax.broadcasted_iota(jnp.int32, (32, 128), 1)
    row = lax.broadcasted_iota(jnp.int32, (32, 128), 0)
    lon_out[...] = jnp.zeros(lon_out.shape, F32)

    def across(k, _):
        te, tw, tn, ts = (tr_ref[i, k] for i in range(4))
        center = 1.0 - te - tw - tn - ts
        pair = (lane == 2 * k) | (lane == 2 * k + 1)
        for t in range(tracers):
            x = v[t, k]
            east = pltpu.roll(te * x, 1, axis=1)
            west = pltpu.roll(tw * x, 127, axis=1)
            north = pltpu.roll(tn * x, 1, axis=0)
            south = pltpu.roll(ts * x, 31, axis=0)
            out = center * x + jnp.where(lane == 0, west, jnp.where(lane == 127, east, east + west))
            w_out[t, k] = out + jnp.where(row == 0, 0.0, north) + jnp.where(row == 31, 0.0, south)
            ends = pltpu.roll(jnp.where(lane == 0, east, west), 2 * k + 1, axis=1)
            lon_out[t] = jnp.where(pair, ends, lon_out[t])
        return 0

    lax.fori_loop(0, layers, across, 0, unroll=2)

    for t in range(tracers):
        at = slice(t * layers, (t + 1) * layers)
        north_out[at, :] = v[t, :, 0, :] * tr_ref[3, :, 0, :] * mask_ref[0:1, :]
        south_out[at, :] = v[t, :, 31, :] * tr_ref[2, :, 31, :] * mask_ref[1:2, :]


def first_step_kernel(f, mix, inv, up, tr, mask, w_out, lon_out, north_out, south_out, v):
    step_body(lambda t, k: 0.0, f, mix, inv, up, tr, mask, (w_out, lon_out, north_out, south_out), v)


def step_kernel(
    w_in, east_in, west_in, north_in, south_in, flux_in, f, mix, inv, up, tr, mask,
    w_out, lon_out, north_out, south_out, flux_out, v, lon,
):
    tracers, layers = f.shape[:2]
    lon_merge(east_in, west_in, lon)

    def base(t, k):
        value = halo_add(w_in[t, k], t, k, layers, lon, north_in, south_in)
        if isinstance(k, int):
            flux_out[t] = flux_in[t] + value
        return value

    step_body(base, f, mix, inv, up, tr, mask, (w_out, lon_out, north_out, south_out), v)


def last_kernel(w_in, east_in, west_in, north_in, south_in, flux_in, adj_out, flux_out, lon):
    tracers, layers = w_in.shape[:2]
    lon_merge(east_in, west_in, lon)

    def finish(k, _):
        for t in range(tracers):
            adj_out[t, k] = halo_add(w_in[t, k], t, k, layers, lon, north_in, south_in)
        return 0

    lax.fori_loop(0, layers, finish, 0, unroll=2)
    flux_out[...] = flux_in[...] + adj_out[:, 0]


def shifts(axis):
    peers = lax.axis_size(axis)
    up = [(i, (i + 1) % peers) for i in range(peers)]
    return up, [(b, a) for a, b in up]


def exchange(lon, north, south):
    lat_up, lat_down = shifts("lat")
    lon_up, lon_down = shifts("lon")
    from_north = lax.ppermute(south, "lat", lat_up)
    from_south = lax.ppermute(north, "lat", lat_down)
    from_west = lax.ppermute(lon, "lon", lon_up)
    from_east = lax.ppermute(lon, "lon", lon_down)
    return from_east, from_west, from_north, from_south


def body(
    transport, mixing, trajectory, kernel_table, track_tile, sound_cell, kernel_index, observed, precision
):
    ntiles = lax.axis_size(("lat", "lon"))
    steps, tracers, layers, rows, cols = trajectory.shape
    field = sds(tracers, layers, rows, cols)
    plane = sds(tracers, rows, cols)
    edge = sds(tracers * layers, cols)
    slots = ntiles * CAP
    outgoing = call(
        route_kernel,
        sds(ntiles, 2, 128),
        track_tile[:, :, 0],
        sound_cell,
        kernel_index,
        observed,
        precision,
    )
    got = lax.all_to_all(outgoing, ("lat", "lon"), split_axis=0, concat_axis=0, tiled=True)
    inverse, upper = call(
        setup_kernel, (sds(layers, rows, cols), sds(layers - 1, rows, cols)), mixing
    )
    lat = lax.axis_index("lat")
    mask = jnp.stack([lat > 0, lat < lax.axis_size("lat") - 1]).astype(F32)
    mask = jnp.broadcast_to(mask[:, None], (2, cols))
    snd = call(unpack_kernel, sds(steps, 8, slots), got)
    table = kernel_table.T
    chunk = 256

    def forcing(s):
        return call(
            functools.partial(forcing_kernel, s, chunk),
            field,
            snd,
            trajectory,
            table,
            scratch=(
                pltpu.VMEM((256, slots), BF16),
                pltpu.VMEM((layers, 16, slots), F32),
                pltpu.VMEM((8, slots), F32),
            ),
        )

    fixed = (mixing, inverse, upper, transport, mask)
    v = pltpu.VMEM((tracers, layers, rows, cols), F32)
    lon = pltpu.VMEM((tracers, rows, cols), F32)
    moved = (field, plane, edge, edge)
    w, *edges = call(first_step_kernel, moved, forcing(steps - 1), *fixed, scratch=(v,))
    flux = jnp.zeros((tracers, rows, cols), F32)
    for s in range(steps - 2, -1, -1):
        halos = exchange(*edges)
        w, *edges, flux = call(
            step_kernel, moved + (plane,), w, *halos, flux, forcing(s), *fixed, scratch=(v, lon)
        )
    return call(last_kernel, (field, plane), w, *exchange(*edges), flux, scratch=(lon,))


def solution(mesh):
    return jax.shard_map(
        body,
        mesh=mesh,
        in_specs=(
            P(None, None, "lat", "lon"),
            P(None, "lat", "lon"),
            P(None, None, None, "lat", "lon"),
            P(),
            P(None, ("lat", "lon"), None),
            P(None, ("lat", "lon")),
            P(None, ("lat", "lon")),
            P(None, None, ("lat", "lon")),
            P(None, ("lat", "lon")),
        ),
        out_specs=(P(None, None, "lat", "lon"), P(None, "lat", "lon")),
        check_vma=False,
    )
```

```python
import functools

import jax
import jax.numpy as jnp
from jax import lax
from jax.experimental import pallas as pl
from jax.experimental.pallas import tpu as pltpu
from jax.sharding import PartitionSpec as P

CAP = 8
WORDS = 5
F32 = jnp.float32
BF16 = jnp.bfloat16


def split3(x):
    hi = x.astype(BF16)
    rest = x - hi.astype(F32)
    mid = rest.astype(BF16)
    return hi, mid, (rest - mid.astype(F32)).astype(BF16)


def split2(x):
    hi = x.astype(BF16)
    return hi, (x - hi.astype(F32)).astype(BF16)


def dot(a, b):
    return jnp.dot(a, b, preferred_element_type=F32)


def dot_t(a, b):
    return lax.dot_general(a, b, (((1,), (1,)), ((), ())), preferred_element_type=F32)


VMEM = pl.BlockSpec(memory_space=pltpu.VMEM)
HBM = pl.BlockSpec(memory_space=pltpu.HBM)


def call(kernel, outs, *args, scratch=(), vmem=12 << 20, hbm=(), hbm_out=()):
    outs = tuple(outs) if isinstance(outs, (tuple, list)) else (outs,)
    args = [pltpu.with_memory_space_constraint(a, pltpu.HBM) if i in hbm else a for i, a in enumerate(args)]
    done = pl.pallas_call(
        kernel,
        out_shape=outs,
        in_specs=[HBM if i in hbm else VMEM for i in range(len(args))],
        out_specs=tuple(HBM if i in hbm_out else VMEM for i in range(len(outs))),
        scratch_shapes=list(scratch),
        compiler_params=pltpu.CompilerParams(vmem_limit_bytes=vmem),
    )(*args)
    return done if len(outs) > 1 else done[0]


def sds(*shape, dtype=F32):
    return jax.ShapeDtypeStruct(shape, dtype)


def route_kernel(
    tile_in, cell_in, index_in, obs_in, prec_in, out_ref, tile_ref, cell_ref, index_ref, obs_ref, prec_ref, sems
):
    copies = [
        pltpu.make_async_copy(src, dst, sems.at[i])
        for i, (src, dst) in enumerate(
            (
                (tile_in, tile_ref),
                (cell_in, cell_ref),
                (index_in, index_ref),
                (obs_in, obs_ref),
                (prec_in, prec_ref),
            )
        )
    ]
    for copy in copies:
        copy.start()
    steps, count = cell_ref.shape
    ntiles = out_ref.shape[0]
    tile_ids = lax.broadcasted_iota(jnp.int32, (ntiles, count), 0)
    before = (
        lax.broadcasted_iota(jnp.int32, (count, count), 0)
        < lax.broadcasted_iota(jnp.int32, (count, count), 1)
    ).astype(F32).astype(BF16)
    rank_ids = lax.broadcasted_iota(jnp.int32, (CAP, count), 0)
    pad = jnp.zeros((64 - CAP * WORDS, count), F32)
    half = jnp.zeros((64, count), F32)
    for copy in copies:
        copy.wait()
    for pair in range(steps // 2):
        total = None
        for side in range(2):
            s = 2 * pair + side
            mine = tile_ids == tile_ref[s]
            mine_f = mine.astype(F32)
            mine_b = mine_f.astype(BF16)
            seen = dot(mine_b, before)
            rank = jnp.sum(mine_f * seen, axis=0, keepdims=True).astype(jnp.int32)
            at_rank = rank_ids == rank
            code = (index_ref[s : s + 1, :] * 4096 + cell_ref[s : s + 1, :]).astype(F32)
            words = [code] + [obs_ref[t, s : s + 1, :] for t in range(3)] + [prec_ref[s : s + 1, :]]
            rows = [jnp.where(at_rank, w, 0.0) for w in words]
            block = jnp.concatenate(rows + [pad] + [half], axis=0)
            if side == 1:
                block = jnp.concatenate([half] + rows + [pad], axis=0)
            for part in split3(block):
                term = dot_t(mine_b, part)
                total = term if total is None else total + term
        out_ref[:, pair, :] = total


def unpack_kernel(got_ref, out_ref):
    ntiles = got_ref.shape[0]
    for pair in range(2):
        turned = got_ref[:, pair, :].T
        for side in range(2):
            s = 2 * pair + side
            base = 64 * side
            code = turned[base : base + CAP, :].astype(jnp.int32)
            kidx = code // 4096
            cell = code - kidx * 4096
            row = cell // 128
            col = cell - row * 128
            hi = row // 16
            fields = [hi * 128 + col, row - hi * 16, kidx]
            fields = [f.astype(F32) for f in fields]
            fields += [turned[base + CAP * w : base + CAP * (w + 1), :] for w in range(1, WORDS)]
            for f, value in enumerate(fields):
                for r in range(CAP):
                    out_ref[s, f : f + 1, r * ntiles : (r + 1) * ntiles] = value[r : r + 1, :]
            out_ref[s, 7:8, :] = jnp.zeros((1, CAP * ntiles), F32)


def forcing_kernel(s, chunk, snd_ref, traj_ref, table_ref, out_ref, pick, weight):
    tracers, layers = out_ref.shape[:2]
    slots = snd_ref.shape[2]
    nker = table_ref.shape[2]
    cell_ids = lax.broadcasted_iota(jnp.int32, (256, chunk), 0).astype(F32)
    low_ids = lax.broadcasted_iota(jnp.int32, (16, chunk), 0).astype(F32)
    ker_ids = lax.broadcasted_iota(jnp.int32, (nker, chunk), 0).astype(F32)
    for c in range(slots // chunk):
        at = pl.ds(c * chunk, chunk)
        pick[:, at] = jnp.where(cell_ids == snd_ref[s, 0:1, at], 1.0, 0.0).astype(BF16)
        low = jnp.where(low_ids == snd_ref[s, 1:2, at], 1.0, 0.0)
        ker = jnp.where(ker_ids == snd_ref[s, 2:3, at], 1.0, 0.0).astype(BF16)
        w = dot(table_ref[0], ker) + dot(table_ref[1], ker) + dot(table_ref[2], ker)
        for k in range(layers):
            weight[k, :, at] = w[k : k + 1, :] * low
    for t in range(tracers):
        lhs = jnp.concatenate(
            [
                traj_ref[s, t, :, 0:16, :].reshape(layers * 16, 128),
                traj_ref[s, t, :, 16:32, :].reshape(layers * 16, 128),
            ],
            axis=1,
        )
        force = None
        for c in range(slots // chunk):
            at = pl.ds(c * chunk, chunk)
            sampled = dot(lhs, pick[:, at]).reshape(layers, 16, chunk)
            model = jnp.sum(jnp.sum(sampled * weight[:, :, at], axis=0), axis=0, keepdims=True)
            sc = (model - snd_ref[s, 3 + t : 4 + t, at]) * snd_ref[s, 6:7, at]
            hi, lo = split2((weight[:, :, at] * sc).reshape(layers * 16, chunk))
            term = dot_t(hi, pick[:, at]) + dot_t(lo, pick[:, at])
            force = term if force is None else force + term
        out_ref[t, :, 0:16, :] = force[:, 0:128].reshape(layers, 16, 128)
        out_ref[t, :, 16:32, :] = force[:, 128:256].reshape(layers, 16, 128)


def setup_kernel(
    mask_ref, mix_in, tr_in, traj_in, table_in,
    mix_ref, inv_ref, up_ref, coef_ref, lat_w, lon_w, shift_ref, ends_ref, traj_ref, parts_ref, tr_ref, table_ref, sems,
):
    layers = inv_ref.shape[0]
    copies = [
        pltpu.make_async_copy(src, dst, sems.at[i])
        for i, (src, dst) in enumerate(
            ((mix_in, mix_ref), (tr_in, tr_ref), (table_in, table_ref), (traj_in, traj_ref))
        )
    ]
    for copy in copies:
        copy.start()
    src = lax.broadcasted_iota(jnp.int32, (256, 256), 0) % 128
    dst = lax.broadcasted_iota(jnp.int32, (256, 256), 1)
    dst = jnp.where(dst < 128, dst - 1, dst - 127)
    shift_ref[...] = jnp.where(src == dst, 1.0, 0.0).astype(BF16)
    end_row = lax.broadcasted_iota(jnp.int32, (8, 256), 0)
    end_lane = lax.broadcasted_iota(jnp.int32, (8, 256), 1) % 128
    ends = ((end_row == 0) & (end_lane == 127)) | ((end_row == 1) & (end_lane == 0))
    ends = jnp.where(ends, 1.0, 0.0).astype(BF16)
    ends_ref[...] = ends
    copies[0].wait()
    for k in range(layers):
        diag = jnp.ones_like(mix_ref[0])
        if k > 0:
            diag = diag + mix_ref[k - 1]
        if k < layers - 1:
            diag = diag + mix_ref[k]
        if k > 0:
            diag = diag + mix_ref[k - 1] * up
        inv = 1.0 / diag
        inv_ref[k] = inv
        if k < layers - 1:
            up = -mix_ref[k] * inv
            up_ref[k] = up
    copies[1].wait()
    lane = lax.broadcasted_iota(jnp.int32, (32, 128), 1)
    row = lax.broadcasted_iota(jnp.int32, (32, 128), 0)

    def coefs(k, _):
        te, tw, tn, ts = (tr_ref[i, k] for i in range(4))
        coef_ref[0, k] = jnp.where(lane == 0, 0.0, pltpu.roll(te, 1, axis=1))
        coef_ref[1, k] = jnp.where(lane == 127, 0.0, pltpu.roll(tw, 127, axis=1))
        coef_ref[2, k] = jnp.where(row == 0, 0.0, pltpu.roll(tn, 1, axis=0))
        coef_ref[3, k] = jnp.where(row == 31, 0.0, pltpu.roll(ts, 31, axis=0))
        coef_ref[4, k] = 1.0 - te - tw - tn - ts
        return 0

    lax.fori_loop(0, layers, coefs, 0, unroll=4)
    lat_w[0] = tr_ref[3, :, 0, :] * mask_ref[0:1, :]
    lat_w[1] = tr_ref[2, :, 31, :] * mask_ref[1:2, :]
    for side in range(2):
        flat = None
        for part in split3(tr_ref[side].reshape(layers * 32, 128)):
            term = dot_t(ends[:, 0:128], part)
            flat = term if flat is None else flat + term
        lon_w[side] = flat[side : side + 1, :]
    copies[2].wait()
    for i, part in enumerate(split3(table_ref[...])):
        parts_ref[i] = part
    copies[3].wait()


def spread(west_ref, east_ref, halo):
    tracers, layers, rows, cols = halo.shape
    size = layers * rows
    row = lax.broadcasted_iota(jnp.int32, (4, cols), 0)
    lane = lax.broadcasted_iota(jnp.int32, (4, cols), 1)
    place = ((row % 2 == 0) & (lane == 0)) | ((row % 2 == 1) & (lane == cols - 1))
    place = jnp.where(place, 1.0, 0.0).astype(BF16)
    for t in range(tracers):
        at = slice(t * size, (t + 1) * size)
        hi, lo = split2(jnp.concatenate([west_ref[:, at], east_ref[:, at]], axis=0))
        both = jnp.concatenate([hi, lo], axis=0)
        spot = lax.dot_general(both, place, (((0,), (0,)), ((), ())), preferred_element_type=F32)
        halo[t] = spot.reshape(layers, rows, cols)


def received(w_ref, halo, north_ref, south_ref, t, k):
    value = w_ref[t, k] + halo[t, k]
    row = lax.broadcasted_iota(jnp.int32, (8, 128), 0)
    at = pl.ds(t * w_ref.shape[1] + k, 1)
    top = value[0:8] + jnp.where(row == 0, north_ref[at, :], 0.0)
    low = value[24:32] + jnp.where(row == 7, south_ref[at, :], 0.0)
    return jnp.concatenate([top, value[8:24], low], axis=0)


def step_body(base, force_ref, fixed, outs, v):
    mix_ref, inv_ref, up_ref, coef_ref, lat_w, lon_w, shift_ref, ends_ref = fixed
    w_out, east_out, west_out, north_out, south_out = outs
    tracers, layers, rows, cols = force_ref.shape
    d = tuple((force_ref[t, 0] + base(t, 0)) * inv_ref[0] for t in range(tracers))
    for t in range(tracers):
        v[t, 0] = d[t]

    def forward(k, d):
        m, inv = mix_ref[k - 1], inv_ref[k]
        d = tuple((force_ref[t, k] + base(t, k) + m * d[t]) * inv for t in range(tracers))
        for t in range(tracers):
            v[t, k] = d[t]
        return d

    d = lax.fori_loop(1, layers, forward, d, unroll=5)

    def backward(i, x):
        k = layers - 2 - i
        u = up_ref[k]
        x = tuple(v[t, k] - u * x[t] for t in range(tracers))
        for t in range(tracers):
            v[t, k] = x[t]
        return x

    lax.fori_loop(0, layers - 1, backward, d, unroll=5)

    group = 12
    size = group * rows
    for t in range(tracers):
        for g in range(0, layers, group):
            x = v[t, g : g + group]
            hi, lo = split2(x.reshape(size, cols))
            both = jnp.concatenate([hi, lo], axis=1)
            moved = dot(both, shift_ref[...])
            ends = dot_t(ends_ref[...], both)
            to = pl.ds((t * layers + g) * rows, size)
            at = pl.ds(g * rows, size)
            east_out[:, to] = ends[0:1, :] * lon_w[0, :, at]
            west_out[:, to] = ends[1:2, :] * lon_w[1, :, at]
            c = [coef_ref[i, g : g + group].reshape(size, cols) for i in range(5)]
            down = jnp.stack([pltpu.roll(x[i], 1, axis=0) for i in range(group)])
            up = jnp.stack([pltpu.roll(x[i], rows - 1, axis=0) for i in range(group)])
            out = c[4] * x.reshape(size, cols) + c[0] * moved[:, :cols] + c[1] * moved[:, cols:]
            out = out + c[2] * down.reshape(size, cols) + c[3] * up.reshape(size, cols)
            w_out[t, g : g + group] = out.reshape(group, rows, cols)

    for t in range(tracers):
        at = slice(t * layers, (t + 1) * layers)
        north_out[at, :] = v[t, :, 0, :] * lat_w[0]
        south_out[at, :] = v[t, :, rows - 1, :] * lat_w[1]


def first_step_kernel(*refs):
    step_body(lambda t, k: 0.0, refs[0], refs[1:9], refs[9:14], refs[14])


def step_kernel(w_in, west_in, east_in, north_in, south_in, flux_in, *refs):
    force_ref, fixed, outs, (flux_out, v, halo) = refs[0], refs[1:9], refs[9:14], refs[14:]
    spread(west_in, east_in, halo)

    def base(t, k):
        value = received(w_in, halo, north_in, south_in, t, k)
        if isinstance(k, int):
            flux_out[t] = flux_in[t] + value
        return value

    step_body(base, force_ref, fixed, outs, v)


def last_kernel(w_in, west_in, east_in, north_in, south_in, flux_in, adj_out, flux_out, halo, done, sems):
    tracers, layers = w_in.shape[:2]
    spread(west_in, east_in, halo)
    copies = []
    for t in range(tracers):

        def finish(k, _):
            done[t, k] = received(w_in, halo, north_in, south_in, t, k)
            return 0

        lax.fori_loop(0, layers, finish, 0, unroll=4)
        copies.append(pltpu.make_async_copy(done.at[t], adj_out.at[t], sems.at[t]))
        copies[-1].start()
    flux_out[...] = flux_in[...] + done[:, 0]
    for copy in copies:
        copy.wait()


def shifts(axis):
    peers = lax.axis_size(axis)
    up = [(i, (i + 1) % peers) for i in range(peers)]
    return up, [(b, a) for a, b in up]


def exchange(east, west, north, south):
    lat_up, lat_down = shifts("lat")
    lon_up, lon_down = shifts("lon")
    from_north = lax.ppermute(south, "lat", lat_up)
    from_south = lax.ppermute(north, "lat", lat_down)
    from_west = lax.ppermute(east, "lon", lon_up)
    from_east = lax.ppermute(west, "lon", lon_down)
    return from_west, from_east, from_north, from_south


def body(
    transport, mixing, trajectory, kernel_table, track_tile, sound_cell, kernel_index, observed, precision
):
    ntiles = lax.axis_size(("lat", "lon"))
    steps, tracers, layers, rows, cols = trajectory.shape
    count = sound_cell.shape[1]
    field = sds(tracers, layers, rows, cols)
    plane = sds(tracers, rows, cols)
    lat_edge = sds(tracers * layers, cols)
    lon_edge = sds(1, tracers * layers * rows)
    slots = ntiles * CAP
    outgoing = call(
        route_kernel,
        sds(ntiles, 2, 128),
        track_tile.transpose(0, 2, 1),
        sound_cell,
        kernel_index,
        observed.transpose(1, 0, 2),
        precision,
        hbm=range(5),
        scratch=(
            pltpu.VMEM((steps, 1, count), jnp.int32),
            pltpu.VMEM((steps, count), jnp.int32),
            pltpu.VMEM((steps, count), jnp.int32),
            pltpu.VMEM((tracers, steps, count), F32),
            pltpu.VMEM((steps, count), F32),
            pltpu.SemaphoreType.DMA((5,)),
        ),
    )
    got = lax.all_to_all(outgoing, ("lat", "lon"), split_axis=0, concat_axis=0, tiled=True)
    lat = lax.axis_index("lat")
    mask = jnp.stack([lat > 0, lat < lax.axis_size("lat") - 1]).astype(F32)
    mask = jnp.broadcast_to(mask[:, None], (2, cols))
    *fixed, local, table = call(
        setup_kernel,
        (
            sds(*mixing.shape),
            sds(layers, rows, cols),
            sds(*mixing.shape),
            sds(5, layers, rows, cols),
            sds(2, layers, cols),
            sds(2, 1, layers * rows),
            sds(256, 256, dtype=BF16),
            sds(8, 256, dtype=BF16),
            sds(*trajectory.shape, dtype=BF16),
            sds(3, layers, kernel_table.shape[0], dtype=BF16),
        ),
        mask,
        mixing,
        transport,
        trajectory,
        kernel_table.T,
        hbm=(1, 2, 3, 4),
        scratch=(
            pltpu.VMEM(transport.shape, F32),
            pltpu.VMEM(kernel_table.shape[::-1], F32),
            pltpu.SemaphoreType.DMA((4,)),
        ),
    )
    snd = call(unpack_kernel, sds(steps, 8, slots), got)

    def forcing(s):
        return call(
            functools.partial(forcing_kernel, s, 512),
            field,
            snd,
            local,
            table,
            scratch=(pltpu.VMEM((256, slots), BF16), pltpu.VMEM((layers, 16, slots), F32)),
        )

    v = pltpu.VMEM(field.shape, F32)
    moved = (field, lon_edge, lon_edge, lat_edge, lat_edge)
    w, *edges = call(first_step_kernel, moved, forcing(steps - 1), *fixed, scratch=(v,))
    flux = jnp.zeros((tracers, rows, cols), F32)
    for s in range(steps - 2, -1, -1):
        halos = exchange(*edges)
        w, *edges, flux = call(
            step_kernel, moved + (plane,), w, *halos, flux, forcing(s), *fixed, scratch=(v, v)
        )
    return call(
        last_kernel,
        (field, plane),
        w,
        *exchange(*edges),
        flux,
        hbm_out=(0,),
        scratch=(v, v, pltpu.SemaphoreType.DMA((tracers,))),
    )


def solution(mesh):
    return jax.shard_map(
        body,
        mesh=mesh,
        in_specs=(
            P(None, None, "lat", "lon"),
            P(None, "lat", "lon"),
            P(None, None, None, "lat", "lon"),
            P(),
            P(None, ("lat", "lon"), None),
            P(None, ("lat", "lon")),
            P(None, ("lat", "lon")),
            P(None, None, ("lat", "lon")),
            P(None, ("lat", "lon")),
        ),
        out_specs=(P(None, None, "lat", "lon"), P(None, "lat", "lon")),
        check_vma=False,
    )
```

```python
import functools

import jax
import jax.numpy as jnp
from jax import lax
from jax.experimental import pallas as pl
from jax.experimental.pallas import tpu as pltpu
from jax.sharding import PartitionSpec as P

CAP = 8
WORDS = 5
F32 = jnp.float32
BF16 = jnp.bfloat16


def split3(x):
    hi = x.astype(BF16)
    rest = x - hi.astype(F32)
    mid = rest.astype(BF16)
    return hi, mid, (rest - mid.astype(F32)).astype(BF16)


def split2(x):
    hi = x.astype(BF16)
    return hi, (x - hi.astype(F32)).astype(BF16)


def dot(a, b):
    return jnp.dot(a, b, preferred_element_type=F32)


def dot_t(a, b):
    return lax.dot_general(a, b, (((1,), (1,)), ((), ())), preferred_element_type=F32)


VMEM = pl.BlockSpec(memory_space=pltpu.VMEM)
HBM = pl.BlockSpec(memory_space=pltpu.HBM)


def call(kernel, outs, *args, scratch=(), vmem=12 << 20, hbm=(), hbm_out=()):
    outs = tuple(outs) if isinstance(outs, (tuple, list)) else (outs,)
    args = [pltpu.with_memory_space_constraint(a, pltpu.HBM) if i in hbm else a for i, a in enumerate(args)]
    done = pl.pallas_call(
        kernel,
        out_shape=outs,
        in_specs=[HBM if i in hbm else VMEM for i in range(len(args))],
        out_specs=tuple(HBM if i in hbm_out else VMEM for i in range(len(outs))),
        scratch_shapes=list(scratch),
        compiler_params=pltpu.CompilerParams(vmem_limit_bytes=vmem),
    )(*args)
    return done if len(outs) > 1 else done[0]


def sds(*shape, dtype=F32):
    return jax.ShapeDtypeStruct(shape, dtype)


def route_kernel(
    tile_in, cell_in, index_in, obs_in, prec_in, out_ref, tile_ref, cell_ref, index_ref, obs_ref, prec_ref, sems
):
    copies = [
        pltpu.make_async_copy(src, dst, sems.at[i])
        for i, (src, dst) in enumerate(
            (
                (tile_in, tile_ref),
                (cell_in, cell_ref),
                (index_in, index_ref),
                (obs_in, obs_ref),
                (prec_in, prec_ref),
            )
        )
    ]
    for copy in copies:
        copy.start()
    steps, count = cell_ref.shape
    ntiles = out_ref.shape[0]
    tile_ids = lax.broadcasted_iota(jnp.int32, (ntiles, count), 0)
    before = (
        lax.broadcasted_iota(jnp.int32, (count, count), 0)
        < lax.broadcasted_iota(jnp.int32, (count, count), 1)
    ).astype(F32).astype(BF16)
    rank_ids = lax.broadcasted_iota(jnp.int32, (CAP, count), 0)
    pad = jnp.zeros((64 - CAP * WORDS, count), F32)
    half = jnp.zeros((64, count), F32)
    for copy in copies:
        copy.wait()
    for pair in range(steps // 2):
        total = None
        for side in range(2):
            s = 2 * pair + side
            mine = tile_ids == tile_ref[s]
            mine_f = mine.astype(F32)
            mine_b = mine_f.astype(BF16)
            seen = dot(mine_b, before)
            rank = jnp.sum(mine_f * seen, axis=0, keepdims=True).astype(jnp.int32)
            at_rank = rank_ids == rank
            code = (index_ref[s : s + 1, :] * 4096 + cell_ref[s : s + 1, :]).astype(F32)
            words = [code] + [obs_ref[t, s : s + 1, :] for t in range(3)] + [prec_ref[s : s + 1, :]]
            rows = [jnp.where(at_rank, w, 0.0) for w in words]
            block = jnp.concatenate(rows + [pad] + [half], axis=0)
            if side == 1:
                block = jnp.concatenate([half] + rows + [pad], axis=0)
            for part in split3(block):
                term = dot_t(mine_b, part)
                total = term if total is None else total + term
        out_ref[:, pair, :] = total


def unpack_kernel(got_ref, out_ref):
    ntiles = got_ref.shape[0]
    for pair in range(2):
        turned = got_ref[:, pair, :].T
        for side in range(2):
            s = 2 * pair + side
            base = 64 * side
            code = turned[base : base + CAP, :].astype(jnp.int32)
            kidx = code // 4096
            cell = code - kidx * 4096
            row = cell // 128
            col = cell - row * 128
            hi = row // 16
            fields = [hi * 128 + col, row - hi * 16, kidx]
            fields = [f.astype(F32) for f in fields]
            fields += [turned[base + CAP * w : base + CAP * (w + 1), :] for w in range(1, WORDS)]
            for f, value in enumerate(fields):
                for r in range(CAP):
                    out_ref[s, f : f + 1, r * ntiles : (r + 1) * ntiles] = value[r : r + 1, :]
            out_ref[s, 7:8, :] = jnp.zeros((1, CAP * ntiles), F32)


def forcing_kernel(s, chunk, snd_ref, traj_ref, table_ref, out_ref, pick, weight):
    tracers, layers = out_ref.shape[:2]
    slots = snd_ref.shape[2]
    nker = table_ref.shape[2]
    cell_ids = lax.broadcasted_iota(jnp.int32, (256, chunk), 0).astype(F32)
    low_ids = lax.broadcasted_iota(jnp.int32, (16, chunk), 0).astype(F32)
    ker_ids = lax.broadcasted_iota(jnp.int32, (nker, chunk), 0).astype(F32)
    for c in range(slots // chunk):
        at = pl.ds(c * chunk, chunk)
        pick[:, at] = jnp.where(cell_ids == snd_ref[s, 0:1, at], 1.0, 0.0).astype(BF16)
        low = jnp.where(low_ids == snd_ref[s, 1:2, at], 1.0, 0.0)
        ker = jnp.where(ker_ids == snd_ref[s, 2:3, at], 1.0, 0.0).astype(BF16)
        w = dot(table_ref[0], ker) + dot(table_ref[1], ker) + dot(table_ref[2], ker)
        for k in range(layers):
            weight[k, :, at] = w[k : k + 1, :] * low
    for t in range(tracers):
        lhs = jnp.concatenate(
            [
                traj_ref[s, t, :, 0:16, :].reshape(layers * 16, 128),
                traj_ref[s, t, :, 16:32, :].reshape(layers * 16, 128),
            ],
            axis=1,
        )
        force = None
        for c in range(slots // chunk):
            at = pl.ds(c * chunk, chunk)
            sampled = dot(lhs, pick[:, at]).reshape(layers, 16, chunk)
            model = jnp.sum(jnp.sum(sampled * weight[:, :, at], axis=0), axis=0, keepdims=True)
            sc = (model - snd_ref[s, 3 + t : 4 + t, at]) * snd_ref[s, 6:7, at]
            hi, lo = split2((weight[:, :, at] * sc).reshape(layers * 16, chunk))
            term = dot_t(hi, pick[:, at]) + dot_t(lo, pick[:, at])
            force = term if force is None else force + term
        out_ref[t, :, 0:16, :] = force[:, 0:128].reshape(layers, 16, 128)
        out_ref[t, :, 16:32, :] = force[:, 128:256].reshape(layers, 16, 128)


def setup_kernel(
    mask_ref, mix_in, tr_in, traj_in, table_in,
    mix_ref, inv_ref, up_ref, coef_ref, lat_w, lon_w, shift_ref, ends_ref, traj_ref, parts_ref, tr_ref, table_ref, sems,
):
    layers = inv_ref.shape[0]
    copies = [
        pltpu.make_async_copy(src, dst, sems.at[i])
        for i, (src, dst) in enumerate(
            ((mix_in, mix_ref), (tr_in, tr_ref), (table_in, table_ref), (traj_in, traj_ref))
        )
    ]
    for copy in copies:
        copy.start()
    src = lax.broadcasted_iota(jnp.int32, (256, 256), 0) % 128
    dst = lax.broadcasted_iota(jnp.int32, (256, 256), 1)
    dst = jnp.where(dst < 128, dst - 1, dst - 127)
    shift_ref[...] = jnp.where(src == dst, 1.0, 0.0).astype(BF16)
    end_row = lax.broadcasted_iota(jnp.int32, (8, 256), 0)
    end_lane = lax.broadcasted_iota(jnp.int32, (8, 256), 1) % 128
    ends = ((end_row == 0) & (end_lane == 127)) | ((end_row == 1) & (end_lane == 0))
    ends = jnp.where(ends, 1.0, 0.0).astype(BF16)
    ends_ref[...] = ends
    copies[0].wait()
    for k in range(layers):
        diag = jnp.ones_like(mix_ref[0])
        if k > 0:
            diag = diag + mix_ref[k - 1]
        if k < layers - 1:
            diag = diag + mix_ref[k]
        if k > 0:
            diag = diag + mix_ref[k - 1] * up
        inv = 1.0 / diag
        inv_ref[k] = inv
        if k < layers - 1:
            up = -mix_ref[k] * inv
            up_ref[k] = up
    copies[1].wait()
    lane = lax.broadcasted_iota(jnp.int32, (32, 128), 1)
    row = lax.broadcasted_iota(jnp.int32, (32, 128), 0)

    def coefs(k, _):
        te, tw, tn, ts = (tr_ref[i, k] for i in range(4))
        coef_ref[0, k] = jnp.where(lane == 0, 0.0, pltpu.roll(te, 1, axis=1))
        coef_ref[1, k] = jnp.where(lane == 127, 0.0, pltpu.roll(tw, 127, axis=1))
        coef_ref[2, k] = jnp.where(row == 0, 0.0, pltpu.roll(tn, 1, axis=0))
        coef_ref[3, k] = jnp.where(row == 31, 0.0, pltpu.roll(ts, 31, axis=0))
        coef_ref[4, k] = 1.0 - te - tw - tn - ts
        return 0

    lax.fori_loop(0, layers, coefs, 0, unroll=4)
    to_north = tr_ref[3, :, 0, :] * mask_ref[0:1, :]
    to_south = tr_ref[2, :, 31, :] * mask_ref[1:2, :]
    odd = mask_ref[2:3, :]
    lat_w[0] = odd * to_north
    lat_w[1] = (1.0 - odd) * to_south
    lat_w[2] = (1.0 - odd) * to_north
    lat_w[3] = odd * to_south
    odd = mask_ref[3:4, 0:1]
    for side in range(2):
        flat = None
        for part in split3(tr_ref[side].reshape(layers * 32, 128)):
            term = dot_t(ends[:, 0:128], part)
            flat = term if flat is None else flat + term
        flat = flat[side : side + 1, :]
        lon_w[side] = flat * (odd if side else 1.0 - odd)
        lon_w[2 + side] = flat * (1.0 - odd if side else odd)
    copies[2].wait()
    for i, part in enumerate(split3(table_ref[...])):
        parts_ref[i] = part
    copies[3].wait()


def spread(mask_ref, lon_a, lon_b, lat_a, lat_b, halo, lat_halo):
    tracers, layers, rows, cols = halo.shape
    size = layers * rows
    odd = mask_ref[2:3, :] > 0.5
    lat_halo[0] = jnp.where(odd, lat_a[...], lat_b[...])
    lat_halo[1] = jnp.where(odd, lat_b[...], lat_a[...])
    row = lax.broadcasted_iota(jnp.int32, (4, cols), 0)
    lane = lax.broadcasted_iota(jnp.int32, (4, cols), 1)
    other = (row % 2).astype(F32)
    lon_odd = jnp.broadcast_to(mask_ref[3:4, :], (4, cols))
    spot = (other * lon_odd + (1.0 - other) * (1.0 - lon_odd)) * (cols - 1)
    place = jnp.where(lane.astype(F32) == spot, 1.0, 0.0).astype(BF16)
    for t in range(tracers):
        at = slice(t * size, (t + 1) * size)
        hi, lo = split2(jnp.concatenate([lon_a[:, at], lon_b[:, at]], axis=0))
        both = jnp.concatenate([hi, lo], axis=0)
        spot = lax.dot_general(both, place, (((0,), (0,)), ((), ())), preferred_element_type=F32)
        halo[t] = spot.reshape(layers, rows, cols)


def received(w_ref, halo, lat_halo, t, k):
    value = w_ref[t, k] + halo[t, k]
    row = lax.broadcasted_iota(jnp.int32, (8, 128), 0)
    at = pl.ds(t * w_ref.shape[1] + k, 1)
    top = value[0:8] + jnp.where(row == 0, lat_halo[0, at, :], 0.0)
    low = value[24:32] + jnp.where(row == 7, lat_halo[1, at, :], 0.0)
    return jnp.concatenate([top, value[8:24], low], axis=0)


def step_body(base, force_ref, fixed, outs, v):
    mix_ref, inv_ref, up_ref, coef_ref, lat_w, lon_w, shift_ref, ends_ref = fixed
    w_out, lon_a, lon_b, lat_a, lat_b = outs
    tracers, layers, rows, cols = force_ref.shape
    d = tuple((force_ref[t, 0] + base(t, 0)) * inv_ref[0] for t in range(tracers))
    for t in range(tracers):
        v[t, 0] = d[t]

    def forward(k, d):
        m, inv = mix_ref[k - 1], inv_ref[k]
        d = tuple((force_ref[t, k] + base(t, k) + m * d[t]) * inv for t in range(tracers))
        for t in range(tracers):
            v[t, k] = d[t]
        return d

    d = lax.fori_loop(1, layers, forward, d, unroll=5)

    def backward(i, x):
        k = layers - 2 - i
        u = up_ref[k]
        x = tuple(v[t, k] - u * x[t] for t in range(tracers))
        for t in range(tracers):
            v[t, k] = x[t]
        return x

    lax.fori_loop(0, layers - 1, backward, d, unroll=5)

    group = 12
    size = group * rows
    for t in range(tracers):
        for g in range(0, layers, group):
            x = v[t, g : g + group]
            hi, lo = split2(x.reshape(size, cols))
            both = jnp.concatenate([hi, lo], axis=1)
            moved = dot(both, shift_ref[...])
            ends = dot_t(ends_ref[...], both)
            to = pl.ds((t * layers + g) * rows, size)
            at = pl.ds(g * rows, size)
            lon_a[:, to] = ends[0:1, :] * lon_w[0, :, at] + ends[1:2, :] * lon_w[1, :, at]
            lon_b[:, to] = ends[0:1, :] * lon_w[2, :, at] + ends[1:2, :] * lon_w[3, :, at]
            c = [coef_ref[i, g : g + group].reshape(size, cols) for i in range(5)]
            down = jnp.stack([pltpu.roll(x[i], 1, axis=0) for i in range(group)])
            up = jnp.stack([pltpu.roll(x[i], rows - 1, axis=0) for i in range(group)])
            out = c[4] * x.reshape(size, cols) + c[0] * moved[:, :cols] + c[1] * moved[:, cols:]
            out = out + c[2] * down.reshape(size, cols) + c[3] * up.reshape(size, cols)
            w_out[t, g : g + group] = out.reshape(group, rows, cols)

    for t in range(tracers):
        at = slice(t * layers, (t + 1) * layers)
        top, low = v[t, :, 0, :], v[t, :, rows - 1, :]
        lat_a[at, :] = top * lat_w[0] + low * lat_w[1]
        lat_b[at, :] = top * lat_w[2] + low * lat_w[3]


def first_step_kernel(*refs):
    step_body(lambda t, k: 0.0, refs[0], refs[1:9], refs[9:14], refs[14])


def step_kernel(mask_ref, w_in, lon_a, lon_b, lat_a, lat_b, flux_in, *refs):
    force_ref, fixed, outs, (flux_out, v, halo, lat_halo) = refs[0], refs[1:9], refs[9:14], refs[14:]
    spread(mask_ref, lon_a, lon_b, lat_a, lat_b, halo, lat_halo)

    def base(t, k):
        value = received(w_in, halo, lat_halo, t, k)
        if isinstance(k, int):
            flux_out[t] = flux_in[t] + value
        return value

    step_body(base, force_ref, fixed, outs, v)


def last_kernel(
    mask_ref, w_in, lon_a, lon_b, lat_a, lat_b, flux_in, adj_out, flux_out, halo, lat_halo, done, sems
):
    tracers, layers = w_in.shape[:2]
    spread(mask_ref, lon_a, lon_b, lat_a, lat_b, halo, lat_halo)
    copies = []
    for t in range(tracers):

        def finish(k, _):
            done[t, k] = received(w_in, halo, lat_halo, t, k)
            return 0

        lax.fori_loop(0, layers, finish, 0, unroll=4)
        copies.append(pltpu.make_async_copy(done.at[t], adj_out.at[t], sems.at[t]))
        copies[-1].start()
    flux_out[...] = flux_in[...] + done[:, 0]
    for copy in copies:
        copy.wait()


def swaps(axis):
    peers = lax.axis_size(axis)
    near = [(i, i + 1 - 2 * (i % 2)) for i in range(peers)]
    return near, [((i + 1) % peers, (j + 1) % peers) for i, j in near]


def exchange(lon_a, lon_b, lat_a, lat_b):
    lat_near, lat_far = swaps("lat")
    lon_near, lon_far = swaps("lon")
    lon_b = lax.ppermute(lon_b, "lon", lon_far)
    lat_b = lax.ppermute(lat_b, "lat", lat_far)
    lon_a = lax.ppermute(lon_a, "lon", lon_near)
    lat_a = lax.ppermute(lat_a, "lat", lat_near)
    return lon_a, lon_b, lat_a, lat_b


def body(
    transport, mixing, trajectory, kernel_table, track_tile, sound_cell, kernel_index, observed, precision
):
    ntiles = lax.axis_size(("lat", "lon"))
    steps, tracers, layers, rows, cols = trajectory.shape
    count = sound_cell.shape[1]
    field = sds(tracers, layers, rows, cols)
    plane = sds(tracers, rows, cols)
    lat_edge = sds(tracers * layers, cols)
    lon_edge = sds(1, tracers * layers * rows)
    slots = ntiles * CAP
    outgoing = call(
        route_kernel,
        sds(ntiles, 2, 128),
        track_tile.transpose(0, 2, 1),
        sound_cell,
        kernel_index,
        observed.transpose(1, 0, 2),
        precision,
        hbm=range(5),
        scratch=(
            pltpu.VMEM((steps, 1, count), jnp.int32),
            pltpu.VMEM((steps, count), jnp.int32),
            pltpu.VMEM((steps, count), jnp.int32),
            pltpu.VMEM((tracers, steps, count), F32),
            pltpu.VMEM((steps, count), F32),
            pltpu.SemaphoreType.DMA((5,)),
        ),
    )
    got = lax.all_to_all(outgoing, ("lat", "lon"), split_axis=0, concat_axis=0, tiled=True)
    lat, lon = lax.axis_index("lat"), lax.axis_index("lon")
    mask = jnp.stack([lat > 0, lat < lax.axis_size("lat") - 1, lat % 2 > 0, lon % 2 > 0]).astype(F32)
    mask = jnp.broadcast_to(mask[:, None], (4, cols))
    *fixed, local, table = call(
        setup_kernel,
        (
            sds(*mixing.shape),
            sds(layers, rows, cols),
            sds(*mixing.shape),
            sds(5, layers, rows, cols),
            sds(4, layers, cols),
            sds(4, 1, layers * rows),
            sds(256, 256, dtype=BF16),
            sds(8, 256, dtype=BF16),
            sds(*trajectory.shape, dtype=BF16),
            sds(3, layers, kernel_table.shape[0], dtype=BF16),
        ),
        mask,
        mixing,
        transport,
        trajectory,
        kernel_table.T,
        hbm=(1, 2, 3, 4),
        scratch=(
            pltpu.VMEM(transport.shape, F32),
            pltpu.VMEM(kernel_table.shape[::-1], F32),
            pltpu.SemaphoreType.DMA((4,)),
        ),
    )
    snd = call(unpack_kernel, sds(steps, 8, slots), got)

    def forcing(s):
        return call(
            functools.partial(forcing_kernel, s, 512),
            field,
            snd,
            local,
            table,
            scratch=(pltpu.VMEM((256, slots), BF16), pltpu.VMEM((layers, 16, slots), F32)),
        )

    v = pltpu.VMEM(field.shape, F32)
    lat_halo = pltpu.VMEM((2,) + lat_edge.shape, F32)
    moved = (field, lon_edge, lon_edge, lat_edge, lat_edge)
    w, *edges = call(first_step_kernel, moved, forcing(steps - 1), *fixed, scratch=(v,))
    flux = jnp.zeros((tracers, rows, cols), F32)
    for s in range(steps - 2, -1, -1):
        halos = exchange(*edges)
        w, *edges, flux = call(
            step_kernel,
            moved + (plane,),
            mask,
            w,
            *halos,
            flux,
            forcing(s),
            *fixed,
            scratch=(v, v, lat_halo),
        )
    return call(
        last_kernel,
        (field, plane),
        mask,
        w,
        *exchange(*edges),
        flux,
        hbm_out=(0,),
        scratch=(v, lat_halo, v, pltpu.SemaphoreType.DMA((tracers,))),
    )


def solution(mesh):
    return jax.shard_map(
        body,
        mesh=mesh,
        in_specs=(
            P(None, None, "lat", "lon"),
            P(None, "lat", "lon"),
            P(None, None, None, "lat", "lon"),
            P(),
            P(None, ("lat", "lon"), None),
            P(None, ("lat", "lon")),
            P(None, ("lat", "lon")),
            P(None, None, ("lat", "lon")),
            P(None, ("lat", "lon")),
        ),
        out_specs=(P(None, None, "lat", "lon"), P(None, "lat", "lon")),
        check_vma=False,
    )
```

```python
import functools

import jax
import jax.numpy as jnp
from jax import lax
from jax.experimental import pallas as pl
from jax.experimental.pallas import tpu as pltpu
from jax.sharding import PartitionSpec as P

CAP = 8
WORDS = 5
F32 = jnp.float32
BF16 = jnp.bfloat16


def split3(x):
    hi = x.astype(BF16)
    rest = x - hi.astype(F32)
    mid = rest.astype(BF16)
    return hi, mid, (rest - mid.astype(F32)).astype(BF16)


def split2(x):
    hi = x.astype(BF16)
    return hi, (x - hi.astype(F32)).astype(BF16)


def dot(a, b):
    return jnp.dot(a, b, preferred_element_type=F32)


def dot_t(a, b):
    return lax.dot_general(a, b, (((1,), (1,)), ((), ())), preferred_element_type=F32)


VMEM = pl.BlockSpec(memory_space=pltpu.VMEM)
HBM = pl.BlockSpec(memory_space=pltpu.HBM)


def call(kernel, outs, *args, scratch=(), vmem=12 << 20, hbm=(), hbm_out=()):
    outs = tuple(outs) if isinstance(outs, (tuple, list)) else (outs,)
    args = [pltpu.with_memory_space_constraint(a, pltpu.HBM) if i in hbm else a for i, a in enumerate(args)]
    done = pl.pallas_call(
        kernel,
        out_shape=tuple(pltpu.HBM(o.shape, o.dtype) if i in hbm_out else o for i, o in enumerate(outs)),
        in_specs=[HBM if i in hbm else VMEM for i in range(len(args))],
        out_specs=tuple(HBM if i in hbm_out else VMEM for i in range(len(outs))),
        scratch_shapes=list(scratch),
        compiler_params=pltpu.CompilerParams(vmem_limit_bytes=vmem),
    )(*args)
    return done if len(outs) > 1 else done[0]


def sds(*shape, dtype=F32):
    return jax.ShapeDtypeStruct(shape, dtype)


def route_kernel(
    tile_in, cell_in, index_in, obs_in, prec_in, out_ref, tile_ref, cell_ref, index_ref, obs_ref, prec_ref, sems
):
    copies = [
        pltpu.make_async_copy(src, dst, sems.at[i])
        for i, (src, dst) in enumerate(
            (
                (tile_in, tile_ref),
                (cell_in, cell_ref),
                (index_in, index_ref),
                (obs_in, obs_ref),
                (prec_in, prec_ref),
            )
        )
    ]
    for copy in copies:
        copy.start()
    steps, count = cell_ref.shape
    ntiles = out_ref.shape[0]
    tile_ids = lax.broadcasted_iota(jnp.int32, (ntiles, count), 0)
    before = (
        lax.broadcasted_iota(jnp.int32, (count, count), 0)
        < lax.broadcasted_iota(jnp.int32, (count, count), 1)
    ).astype(F32).astype(BF16)
    rank_ids = lax.broadcasted_iota(jnp.int32, (CAP, count), 0)
    pad = jnp.zeros((64 - CAP * WORDS, count), F32)
    half = jnp.zeros((64, count), F32)
    for copy in copies:
        copy.wait()
    for pair in range(steps // 2):
        total = None
        for side in range(2):
            s = 2 * pair + side
            mine = tile_ids == tile_ref[s]
            mine_f = mine.astype(F32)
            mine_b = mine_f.astype(BF16)
            seen = dot(mine_b, before)
            rank = jnp.sum(mine_f * seen, axis=0, keepdims=True).astype(jnp.int32)
            at_rank = rank_ids == rank
            code = (index_ref[s : s + 1, :] * 4096 + cell_ref[s : s + 1, :]).astype(F32)
            words = [code] + [obs_ref[t, s : s + 1, :] for t in range(3)] + [prec_ref[s : s + 1, :]]
            rows = [jnp.where(at_rank, w, 0.0) for w in words]
            block = jnp.concatenate(rows + [pad] + [half], axis=0)
            if side == 1:
                block = jnp.concatenate([half] + rows + [pad], axis=0)
            for part in split3(block):
                term = dot_t(mine_b, part)
                total = term if total is None else total + term
        out_ref[:, pair, :] = total


def unpack_kernel(got_ref, out_ref):
    ntiles = got_ref.shape[0]
    for pair in range(2):
        turned = got_ref[:, pair, :].T
        for side in range(2):
            s = 2 * pair + side
            base = 64 * side
            code = turned[base : base + CAP, :].astype(jnp.int32)
            kidx = code // 4096
            cell = code - kidx * 4096
            row = cell // 128
            col = cell - row * 128
            hi = row // 16
            fields = [hi * 128 + col, row - hi * 16, kidx]
            fields = [f.astype(F32) for f in fields]
            fields += [turned[base + CAP * w : base + CAP * (w + 1), :] for w in range(1, WORDS)]
            for f, value in enumerate(fields):
                for r in range(CAP):
                    out_ref[s, f : f + 1, r * ntiles : (r + 1) * ntiles] = value[r : r + 1, :]
            out_ref[s, 7:8, :] = jnp.zeros((1, CAP * ntiles), F32)


def forcing_kernel(s, chunk, snd_ref, traj_ref, table_in, out_ref, pick, weight, table_ref, sem):
    copy = pltpu.make_async_copy(table_in, table_ref, sem)
    copy.start()
    forcing_body(s, chunk, snd_ref, traj_ref, copy, table_ref, out_ref, pick, weight)


def forcing_body(s, chunk, snd_ref, traj_ref, copy, table_ref, out_ref, pick, weight):
    tracers, layers = out_ref.shape[:2]
    slots = snd_ref.shape[2]
    nker = table_ref.shape[1]
    cell_ids = lax.broadcasted_iota(jnp.int32, (256, chunk), 0).astype(F32)
    low_ids = lax.broadcasted_iota(jnp.int32, (16, chunk), 0).astype(F32)
    ker_ids = lax.broadcasted_iota(jnp.int32, (nker, chunk), 0).astype(F32)
    for c in range(slots // chunk):
        at = pl.ds(c * chunk, chunk)
        pick[:, at] = jnp.where(cell_ids == snd_ref[s, 0:1, at], 1.0, 0.0).astype(BF16)
    copy.wait()
    table = split3(table_ref[...])
    for c in range(slots // chunk):
        at = pl.ds(c * chunk, chunk)
        low = jnp.where(low_ids == snd_ref[s, 1:2, at], 1.0, 0.0)
        ker = jnp.where(ker_ids == snd_ref[s, 2:3, at], 1.0, 0.0).astype(BF16)
        w = dot(table[0], ker) + dot(table[1], ker) + dot(table[2], ker)
        for k in range(layers):
            weight[k, :, at] = w[k : k + 1, :] * low
    for t in range(tracers):
        lhs = jnp.concatenate(
            [
                traj_ref[s, t, :, 0:16, :].reshape(layers * 16, 128),
                traj_ref[s, t, :, 16:32, :].reshape(layers * 16, 128),
            ],
            axis=1,
        )
        force = None
        for c in range(slots // chunk):
            at = pl.ds(c * chunk, chunk)
            sampled = dot(lhs, pick[:, at]).reshape(layers, 16, chunk)
            model = jnp.sum(jnp.sum(sampled * weight[:, :, at], axis=0), axis=0, keepdims=True)
            sc = (model - snd_ref[s, 3 + t : 4 + t, at]) * snd_ref[s, 6:7, at]
            hi, lo = split2((weight[:, :, at] * sc).reshape(layers * 16, chunk))
            term = dot_t(hi, pick[:, at]) + dot_t(lo, pick[:, at])
            force = term if force is None else force + term
        out_ref[t, :, 0:16, :] = force[:, 0:128].reshape(layers, 16, 128)
        out_ref[t, :, 16:32, :] = force[:, 128:256].reshape(layers, 16, 128)


def end_rows():
    row = lax.broadcasted_iota(jnp.int32, (8, 256), 0)
    lane = lax.broadcasted_iota(jnp.int32, (8, 256), 1) % 128
    ends = ((row == 0) & (lane == 127)) | ((row == 1) & (lane == 0))
    return jnp.where(ends, 1.0, 0.0).astype(BF16)


def lane_shifts():
    src = lax.broadcasted_iota(jnp.int32, (256, 256), 0) % 128
    dst = lax.broadcasted_iota(jnp.int32, (256, 256), 1)
    dst = jnp.where(dst < 128, dst - 1, dst - 127)
    return jnp.where(src == dst, 1.0, 0.0).astype(BF16)


def views(planes_ref):
    layers = (planes_ref.shape[0] + 1) // 7
    part = [planes_ref.at[pl.ds(i * layers, layers)] for i in range(6)]
    return part[5], planes_ref.at[pl.ds(6 * layers, layers - 1)], part[:5]


def setup_kernel(
    mask_ref, mix_in, tr_in, traj_in, planes_out, lat_out, lon_out, traj_ref,
    mix_ref, tr_ref, planes_ref, lat_w, lon_w, in_sems, out_sems,
):
    layers = tr_ref.shape[1]
    inv_ref, up_ref, coef_ref = views(planes_ref)
    copies = [
        pltpu.make_async_copy(src, dst, in_sems.at[i])
        for i, (src, dst) in enumerate(((mix_in, mix_ref), (tr_in, tr_ref), (traj_in, traj_ref)))
    ]
    for copy in copies:
        copy.start()
    sent = []

    def send(src, dst):
        sent.append(pltpu.make_async_copy(src, dst, out_sems.at[len(sent)]))
        sent[-1].start()

    copies[0].wait()
    for k in range(layers):
        diag = jnp.ones_like(mix_ref[0])
        if k > 0:
            diag = diag + mix_ref[k - 1]
        if k < layers - 1:
            diag = diag + mix_ref[k]
        if k > 0:
            diag = diag + mix_ref[k - 1] * up
        inv = 1.0 / diag
        inv_ref[k] = inv
        if k < layers - 1:
            up = -mix_ref[k] * inv
            up_ref[k] = up
    at = pl.ds(5 * layers, 2 * layers - 1)
    send(planes_ref.at[at], planes_out.at[at])
    copies[1].wait()
    lane = lax.broadcasted_iota(jnp.int32, (32, 128), 1)
    row = lax.broadcasted_iota(jnp.int32, (32, 128), 0)

    def coefs(k, _):
        te, tw, tn, ts = (tr_ref[i, k] for i in range(4))
        coef_ref[0][k] = jnp.where(lane == 0, 0.0, pltpu.roll(te, 1, axis=1))
        coef_ref[1][k] = jnp.where(lane == 127, 0.0, pltpu.roll(tw, 127, axis=1))
        coef_ref[2][k] = jnp.where(row == 0, 0.0, pltpu.roll(tn, 1, axis=0))
        coef_ref[3][k] = jnp.where(row == 31, 0.0, pltpu.roll(ts, 31, axis=0))
        coef_ref[4][k] = 1.0 - te - tw - tn - ts
        return 0

    group = layers // 3
    for g in range(3):
        lax.fori_loop(g * group, (g + 1) * group, coefs, 0, unroll=4)
        for i in range(5):
            at = pl.ds(i * layers + g * group, group)
            send(planes_ref.at[at], planes_out.at[at])
    to_north = tr_ref[3, :, 0, :] * mask_ref[0:1, :]
    to_south = tr_ref[2, :, 31, :] * mask_ref[1:2, :]
    odd = mask_ref[2:3, :]
    lat_w[0] = odd * to_north
    lat_w[1] = (1.0 - odd) * to_south
    lat_w[2] = (1.0 - odd) * to_north
    lat_w[3] = odd * to_south
    send(lat_w, lat_out)
    odd = mask_ref[3:4, 0:1]
    ends = end_rows()[:, 0:128]
    for side in range(2):
        flat = None
        for part in split3(tr_ref[side].reshape(layers * 32, 128)):
            term = dot_t(ends, part)
            flat = term if flat is None else flat + term
        flat = flat[side : side + 1, :]
        lon_w[side] = flat * (odd if side else 1.0 - odd)
        lon_w[2 + side] = flat * (1.0 - odd if side else odd)
    send(lon_w, lon_out)
    for copy in copies[2:] + sent:
        copy.wait()


def spread(mask_ref, lon_a, lon_b, lat_a, lat_b, halo, lat_halo):
    tracers, layers, rows, cols = halo.shape
    size = layers * rows
    odd = mask_ref[2:3, :] > 0.5
    lat_halo[0] = jnp.where(odd, lat_a[...], lat_b[...])
    lat_halo[1] = jnp.where(odd, lat_b[...], lat_a[...])
    row = lax.broadcasted_iota(jnp.int32, (4, cols), 0)
    lane = lax.broadcasted_iota(jnp.int32, (4, cols), 1)
    other = (row % 2).astype(F32)
    lon_odd = jnp.broadcast_to(mask_ref[3:4, :], (4, cols))
    spot = (other * lon_odd + (1.0 - other) * (1.0 - lon_odd)) * (cols - 1)
    place = jnp.where(lane.astype(F32) == spot, 1.0, 0.0).astype(BF16)
    for t in range(tracers):
        at = slice(t * size, (t + 1) * size)
        hi, lo = split2(jnp.concatenate([lon_a[:, at], lon_b[:, at]], axis=0))
        both = jnp.concatenate([hi, lo], axis=0)
        spot = lax.dot_general(both, place, (((0,), (0,)), ((), ())), preferred_element_type=F32)
        halo[t] = spot.reshape(layers, rows, cols)


def received(w_ref, halo, lat_halo, t, k):
    value = w_ref[t, k] + halo[t, k]
    row = lax.broadcasted_iota(jnp.int32, (8, 128), 0)
    at = pl.ds(t * w_ref.shape[1] + k, 1)
    top = value[0:8] + jnp.where(row == 0, lat_halo[0, at, :], 0.0)
    low = value[24:32] + jnp.where(row == 7, lat_halo[1, at, :], 0.0)
    return jnp.concatenate([top, value[8:24], low], axis=0)


def step_body(base, force_ref, fixed, outs, v):
    mix_ref, planes_ref, lat_w, lon_w = fixed
    inv_ref, up_ref, coef_ref = views(planes_ref)
    shifts, end_lanes = lane_shifts(), end_rows()
    w_out, lon_a, lon_b, lat_a, lat_b = outs
    tracers, layers, rows, cols = force_ref.shape
    d = tuple((force_ref[t, 0] + base(t, 0)) * inv_ref[0] for t in range(tracers))
    for t in range(tracers):
        v[t, 0] = d[t]

    def forward(k, d):
        m, inv = mix_ref[k - 1], inv_ref[k]
        d = tuple((force_ref[t, k] + base(t, k) + m * d[t]) * inv for t in range(tracers))
        for t in range(tracers):
            v[t, k] = d[t]
        return d

    d = lax.fori_loop(1, layers, forward, d, unroll=5)

    def backward(i, x):
        k = layers - 2 - i
        u = up_ref[k]
        x = tuple(v[t, k] - u * x[t] for t in range(tracers))
        for t in range(tracers):
            v[t, k] = x[t]
        return x

    lax.fori_loop(0, layers - 1, backward, d, unroll=5)

    group = 12
    size = group * rows
    for t in range(tracers):
        for g in range(0, layers, group):
            x = v[t, g : g + group]
            hi, lo = split2(x.reshape(size, cols))
            both = jnp.concatenate([hi, lo], axis=1)
            moved = dot(both, shifts)
            ends = dot_t(end_lanes, both)
            to = pl.ds((t * layers + g) * rows, size)
            at = pl.ds(g * rows, size)
            lon_a[:, to] = ends[0:1, :] * lon_w[0, :, at] + ends[1:2, :] * lon_w[1, :, at]
            lon_b[:, to] = ends[0:1, :] * lon_w[2, :, at] + ends[1:2, :] * lon_w[3, :, at]
            c = [coef_ref[i][g : g + group].reshape(size, cols) for i in range(5)]
            down = jnp.stack([pltpu.roll(x[i], 1, axis=0) for i in range(group)])
            up = jnp.stack([pltpu.roll(x[i], rows - 1, axis=0) for i in range(group)])
            out = c[4] * x.reshape(size, cols) + c[0] * moved[:, :cols] + c[1] * moved[:, cols:]
            out = out + c[2] * down.reshape(size, cols) + c[3] * up.reshape(size, cols)
            w_out[t, g : g + group] = out.reshape(group, rows, cols)

    for t in range(tracers):
        at = slice(t * layers, (t + 1) * layers)
        top, low = v[t, :, 0, :], v[t, :, rows - 1, :]
        lat_a[at, :] = top * lat_w[0] + low * lat_w[1]
        lat_b[at, :] = top * lat_w[2] + low * lat_w[3]


def head_kernel(s, chunk, got_ref, traj_ref, table_in, *refs):
    sources, (out_ref, snd_ref), held = refs[0:4], refs[4:6], refs[6:10]
    pick, weight, table_ref, sem, sems = refs[10:]
    copy = pltpu.make_async_copy(table_in, table_ref, sem)
    copy.start()
    copies = [pltpu.make_async_copy(a, b, sems.at[i]) for i, (a, b) in enumerate(zip(sources, held))]
    for held_copy in copies:
        held_copy.start()
    unpack_kernel(got_ref, snd_ref)
    forcing_body(s, chunk, snd_ref, traj_ref, copy, table_ref, out_ref, pick, weight)
    for held_copy in copies:
        held_copy.wait()


def first_step_kernel(*refs):
    step_body(lambda t, k: 0.0, refs[0], refs[1:5], refs[5:10], refs[10])


def step_kernel(mask_ref, w_in, lon_a, lon_b, lat_a, lat_b, flux_in, *refs):
    force_ref, fixed, outs, (flux_out, v, halo, lat_halo) = refs[0], refs[1:5], refs[5:10], refs[10:]
    spread(mask_ref, lon_a, lon_b, lat_a, lat_b, halo, lat_halo)

    def base(t, k):
        value = received(w_in, halo, lat_halo, t, k)
        if isinstance(k, int):
            flux_out[t] = flux_in[t] + value
        return value

    step_body(base, force_ref, fixed, outs, v)


def last_kernel(
    mask_ref, w_in, lon_a, lon_b, lat_a, lat_b, flux_in, adj_out, flux_out, halo, lat_halo, done, sems
):
    tracers, layers = w_in.shape[:2]
    spread(mask_ref, lon_a, lon_b, lat_a, lat_b, halo, lat_halo)
    copies = []
    for t in range(tracers):

        def finish(k, _):
            done[t, k] = received(w_in, halo, lat_halo, t, k)
            return 0

        group = layers // 3
        for g in range(3):
            lax.fori_loop(g * group, (g + 1) * group, finish, 0, unroll=4)
            at = (t, pl.ds(g * group, group))
            copies.append(pltpu.make_async_copy(done.at[at], adj_out.at[at], sems.at[3 * t + g]))
            copies[-1].start()
    flux_out[...] = flux_in[...] + done[:, 0]
    for copy in copies:
        copy.wait()


def swaps(axis):
    peers = lax.axis_size(axis)
    near = [(i, i + 1 - 2 * (i % 2)) for i in range(peers)]
    return near, [((i + 1) % peers, (j + 1) % peers) for i, j in near]


def exchange(lon_a, lon_b, lat_a, lat_b):
    lat_near, lat_far = swaps("lat")
    lon_near, lon_far = swaps("lon")
    lon_b = lax.ppermute(lon_b, "lon", lon_far)
    lat_b = lax.ppermute(lat_b, "lat", lat_far)
    lon_a = lax.ppermute(lon_a, "lon", lon_near)
    lat_a = lax.ppermute(lat_a, "lat", lat_near)
    return lon_a, lon_b, lat_a, lat_b


def body(
    transport, mixing, trajectory, kernel_table, track_tile, sound_cell, kernel_index, observed, precision
):
    ntiles = lax.axis_size(("lat", "lon"))
    steps, tracers, layers, rows, cols = trajectory.shape
    count = sound_cell.shape[1]
    field = sds(tracers, layers, rows, cols)
    plane = sds(tracers, rows, cols)
    lat_edge = sds(tracers * layers, cols)
    lon_edge = sds(1, tracers * layers * rows)
    slots = ntiles * CAP
    outgoing = call(
        route_kernel,
        sds(ntiles, 2, 128),
        track_tile.transpose(0, 2, 1),
        sound_cell,
        kernel_index,
        observed.transpose(1, 0, 2),
        precision,
        hbm=range(5),
        scratch=(
            pltpu.VMEM((steps, 1, count), jnp.int32),
            pltpu.VMEM((steps, count), jnp.int32),
            pltpu.VMEM((steps, count), jnp.int32),
            pltpu.VMEM((tracers, steps, count), F32),
            pltpu.VMEM((steps, count), F32),
            pltpu.SemaphoreType.DMA((5,)),
        ),
    )
    got = lax.all_to_all(outgoing, ("lat", "lon"), split_axis=0, concat_axis=0, tiled=True)
    lat, lon = lax.axis_index("lat"), lax.axis_index("lon")
    mask = jnp.stack([lat > 0, lat < lax.axis_size("lat") - 1, lat % 2 > 0, lon % 2 > 0]).astype(F32)
    mask = jnp.broadcast_to(mask[:, None], (4, cols))
    planes = (sds(7 * layers - 1, rows, cols),)
    weights = (sds(4, layers, cols), sds(4, 1, layers * rows))
    *fixed, local = call(
        setup_kernel,
        planes + weights + (sds(*trajectory.shape, dtype=BF16),),
        mask,
        mixing,
        transport,
        trajectory,
        hbm=(1, 2, 3),
        hbm_out=range(3),
        scratch=[pltpu.VMEM(x.shape, F32) for x in (mixing, transport) + planes + weights]
        + [pltpu.SemaphoreType.DMA((3,)), pltpu.SemaphoreType.DMA((18,))],
    )
    fixed = (mixing, *fixed)
    table = kernel_table.T
    work = (
        pltpu.VMEM((256, slots), BF16),
        pltpu.VMEM((layers, 16, slots), F32),
        pltpu.VMEM(table.shape, F32),
        pltpu.SemaphoreType.DMA,
    )

    def forcing(s):
        return call(
            functools.partial(forcing_kernel, s, 512),
            field,
            snd,
            local,
            table,
            hbm=(2,),
            scratch=work,
        )

    force, snd, *fixed = call(
        functools.partial(head_kernel, steps - 1, 512),
        (field, sds(steps, 8, slots)) + tuple(sds(*x.shape) for x in fixed),
        got,
        local,
        table,
        *fixed,
        hbm=range(2, 7),
        scratch=work + (pltpu.SemaphoreType.DMA((4,)),),
    )
    v = pltpu.VMEM(field.shape, F32)
    lat_halo = pltpu.VMEM((2,) + lat_edge.shape, F32)
    moved = (field, lon_edge, lon_edge, lat_edge, lat_edge)
    w, *edges = call(first_step_kernel, moved, force, *fixed, scratch=(v,))
    flux = jnp.zeros((tracers, rows, cols), F32)
    for s in range(steps - 2, -1, -1):
        halos = exchange(*edges)
        w, *edges, flux = call(
            step_kernel,
            moved + (plane,),
            mask,
            w,
            *halos,
            flux,
            forcing(s),
            *fixed,
            scratch=(v, v, lat_halo),
        )
    return call(
        last_kernel,
        (field, plane),
        mask,
        w,
        *exchange(*edges),
        flux,
        hbm_out=(0,),
        scratch=(v, lat_halo, v, pltpu.SemaphoreType.DMA((3 * tracers,))),
    )


def solution(mesh):
    return jax.shard_map(
        body,
        mesh=mesh,
        in_specs=(
            P(None, None, "lat", "lon"),
            P(None, "lat", "lon"),
            P(None, None, None, "lat", "lon"),
            P(),
            P(None, ("lat", "lon"), None),
            P(None, ("lat", "lon")),
            P(None, ("lat", "lon")),
            P(None, None, ("lat", "lon")),
            P(None, ("lat", "lon")),
        ),
        out_specs=(P(None, None, "lat", "lon"), P(None, "lat", "lon")),
        check_vma=False,
    )
```

```python
import functools

import jax
import jax.numpy as jnp
from jax import lax
from jax.experimental import pallas as pl
from jax.experimental.pallas import tpu as pltpu
from jax.sharding import PartitionSpec as P

CAP = 8
WORDS = 5
F32 = jnp.float32
BF16 = jnp.bfloat16


def split3(x):
    hi = x.astype(BF16)
    rest = x - hi.astype(F32)
    mid = rest.astype(BF16)
    return hi, mid, (rest - mid.astype(F32)).astype(BF16)


def split2(x):
    hi = x.astype(BF16)
    return hi, (x - hi.astype(F32)).astype(BF16)


def dot(a, b):
    return jnp.dot(a, b, preferred_element_type=F32)


def dot_t(a, b):
    return lax.dot_general(a, b, (((1,), (1,)), ((), ())), preferred_element_type=F32)


VMEM = pl.BlockSpec(memory_space=pltpu.VMEM)
HBM = pl.BlockSpec(memory_space=pltpu.HBM)


def call(kernel, outs, *args, scratch=(), vmem=12 << 20, hbm=(), hbm_out=()):
    outs = tuple(outs) if isinstance(outs, (tuple, list)) else (outs,)
    args = [pltpu.with_memory_space_constraint(a, pltpu.HBM) if i in hbm else a for i, a in enumerate(args)]
    done = pl.pallas_call(
        kernel,
        out_shape=tuple(pltpu.HBM(o.shape, o.dtype) if i in hbm_out else o for i, o in enumerate(outs)),
        in_specs=[HBM if i in hbm else VMEM for i in range(len(args))],
        out_specs=tuple(HBM if i in hbm_out else VMEM for i in range(len(outs))),
        scratch_shapes=list(scratch),
        compiler_params=pltpu.CompilerParams(vmem_limit_bytes=vmem),
    )(*args)
    return done if len(outs) > 1 else done[0]


def sds(*shape, dtype=F32):
    return jax.ShapeDtypeStruct(shape, dtype)


def route_kernel(
    tile_in, cell_in, index_in, obs_in, prec_in, out_ref, tile_ref, cell_ref, index_ref, obs_ref, prec_ref, sems
):
    copies = [
        pltpu.make_async_copy(src, dst, sems.at[i])
        for i, (src, dst) in enumerate(
            (
                (tile_in, tile_ref),
                (cell_in, cell_ref),
                (index_in, index_ref),
                (obs_in, obs_ref),
                (prec_in, prec_ref),
            )
        )
    ]
    for copy in copies:
        copy.start()
    steps, count = cell_ref.shape
    ntiles = out_ref.shape[0]
    tile_ids = lax.broadcasted_iota(jnp.int32, (ntiles, count), 0)
    before = (
        lax.broadcasted_iota(jnp.int32, (count, count), 0)
        < lax.broadcasted_iota(jnp.int32, (count, count), 1)
    ).astype(F32).astype(BF16)
    rank_ids = lax.broadcasted_iota(jnp.int32, (CAP, count), 0)
    pad = jnp.zeros((64 - CAP * WORDS, count), F32)
    half = jnp.zeros((64, count), F32)
    for copy in copies:
        copy.wait()
    for pair in range(steps // 2):
        total = None
        for side in range(2):
            s = 2 * pair + side
            mine = tile_ids == tile_ref[s]
            mine_f = mine.astype(F32)
            mine_b = mine_f.astype(BF16)
            seen = dot(mine_b, before)
            rank = jnp.sum(mine_f * seen, axis=0, keepdims=True).astype(jnp.int32)
            at_rank = rank_ids == rank
            code = (index_ref[s : s + 1, :] * 4096 + cell_ref[s : s + 1, :]).astype(F32)
            words = [code] + [obs_ref[t, s : s + 1, :] for t in range(3)] + [prec_ref[s : s + 1, :]]
            rows = [jnp.where(at_rank, w, 0.0) for w in words]
            block = jnp.concatenate(rows + [pad] + [half], axis=0)
            if side == 1:
                block = jnp.concatenate([half] + rows + [pad], axis=0)
            for part in split3(block):
                term = dot_t(mine_b, part)
                total = term if total is None else total + term
        out_ref[:, pair, :] = total


def unpack_kernel(got_ref, out_ref):
    ntiles = got_ref.shape[0]
    for pair in range(2):
        turned = got_ref[:, pair, :].T
        for side in range(2):
            s = 2 * pair + side
            base = 64 * side
            code = turned[base : base + CAP, :].astype(jnp.int32)
            kidx = code // 4096
            cell = code - kidx * 4096
            row = cell // 128
            col = cell - row * 128
            hi = row // 16
            fields = [hi * 128 + col, row - hi * 16, kidx]
            fields = [f.astype(F32) for f in fields]
            fields += [turned[base + CAP * w : base + CAP * (w + 1), :] for w in range(1, WORDS)]
            for f, value in enumerate(fields):
                for r in range(CAP):
                    out_ref[s, f : f + 1, r * ntiles : (r + 1) * ntiles] = value[r : r + 1, :]
            out_ref[s, 7:8, :] = jnp.zeros((1, CAP * ntiles), F32)


def forcing_kernel(s, chunk, snd_ref, traj_ref, table_ref, out_ref, pick, weight):
    forcing_body(s, chunk, snd_ref, traj_ref.at[s], table_ref, out_ref, pick, weight)


def forcing_body(s, chunk, snd_ref, step_traj, table_ref, out_ref, pick, weight):
    tracers, layers = out_ref.shape[:2]
    slots = snd_ref.shape[2]
    nker = table_ref.shape[2]
    cell_ids = lax.broadcasted_iota(jnp.int32, (256, chunk), 0).astype(F32)
    low_ids = lax.broadcasted_iota(jnp.int32, (16, chunk), 0).astype(F32)
    ker_ids = lax.broadcasted_iota(jnp.int32, (nker, chunk), 0).astype(F32)
    for c in range(slots // chunk):
        at = pl.ds(c * chunk, chunk)
        pick[:, at] = jnp.where(cell_ids == snd_ref[s, 0:1, at], 1.0, 0.0).astype(BF16)
        low = jnp.where(low_ids == snd_ref[s, 1:2, at], 1.0, 0.0)
        ker = jnp.where(ker_ids == snd_ref[s, 2:3, at], 1.0, 0.0).astype(BF16)
        w = dot(table_ref[0], ker) + dot(table_ref[1], ker) + dot(table_ref[2], ker)
        for k in range(layers):
            weight[k, :, at] = w[k : k + 1, :] * low
    for t in range(tracers):
        lhs = jnp.concatenate(
            [
                step_traj[t, :, 0:16, :].reshape(layers * 16, 128),
                step_traj[t, :, 16:32, :].reshape(layers * 16, 128),
            ],
            axis=1,
        )
        force = None
        for c in range(slots // chunk):
            at = pl.ds(c * chunk, chunk)
            sampled = dot(lhs, pick[:, at]).reshape(layers, 16, chunk)
            model = jnp.sum(jnp.sum(sampled * weight[:, :, at], axis=0), axis=0, keepdims=True)
            sc = (model - snd_ref[s, 3 + t : 4 + t, at]) * snd_ref[s, 6:7, at]
            hi, lo = split2((weight[:, :, at] * sc).reshape(layers * 16, chunk))
            term = dot_t(hi, pick[:, at]) + dot_t(lo, pick[:, at])
            force = term if force is None else force + term
        out_ref[t, :, 0:16, :] = force[:, 0:128].reshape(layers, 16, 128)
        out_ref[t, :, 16:32, :] = force[:, 128:256].reshape(layers, 16, 128)


def end_rows():
    row = lax.broadcasted_iota(jnp.int32, (8, 256), 0)
    lane = lax.broadcasted_iota(jnp.int32, (8, 256), 1) % 128
    ends = ((row == 0) & (lane == 127)) | ((row == 1) & (lane == 0))
    return jnp.where(ends, 1.0, 0.0).astype(BF16)


def lane_shifts():
    src = lax.broadcasted_iota(jnp.int32, (256, 256), 0) % 128
    dst = lax.broadcasted_iota(jnp.int32, (256, 256), 1)
    dst = jnp.where(dst < 128, dst - 1, dst - 127)
    return jnp.where(src == dst, 1.0, 0.0).astype(BF16)


def views(planes_ref):
    layers = (planes_ref.shape[0] + 1) // 7
    part = [planes_ref.at[pl.ds(i * layers, layers)] for i in range(6)]
    return part[5], planes_ref.at[pl.ds(6 * layers, layers - 1)], part[:5]


def setup_kernel(
    mask_ref, mix_in, tr_in, traj_in, planes_out, lat_out, lon_out, traj_ref,
    mix_ref, tr_ref, planes_ref, lat_w, lon_w, in_sems, out_sems,
):
    layers = tr_ref.shape[1]
    inv_ref, up_ref, coef_ref = views(planes_ref)
    copies = [
        pltpu.make_async_copy(src, dst, in_sems.at[i])
        for i, (src, dst) in enumerate(((mix_in, mix_ref), (tr_in, tr_ref), (traj_in.at[traj_in.shape[0] - 1], traj_ref)))
    ]
    for copy in copies:
        copy.start()
    sent = []

    def send(src, dst):
        sent.append(pltpu.make_async_copy(src, dst, out_sems.at[len(sent)]))
        sent[-1].start()

    copies[0].wait()
    for k in range(layers):
        diag = jnp.ones_like(mix_ref[0])
        if k > 0:
            diag = diag + mix_ref[k - 1]
        if k < layers - 1:
            diag = diag + mix_ref[k]
        if k > 0:
            diag = diag + mix_ref[k - 1] * up
        inv = 1.0 / diag
        inv_ref[k] = inv
        if k < layers - 1:
            up = -mix_ref[k] * inv
            up_ref[k] = up
    at = pl.ds(5 * layers, 2 * layers - 1)
    send(planes_ref.at[at], planes_out.at[at])
    copies[1].wait()
    lane = lax.broadcasted_iota(jnp.int32, (32, 128), 1)
    row = lax.broadcasted_iota(jnp.int32, (32, 128), 0)

    def coefs(k, _):
        te, tw, tn, ts = (tr_ref[i, k] for i in range(4))
        coef_ref[0][k] = jnp.where(lane == 0, 0.0, pltpu.roll(te, 1, axis=1))
        coef_ref[1][k] = jnp.where(lane == 127, 0.0, pltpu.roll(tw, 127, axis=1))
        coef_ref[2][k] = jnp.where(row == 0, 0.0, pltpu.roll(tn, 1, axis=0))
        coef_ref[3][k] = jnp.where(row == 31, 0.0, pltpu.roll(ts, 31, axis=0))
        coef_ref[4][k] = 1.0 - te - tw - tn - ts
        return 0

    group = layers // 3
    for g in range(3):
        lax.fori_loop(g * group, (g + 1) * group, coefs, 0, unroll=4)
        for i in range(5):
            at = pl.ds(i * layers + g * group, group)
            send(planes_ref.at[at], planes_out.at[at])
    to_north = tr_ref[3, :, 0, :] * mask_ref[0:1, :]
    to_south = tr_ref[2, :, 31, :] * mask_ref[1:2, :]
    odd = mask_ref[2:3, :]
    lat_w[0] = odd * to_north
    lat_w[1] = (1.0 - odd) * to_south
    lat_w[2] = (1.0 - odd) * to_north
    lat_w[3] = odd * to_south
    send(lat_w, lat_out)
    odd = mask_ref[3:4, 0:1]
    ends = end_rows()[:, 0:128]
    for side in range(2):
        flat = None
        for part in split3(tr_ref[side].reshape(layers * 32, 128)):
            term = dot_t(ends, part)
            flat = term if flat is None else flat + term
        flat = flat[side : side + 1, :]
        lon_w[side] = flat * (odd if side else 1.0 - odd)
        lon_w[2 + side] = flat * (1.0 - odd if side else odd)
    send(lon_w, lon_out)
    for copy in copies[2:] + sent:
        copy.wait()


def spread(mask_ref, lon_a, lon_b, lat_a, lat_b, halo):
    tracers, layers, rows, cols = halo.shape
    size = layers * rows
    odd = mask_ref[2:3, :] > 0.5
    row = lax.broadcasted_iota(jnp.int32, (4, cols), 0)
    lane = lax.broadcasted_iota(jnp.int32, (4, cols), 1)
    other = (row % 2).astype(F32)
    lon_odd = jnp.broadcast_to(mask_ref[3:4, :], (4, cols))
    spot = (other * lon_odd + (1.0 - other) * (1.0 - lon_odd)) * (cols - 1)
    place = jnp.where(lane.astype(F32) == spot, 1.0, 0.0).astype(BF16)
    for t in range(tracers):
        at = slice(t * size, (t + 1) * size)
        hi, lo = split2(jnp.concatenate([lon_a[:, at], lon_b[:, at]], axis=0))
        both = jnp.concatenate([hi, lo], axis=0)
        spot = lax.dot_general(both, place, (((0,), (0,)), ((), ())), preferred_element_type=F32)
        halo[t] = spot.reshape(layers, rows, cols)
        at = slice(t * layers, (t + 1) * layers)
        halo[t, :, 0, :] += jnp.where(odd, lat_a[at, :], lat_b[at, :])
        halo[t, :, rows - 1, :] += jnp.where(odd, lat_b[at, :], lat_a[at, :])


def step_body(base, force_ref, fixed, outs, v):
    mix_ref, planes_ref, lat_w, lon_w = fixed
    inv_ref, up_ref, coef_ref = views(planes_ref)
    shifts, end_lanes = lane_shifts(), end_rows()
    w_out, lon_a, lon_b, lat_a, lat_b = outs
    tracers, layers, rows, cols = force_ref.shape
    d = tuple((force_ref[t, 0] + base(t, 0)) * inv_ref[0] for t in range(tracers))
    for t in range(tracers):
        v[t, 0] = d[t]

    def forward(k, d):
        m, inv = mix_ref[k - 1], inv_ref[k]
        d = tuple((force_ref[t, k] + base(t, k) + m * d[t]) * inv for t in range(tracers))
        for t in range(tracers):
            v[t, k] = d[t]
        return d

    d = lax.fori_loop(1, layers, forward, d, unroll=5)

    def backward(i, x):
        k = layers - 2 - i
        u = up_ref[k]
        x = tuple(v[t, k] - u * x[t] for t in range(tracers))
        for t in range(tracers):
            v[t, k] = x[t]
        return x

    lax.fori_loop(0, layers - 1, backward, d, unroll=5)

    group = 12
    size = group * rows
    for t in range(tracers):
        for g in range(0, layers, group):
            x = v[t, g : g + group]
            hi, lo = split2(x.reshape(size, cols))
            both = jnp.concatenate([hi, lo], axis=1)
            moved = dot(both, shifts)
            ends = dot_t(end_lanes, both)
            to = pl.ds((t * layers + g) * rows, size)
            at = pl.ds(g * rows, size)
            lon_a[:, to] = ends[0:1, :] * lon_w[0, :, at] + ends[1:2, :] * lon_w[1, :, at]
            lon_b[:, to] = ends[0:1, :] * lon_w[2, :, at] + ends[1:2, :] * lon_w[3, :, at]
            c = [coef_ref[i][g : g + group].reshape(size, cols) for i in range(5)]
            down = jnp.stack([pltpu.roll(x[i], 1, axis=0) for i in range(group)])
            up = jnp.stack([pltpu.roll(x[i], rows - 1, axis=0) for i in range(group)])
            out = c[4] * x.reshape(size, cols) + c[0] * moved[:, :cols] + c[1] * moved[:, cols:]
            out = out + c[2] * down.reshape(size, cols) + c[3] * up.reshape(size, cols)
            w_out[t, g : g + group] = out.reshape(group, rows, cols)

    for t in range(tracers):
        at = slice(t * layers, (t + 1) * layers)
        top, low = v[t, :, 0, :], v[t, :, rows - 1, :]
        lat_a[at, :] = top * lat_w[0] + low * lat_w[1]
        lat_b[at, :] = top * lat_w[2] + low * lat_w[3]


def head_kernel(s, chunk, got_ref, traj_ref, table_in, traj_in, *refs):
    sources, (out_ref, snd_ref, parts_ref, rest_ref), held = refs[0:4], refs[4:8], refs[8:12]
    pick, weight, table_ref, sem, sems = refs[12:]
    table_copy = pltpu.make_async_copy(table_in, table_ref, sem)
    table_copy.start()
    pairs = list(zip(sources, held)) + [(traj_in.at[pl.ds(0, s)], rest_ref)]
    copies = [pltpu.make_async_copy(a, b, sems.at[i]) for i, (a, b) in enumerate(pairs)]
    for copy in copies:
        copy.start()
    unpack_kernel(got_ref, snd_ref)
    table_copy.wait()
    for i, part in enumerate(split3(table_ref[...])):
        parts_ref[i] = part
    forcing_body(s, chunk, snd_ref, traj_ref, parts_ref, out_ref, pick, weight)
    for copy in copies:
        copy.wait()


def first_step_kernel(*refs):
    step_body(lambda t, k: 0.0, refs[0], refs[1:5], refs[5:10], refs[10])


def step_kernel(mask_ref, w_in, lat_b, lat_a, lon_b, lon_a, flux_in, *refs):
    force_ref, fixed, outs, (flux_out, v, halo) = refs[0], refs[1:5], refs[5:10], refs[10:]
    spread(mask_ref, lon_a, lon_b, lat_a, lat_b, halo)

    def base(t, k):
        value = w_in[t, k] + halo[t, k]
        if isinstance(k, int):
            flux_out[t] = flux_in[t] + value
        return value

    step_body(base, force_ref, fixed, outs, v)


def last_kernel(
    mask_ref, w_in, lat_b, lat_a, lon_b, lon_a, flux_in, adj_out, flux_out, halo, done, sems
):
    tracers, layers = w_in.shape[:2]
    spread(mask_ref, lon_a, lon_b, lat_a, lat_b, halo)
    copies = []
    group = layers // 3
    for t in range(tracers):
        for g in range(3):
            at = (t, pl.ds(g * group, group))
            done[at] = w_in[at] + halo[at]
            copies.append(pltpu.make_async_copy(done.at[at], adj_out.at[at], sems.at[3 * t + g]))
            copies[-1].start()
    flux_out[...] = flux_in[...] + done[:, 0]
    for copy in copies:
        copy.wait()


def swaps(axis):
    peers = lax.axis_size(axis)
    near = [(i, i + 1 - 2 * (i % 2)) for i in range(peers)]
    return near, [((i + 1) % peers, (j + 1) % peers) for i, j in near]


def exchange(lon_a, lon_b, lat_a, lat_b):
    lat_near, lat_far = swaps("lat")
    lon_near, lon_far = swaps("lon")
    lon_b = lax.ppermute(lon_b, "lon", lon_far)
    lat_b = lax.ppermute(lat_b, "lat", lat_far)
    lon_a = lax.ppermute(lon_a, "lon", lon_near)
    lat_a = lax.ppermute(lat_a, "lat", lat_near)
    return lat_b, lat_a, lon_b, lon_a


def body(
    transport, mixing, trajectory, kernel_table, track_tile, sound_cell, kernel_index, observed, precision
):
    ntiles = lax.axis_size(("lat", "lon"))
    steps, tracers, layers, rows, cols = trajectory.shape
    count = sound_cell.shape[1]
    field = sds(tracers, layers, rows, cols)
    plane = sds(tracers, rows, cols)
    lat_edge = sds(tracers * layers, cols)
    lon_edge = sds(1, 14336)
    slots = ntiles * CAP
    outgoing = call(
        route_kernel,
        sds(ntiles, 2, 128),
        track_tile.transpose(0, 2, 1),
        sound_cell,
        kernel_index,
        observed.transpose(1, 0, 2),
        precision,
        hbm=range(5),
        scratch=(
            pltpu.VMEM((steps, 1, count), jnp.int32),
            pltpu.VMEM((steps, count), jnp.int32),
            pltpu.VMEM((steps, count), jnp.int32),
            pltpu.VMEM((tracers, steps, count), F32),
            pltpu.VMEM((steps, count), F32),
            pltpu.SemaphoreType.DMA((5,)),
        ),
    )
    got = lax.all_to_all(outgoing, ("lat", "lon"), split_axis=0, concat_axis=0, tiled=True)
    lat, lon = lax.axis_index("lat"), lax.axis_index("lon")
    mask = jnp.stack([lat > 0, lat < lax.axis_size("lat") - 1, lat % 2 > 0, lon % 2 > 0]).astype(F32)
    mask = jnp.broadcast_to(mask[:, None], (4, cols))
    planes = (sds(7 * layers - 1, rows, cols),)
    weights = (sds(4, layers, cols), sds(4, 1, layers * rows))
    *fixed, local = call(
        setup_kernel,
        planes + weights + (sds(*trajectory.shape[1:], dtype=BF16),),
        mask,
        mixing,
        transport,
        trajectory,
        hbm=(1, 2, 3),
        hbm_out=range(3),
        scratch=[pltpu.VMEM(x.shape, F32) for x in (mixing, transport) + planes + weights]
        + [pltpu.SemaphoreType.DMA((3,)), pltpu.SemaphoreType.DMA((18,))],
    )
    fixed = (mixing, *fixed)
    table = kernel_table.T
    work = (pltpu.VMEM((256, slots), BF16), pltpu.VMEM((layers, 16, slots), F32))

    force, snd, parts, rest, *fixed = call(
        functools.partial(head_kernel, steps - 1, 512),
        (
            field,
            sds(steps, 8, slots),
            sds(3, *table.shape, dtype=BF16),
            sds(steps - 1, *trajectory.shape[1:], dtype=BF16),
        )
        + tuple(sds(*x.shape) for x in fixed),
        got,
        local,
        table,
        trajectory,
        *fixed,
        hbm=range(2, 8),
        scratch=work
        + (pltpu.VMEM(table.shape, F32), pltpu.SemaphoreType.DMA, pltpu.SemaphoreType.DMA((5,))),
    )

    def forcing(s):
        return call(
            functools.partial(forcing_kernel, s, 512), field, snd, rest, parts, scratch=work
        )

    v = pltpu.VMEM(field.shape, F32)
    moved = (field, lon_edge, lon_edge, lat_edge, lat_edge)
    w, *edges = call(first_step_kernel, moved, force, *fixed, scratch=(v,))
    flux = jnp.zeros((tracers, rows, cols), F32)
    for s in range(steps - 2, -1, -1):
        halos = exchange(*edges)
        w, *edges, flux = call(
            step_kernel,
            moved + (plane,),
            mask,
            w,
            *halos,
            flux,
            forcing(s),
            *fixed,
            scratch=(v, v),
        )
    return call(
        last_kernel,
        (field, plane),
        mask,
        w,
        *exchange(*edges),
        flux,
        hbm_out=(0,),
        scratch=(v, v, pltpu.SemaphoreType.DMA((3 * tracers,))),
    )


def solution(mesh):
    return jax.shard_map(
        body,
        mesh=mesh,
        in_specs=(
            P(None, None, "lat", "lon"),
            P(None, "lat", "lon"),
            P(None, None, None, "lat", "lon"),
            P(),
            P(None, ("lat", "lon"), None),
            P(None, ("lat", "lon")),
            P(None, ("lat", "lon")),
            P(None, None, ("lat", "lon")),
            P(None, ("lat", "lon")),
        ),
        out_specs=(P(None, None, "lat", "lon"), P(None, "lat", "lon")),
        check_vma=False,
    )
```

```python
import functools

import jax
import jax.numpy as jnp
from jax import lax
from jax.experimental import pallas as pl
from jax.experimental.pallas import tpu as pltpu
from jax.sharding import PartitionSpec as P

CAP = 8
WORDS = 5
F32 = jnp.float32
BF16 = jnp.bfloat16


def split3(x):
    hi = x.astype(BF16)
    rest = x - hi.astype(F32)
    mid = rest.astype(BF16)
    return hi, mid, (rest - mid.astype(F32)).astype(BF16)


def split2(x):
    hi = x.astype(BF16)
    return hi, (x - hi.astype(F32)).astype(BF16)


def dot(a, b):
    return jnp.dot(a, b, preferred_element_type=F32)


def dot_t(a, b):
    return lax.dot_general(a, b, (((1,), (1,)), ((), ())), preferred_element_type=F32)


VMEM = pl.BlockSpec(memory_space=pltpu.VMEM)
HBM = pl.BlockSpec(memory_space=pltpu.HBM)


def call(kernel, outs, *args, scratch=(), vmem=12 << 20, hbm=(), hbm_out=()):
    outs = tuple(outs) if isinstance(outs, (tuple, list)) else (outs,)
    args = [pltpu.with_memory_space_constraint(a, pltpu.HBM) if i in hbm else a for i, a in enumerate(args)]
    done = pl.pallas_call(
        kernel,
        out_shape=tuple(pltpu.HBM(o.shape, o.dtype) if i in hbm_out else o for i, o in enumerate(outs)),
        in_specs=[HBM if i in hbm else VMEM for i in range(len(args))],
        out_specs=tuple(HBM if i in hbm_out else VMEM for i in range(len(outs))),
        scratch_shapes=list(scratch),
        compiler_params=pltpu.CompilerParams(vmem_limit_bytes=vmem),
    )(*args)
    return done if len(outs) > 1 else done[0]


def sds(*shape, dtype=F32):
    return jax.ShapeDtypeStruct(shape, dtype)


def route_kernel(
    tile_in, cell_in, index_in, obs_in, prec_in, out_ref, tile_ref, cell_ref, index_ref, obs_ref, prec_ref, sems
):
    copies = [
        pltpu.make_async_copy(src, dst, sems.at[i])
        for i, (src, dst) in enumerate(
            (
                (tile_in, tile_ref),
                (cell_in, cell_ref),
                (index_in, index_ref),
                (obs_in, obs_ref),
                (prec_in, prec_ref),
            )
        )
    ]
    for copy in copies:
        copy.start()
    steps, count = cell_ref.shape
    ntiles = out_ref.shape[0]
    tile_ids = lax.broadcasted_iota(jnp.int32, (ntiles, count), 0)
    before = (
        lax.broadcasted_iota(jnp.int32, (count, count), 0)
        < lax.broadcasted_iota(jnp.int32, (count, count), 1)
    ).astype(F32).astype(BF16)
    rank_ids = lax.broadcasted_iota(jnp.int32, (CAP, count), 0)
    pad = jnp.zeros((64 - CAP * WORDS, count), F32)
    half = jnp.zeros((64, count), F32)
    for copy in copies:
        copy.wait()
    for pair in range(steps // 2):
        total = None
        for side in range(2):
            s = 2 * pair + side
            mine = tile_ids == tile_ref[s]
            mine_f = mine.astype(F32)
            mine_b = mine_f.astype(BF16)
            seen = dot(mine_b, before)
            rank = jnp.sum(mine_f * seen, axis=0, keepdims=True).astype(jnp.int32)
            at_rank = rank_ids == rank
            code = (index_ref[s : s + 1, :] * 4096 + cell_ref[s : s + 1, :]).astype(F32)
            words = [code] + [obs_ref[t, s : s + 1, :] for t in range(3)] + [prec_ref[s : s + 1, :]]
            rows = [jnp.where(at_rank, w, 0.0) for w in words]
            block = jnp.concatenate(rows + [pad] + [half], axis=0)
            if side == 1:
                block = jnp.concatenate([half] + rows + [pad], axis=0)
            for part in split3(block):
                term = dot_t(mine_b, part)
                total = term if total is None else total + term
        out_ref[:, pair, :] = total


def unpack_kernel(got_ref, out_ref):
    ntiles = got_ref.shape[0]
    for pair in range(2):
        turned = got_ref[:, pair, :].T
        for side in range(2):
            s = 2 * pair + side
            base = 64 * side
            code = turned[base : base + CAP, :].astype(jnp.int32)
            kidx = code // 4096
            cell = code - kidx * 4096
            row = cell // 128
            col = cell - row * 128
            hi = row // 16
            fields = [hi * 128 + col, row - hi * 16, kidx]
            fields = [f.astype(F32) for f in fields]
            fields += [turned[base + CAP * w : base + CAP * (w + 1), :] for w in range(1, WORDS)]
            for f, value in enumerate(fields):
                for r in range(CAP):
                    out_ref[s, f : f + 1, r * ntiles : (r + 1) * ntiles] = value[r : r + 1, :]
            out_ref[s, 7:8, :] = jnp.zeros((1, CAP * ntiles), F32)


def forcing_kernel(s, chunk, snd_ref, traj_ref, table_ref, *refs):
    if s == 0:
        out_ref, pick, weight = refs
    else:
        traj_in, out_ref, next_ref, pick, weight, sem = refs
        copy = pltpu.make_async_copy(traj_in.at[s - 1], next_ref, sem)
        copy.start()
    forcing_body(s, chunk, snd_ref, traj_ref, table_ref, out_ref, pick, weight)
    if s > 0:
        copy.wait()


def forcing_body(s, chunk, snd_ref, step_traj, table_ref, out_ref, pick, weight):
    tracers, layers = out_ref.shape[:2]
    slots = snd_ref.shape[2]
    nker = table_ref.shape[2]
    cell_ids = lax.broadcasted_iota(jnp.int32, (256, chunk), 0).astype(F32)
    low_ids = lax.broadcasted_iota(jnp.int32, (16, chunk), 0).astype(F32)
    ker_ids = lax.broadcasted_iota(jnp.int32, (nker, chunk), 0).astype(F32)
    for c in range(slots // chunk):
        at = pl.ds(c * chunk, chunk)
        pick[:, at] = jnp.where(cell_ids == snd_ref[s, 0:1, at], 1.0, 0.0).astype(BF16)
        low = jnp.where(low_ids == snd_ref[s, 1:2, at], 1.0, 0.0)
        ker = jnp.where(ker_ids == snd_ref[s, 2:3, at], 1.0, 0.0).astype(BF16)
        w = dot(table_ref[0], ker) + dot(table_ref[1], ker) + dot(table_ref[2], ker)
        for k in range(layers):
            weight[k, :, at] = w[k : k + 1, :] * low
    for t in range(tracers):
        lhs = jnp.concatenate(
            [
                step_traj[t, :, 0:16, :].reshape(layers * 16, 128),
                step_traj[t, :, 16:32, :].reshape(layers * 16, 128),
            ],
            axis=1,
        )
        force = None
        for c in range(slots // chunk):
            at = pl.ds(c * chunk, chunk)
            sampled = dot(lhs, pick[:, at]).reshape(layers, 16, chunk)
            model = jnp.sum(jnp.sum(sampled * weight[:, :, at], axis=0), axis=0, keepdims=True)
            sc = (model - snd_ref[s, 3 + t : 4 + t, at]) * snd_ref[s, 6:7, at]
            hi, lo = split2((weight[:, :, at] * sc).reshape(layers * 16, chunk))
            term = dot_t(hi, pick[:, at]) + dot_t(lo, pick[:, at])
            force = term if force is None else force + term
        out_ref[t, :, 0:16, :] = force[:, 0:128].reshape(layers, 16, 128)
        out_ref[t, :, 16:32, :] = force[:, 128:256].reshape(layers, 16, 128)


def end_rows():
    row = lax.broadcasted_iota(jnp.int32, (8, 256), 0)
    lane = lax.broadcasted_iota(jnp.int32, (8, 256), 1) % 128
    ends = ((row == 0) & (lane == 127)) | ((row == 1) & (lane == 0))
    return jnp.where(ends, 1.0, 0.0).astype(BF16)


def lane_shifts():
    src = lax.broadcasted_iota(jnp.int32, (256, 256), 0) % 128
    dst = lax.broadcasted_iota(jnp.int32, (256, 256), 1)
    dst = jnp.where(dst < 128, dst - 1, dst - 127)
    return jnp.where(src == dst, 1.0, 0.0).astype(BF16)


def columns(column_ref, layers):
    at = [0, layers - 1, 2 * layers - 1]
    sizes = [layers - 1, layers, layers - 1]
    return [column_ref.at[pl.ds(a, n)] for a, n in zip(at, sizes)]


def setup_kernel(
    mask_ref, mix_in, tr_in, traj_in, coef_out, column_ref, lat_w, lon_w, traj_ref,
    tr_ref, flat_ref, in_sems, out_sems,
):
    layers = tr_ref.shape[1]
    mix_ref, inv_ref, up_ref = columns(column_ref, layers)
    copies = [
        pltpu.make_async_copy(src, dst, in_sems.at[i])
        for i, (src, dst) in enumerate(((mix_in, mix_ref), (tr_in, tr_ref), (traj_in.at[traj_in.shape[0] - 1], traj_ref)))
    ]
    for copy in copies:
        copy.start()
    sent = []

    def send(src, dst):
        sent.append(pltpu.make_async_copy(src, dst, out_sems.at[len(sent)]))
        sent[-1].start()

    copies[0].wait()
    for k in range(layers):
        diag = jnp.ones_like(mix_ref[0])
        if k > 0:
            diag = diag + mix_ref[k - 1]
        if k < layers - 1:
            diag = diag + mix_ref[k]
        if k > 0:
            diag = diag + mix_ref[k - 1] * up
        inv = 1.0 / diag
        inv_ref[k] = inv
        if k < layers - 1:
            up = -mix_ref[k] * inv
            up_ref[k] = up
    copies[1].wait()
    lane = lax.broadcasted_iota(jnp.int32, (32, 128), 1)
    row = lax.broadcasted_iota(jnp.int32, (32, 128), 0)

    def coefs(k, _):
        te, tw, tn, ts = (tr_ref[i, k] for i in range(4))
        flat_ref[0 * layers + k] = jnp.where(lane == 0, 0.0, pltpu.roll(te, 1, axis=1))
        flat_ref[1 * layers + k] = jnp.where(lane == 127, 0.0, pltpu.roll(tw, 127, axis=1))
        flat_ref[2 * layers + k] = jnp.where(row == 0, 0.0, pltpu.roll(tn, 1, axis=0))
        flat_ref[3 * layers + k] = jnp.where(row == 31, 0.0, pltpu.roll(ts, 31, axis=0))
        flat_ref[4 * layers + k] = 1.0 - te - tw - tn - ts
        return 0

    group = layers // 3
    for g in range(3):
        lax.fori_loop(g * group, (g + 1) * group, coefs, 0, unroll=4)
        for i in range(5):
            at = pl.ds(i * layers + g * group, group)
            send(flat_ref.at[at], coef_out.at[at])
    to_north = tr_ref[3, :, 0, :] * mask_ref[0:1, :]
    to_south = tr_ref[2, :, 31, :] * mask_ref[1:2, :]
    odd = mask_ref[2:3, :]
    lat_w[0] = odd * to_north
    lat_w[1] = (1.0 - odd) * to_south
    lat_w[2] = (1.0 - odd) * to_north
    lat_w[3] = odd * to_south
    odd = mask_ref[3:4, 0:1]
    ends = end_rows()[:, 0:128]
    for side in range(2):
        flat = None
        for part in split3(tr_ref[side].reshape(layers * 32, 128)):
            term = dot_t(ends, part)
            flat = term if flat is None else flat + term
        flat = flat[side : side + 1, :]
        lon_w[side] = flat * (odd if side else 1.0 - odd)
        lon_w[2 + side] = flat * (1.0 - odd if side else odd)
    for copy in copies[2:] + sent:
        copy.wait()


def spread(mask_ref, lon_a, lon_b, lat_a, lat_b, halo):
    tracers, layers, rows, cols = halo.shape
    size = layers * rows
    odd = mask_ref[2:3, :] > 0.5
    row = lax.broadcasted_iota(jnp.int32, (4, cols), 0)
    lane = lax.broadcasted_iota(jnp.int32, (4, cols), 1)
    other = (row % 2).astype(F32)
    lon_odd = jnp.broadcast_to(mask_ref[3:4, :], (4, cols))
    spot = (other * lon_odd + (1.0 - other) * (1.0 - lon_odd)) * (cols - 1)
    place = jnp.where(lane.astype(F32) == spot, 1.0, 0.0).astype(BF16)
    for t in range(tracers):
        at = slice(t * size, (t + 1) * size)
        hi, lo = split2(jnp.concatenate([lon_a[:, at], lon_b[:, at]], axis=0))
        both = jnp.concatenate([hi, lo], axis=0)
        spot = lax.dot_general(both, place, (((0,), (0,)), ((), ())), preferred_element_type=F32)
        halo[t] = spot.reshape(layers, rows, cols)
        at = slice(t * layers, (t + 1) * layers)
        halo[t, :, 0, :] += jnp.where(odd, lat_a[at, :], lat_b[at, :])
        halo[t, :, rows - 1, :] += jnp.where(odd, lat_b[at, :], lat_a[at, :])


def vertical(base, force_ref, column_ref, v):
    tracers, layers = v.shape[:2]
    mix_ref, inv_ref, up_ref = columns(column_ref, layers)
    d = tuple((force_ref[t, 0] + base(t, 0)) * inv_ref[0] for t in range(tracers))
    for t in range(tracers):
        v[t, 0] = d[t]

    def forward(k, d):
        m, inv = mix_ref[k - 1], inv_ref[k]
        d = tuple((force_ref[t, k] + base(t, k) + m * d[t]) * inv for t in range(tracers))
        for t in range(tracers):
            v[t, k] = d[t]
        return d

    d = lax.fori_loop(1, layers, forward, d, unroll=5)

    def backward(i, x):
        k = layers - 2 - i
        u = up_ref[k]
        x = tuple(v[t, k] - u * x[t] for t in range(tracers))
        for t in range(tracers):
            v[t, k] = x[t]
        return x

    lax.fori_loop(0, layers - 1, backward, d, unroll=5)


def horizontal(v, coef_ref=None, w_out=None, weights=None, edges=None):
    tracers, layers, rows, cols = v.shape
    shifts, end_lanes = lane_shifts(), end_rows()
    group = 12
    size = group * rows
    for t in range(tracers):
        for g in range(0, layers, group):
            x = v[t, g : g + group]
            both = jnp.concatenate(split2(x.reshape(size, cols)), axis=1)
            if edges is not None:
                (_, lon_w), (lon_a, lon_b) = weights, edges[:2]
                ends = dot_t(end_lanes, both)
                to = pl.ds((t * layers + g) * rows, size)
                at = pl.ds(g * rows, size)
                lon_a[:, to] = ends[0:1, :] * lon_w[0, :, at] + ends[1:2, :] * lon_w[1, :, at]
                lon_b[:, to] = ends[0:1, :] * lon_w[2, :, at] + ends[1:2, :] * lon_w[3, :, at]
            if w_out is not None:
                moved = dot(both, shifts)
                c = [coef_ref[i * layers + g : i * layers + g + group].reshape(size, cols) for i in range(5)]
                down = jnp.stack([pltpu.roll(x[i], 1, axis=0) for i in range(group)])
                up = jnp.stack([pltpu.roll(x[i], rows - 1, axis=0) for i in range(group)])
                out = c[4] * x.reshape(size, cols) + c[0] * moved[:, :cols] + c[1] * moved[:, cols:]
                out = out + c[2] * down.reshape(size, cols) + c[3] * up.reshape(size, cols)
                w_out[t, g : g + group] = out.reshape(group, rows, cols)
        if edges is not None:
            (lat_w, _), (lat_a, lat_b) = weights, edges[2:]
            at = slice(t * layers, (t + 1) * layers)
            top, low = v[t, :, 0, :], v[t, :, rows - 1, :]
            lat_a[at, :] = top * lat_w[0] + low * lat_w[1]
            lat_b[at, :] = top * lat_w[2] + low * lat_w[3]


def head_kernel(
    s, chunk, got_ref, traj_ref, table_in, traj_in, coef_in,
    out_ref, snd_ref, parts_ref, next_ref, coef_ref, pick, weight, table_ref, sems,
):
    pairs = ((table_in, table_ref), (traj_in.at[s - 1], next_ref), (coef_in, coef_ref))
    copies = [pltpu.make_async_copy(a, b, sems.at[i]) for i, (a, b) in enumerate(pairs)]
    for copy in copies:
        copy.start()
    unpack_kernel(got_ref, snd_ref)
    copies[0].wait()
    for i, part in enumerate(split3(table_ref[...])):
        parts_ref[i] = part
    forcing_body(s, chunk, snd_ref, traj_ref, parts_ref, out_ref, pick, weight)
    for copy in copies[1:]:
        copy.wait()


def first_step_kernel(force_ref, column_ref, coef_ref, lat_w, lon_w, w_out, *refs):
    edges, v = refs[:4], refs[4]
    vertical(lambda t, k: 0.0, force_ref, column_ref, v)
    horizontal(v, coef_ref, w_out, (lat_w, lon_w), edges)


def step_kernel(
    whole, mask_ref, w_in, lat_b, lat_a, lon_b, lon_a, flux_in, force_ref, column_ref, coef_ref, lat_w, lon_w,
    w_out, *refs,
):
    edges, flux_out, halo, v = refs[:4], refs[4], refs[5], refs[6] if whole else w_out
    spread(mask_ref, lon_a, lon_b, lat_a, lat_b, halo)

    def base(t, k):
        value = w_in[t, k] + halo[t, k]
        if isinstance(k, int):
            flux_out[t] = flux_in[t] + value
        return value

    vertical(base, force_ref, column_ref, v)
    horizontal(v, coef_ref if whole else None, w_out if whole else None, (lat_w, lon_w), edges)


def interior_kernel(v, coef_ref, w_out):
    horizontal(v, coef_ref, w_out)


def last_kernel(
    mask_ref, w_in, lat_b, lat_a, lon_b, lon_a, flux_in, adj_out, flux_out, halo, done, sems
):
    tracers, layers = w_in.shape[:2]
    spread(mask_ref, lon_a, lon_b, lat_a, lat_b, halo)
    copies = []
    group = layers // 3
    for t in range(tracers):
        for g in range(3):
            at = (t, pl.ds(g * group, group))
            done[at] = w_in[at] + halo[at]
            copies.append(pltpu.make_async_copy(done.at[at], adj_out.at[at], sems.at[3 * t + g]))
            copies[-1].start()
    flux_out[...] = flux_in[...] + done[:, 0]
    for copy in copies:
        copy.wait()


def swaps(axis):
    peers = lax.axis_size(axis)
    near = [(i, i + 1 - 2 * (i % 2)) for i in range(peers)]
    return near, [((i + 1) % peers, (j + 1) % peers) for i, j in near]


def exchange(lon_a, lon_b, lat_a, lat_b):
    lat_near, lat_far = swaps("lat")
    lon_near, lon_far = swaps("lon")
    lon_b = lax.ppermute(lon_b, "lon", lon_far)
    lat_b = lax.ppermute(lat_b, "lat", lat_far)
    lon_a = lax.ppermute(lon_a, "lon", lon_near)
    lat_a = lax.ppermute(lat_a, "lat", lat_near)
    return lat_b, lat_a, lon_b, lon_a


def body(
    transport, mixing, trajectory, kernel_table, track_tile, sound_cell, kernel_index, observed, precision
):
    ntiles = lax.axis_size(("lat", "lon"))
    steps, tracers, layers, rows, cols = trajectory.shape
    count = sound_cell.shape[1]
    field = sds(tracers, layers, rows, cols)
    plane = sds(tracers, rows, cols)
    lat_edge = sds(tracers * layers, cols)
    lon_edge = sds(1, 14336)
    slots = ntiles * CAP
    outgoing = call(
        route_kernel,
        sds(ntiles, 2, 128),
        track_tile.transpose(0, 2, 1),
        sound_cell,
        kernel_index,
        observed.transpose(1, 0, 2),
        precision,
        hbm=range(5),
        scratch=(
            pltpu.VMEM((steps, 1, count), jnp.int32),
            pltpu.VMEM((steps, count), jnp.int32),
            pltpu.VMEM((steps, count), jnp.int32),
            pltpu.VMEM((tracers, steps, count), F32),
            pltpu.VMEM((steps, count), F32),
            pltpu.SemaphoreType.DMA((5,)),
        ),
    )
    got = lax.all_to_all(outgoing, ("lat", "lon"), split_axis=0, concat_axis=0, tiled=True)
    lat, lon = lax.axis_index("lat"), lax.axis_index("lon")
    mask = jnp.stack([lat > 0, lat < lax.axis_size("lat") - 1, lat % 2 > 0, lon % 2 > 0]).astype(F32)
    mask = jnp.broadcast_to(mask[:, None], (4, cols))
    one_step = sds(*trajectory.shape[1:], dtype=BF16)
    coef, column, lat_w, lon_w, now = call(
        setup_kernel,
        (
            sds(5 * layers, rows, cols),
            sds(3 * layers - 2, rows, cols),
            sds(4, layers, cols),
            sds(4, 1, layers * rows),
            one_step,
        ),
        mask,
        mixing,
        transport,
        trajectory,
        hbm=(1, 2, 3),
        hbm_out=(0,),
        scratch=(
            pltpu.VMEM(transport.shape, F32),
            pltpu.VMEM((5 * layers, rows, cols), F32),
            pltpu.SemaphoreType.DMA((3,)),
            pltpu.SemaphoreType.DMA((15,)),
        ),
    )
    table = kernel_table.T
    work = (pltpu.VMEM((256, slots), BF16), pltpu.VMEM((layers, 16, slots), F32))
    force, snd, parts, now, coef = call(
        functools.partial(head_kernel, steps - 1, 512),
        (
            field,
            sds(steps, 8, slots),
            sds(3, *table.shape, dtype=BF16),
            one_step,
            sds(*coef.shape),
        ),
        got,
        now,
        table,
        trajectory,
        coef,
        hbm=(2, 3, 4),
        scratch=work + (pltpu.VMEM(table.shape, F32), pltpu.SemaphoreType.DMA((3,))),
    )
    fixed = (column, coef, lat_w, lon_w)

    def forcing(s, now):
        kernel = functools.partial(forcing_kernel, s, 512)
        if s == 0:
            return call(kernel, field, snd, now, parts, scratch=work), None
        return call(
            kernel,
            (field, one_step),
            snd,
            now,
            parts,
            trajectory,
            hbm=(3,),
            scratch=work + (pltpu.SemaphoreType.DMA,),
        )

    v = pltpu.VMEM(field.shape, F32)
    moved = (field, lon_edge, lon_edge, lat_edge, lat_edge)
    w, *edges = call(first_step_kernel, moved, force, *fixed, scratch=(v,))
    flux = jnp.zeros((tracers, rows, cols), F32)
    for s in range(steps - 2, -1, -1):
        halos = exchange(*edges)
        force, now = forcing(s, now)
        w, *edges, flux = call(
            functools.partial(step_kernel, s > 0),
            moved + (plane,),
            mask,
            w,
            *halos,
            flux,
            force,
            *fixed,
            scratch=(v, v) if s > 0 else (v,),
        )
    return call(
        last_kernel,
        (field, plane),
        mask,
        call(interior_kernel, field, w, coef),
        *exchange(*edges),
        flux,
        hbm_out=(0,),
        scratch=(v, v, pltpu.SemaphoreType.DMA((3 * tracers,))),
    )


def solution(mesh):
    return jax.shard_map(
        body,
        mesh=mesh,
        in_specs=(
            P(None, None, "lat", "lon"),
            P(None, "lat", "lon"),
            P(None, None, None, "lat", "lon"),
            P(),
            P(None, ("lat", "lon"), None),
            P(None, ("lat", "lon")),
            P(None, ("lat", "lon")),
            P(None, None, ("lat", "lon")),
            P(None, ("lat", "lon")),
        ),
        out_specs=(P(None, None, "lat", "lon"), P(None, "lat", "lon")),
        check_vma=False,
    )
```

```python
import functools

import jax
import jax.numpy as jnp
from jax import lax
from jax.experimental import pallas as pl
from jax.experimental.pallas import tpu as pltpu
from jax.sharding import PartitionSpec as P

CAP = 8
WORDS = 5
F32 = jnp.float32
BF16 = jnp.bfloat16


def split3(x):
    hi = x.astype(BF16)
    rest = x - hi.astype(F32)
    mid = rest.astype(BF16)
    return hi, mid, (rest - mid.astype(F32)).astype(BF16)


def split2(x):
    hi = x.astype(BF16)
    return hi, (x - hi.astype(F32)).astype(BF16)


def dot(a, b):
    return jnp.dot(a, b, preferred_element_type=F32)


def dot_t(a, b):
    return lax.dot_general(a, b, (((1,), (1,)), ((), ())), preferred_element_type=F32)


VMEM = pl.BlockSpec(memory_space=pltpu.VMEM)
HBM = pl.BlockSpec(memory_space=pltpu.HBM)


def call(kernel, outs, *args, scratch=(), vmem=20 << 20, hbm=(), hbm_out=()):
    outs = tuple(outs) if isinstance(outs, (tuple, list)) else (outs,)
    args = [pltpu.with_memory_space_constraint(a, pltpu.HBM) if i in hbm else a for i, a in enumerate(args)]
    done = pl.pallas_call(
        kernel,
        out_shape=tuple(pltpu.HBM(o.shape, o.dtype) if i in hbm_out else o for i, o in enumerate(outs)),
        in_specs=[HBM if i in hbm else VMEM for i in range(len(args))],
        out_specs=tuple(HBM if i in hbm_out else VMEM for i in range(len(outs))),
        scratch_shapes=list(scratch),
        compiler_params=pltpu.CompilerParams(vmem_limit_bytes=vmem),
    )(*args)
    return done if len(outs) > 1 else done[0]


def sds(*shape, dtype=F32):
    return jax.ShapeDtypeStruct(shape, dtype)


def route_kernel(
    tile_in, cell_in, index_in, obs_in, prec_in, out_ref, tile_ref, cell_ref, index_ref, obs_ref, prec_ref, sems
):
    copies = [
        pltpu.make_async_copy(src, dst, sems.at[i])
        for i, (src, dst) in enumerate(
            (
                (tile_in, tile_ref),
                (cell_in, cell_ref),
                (index_in, index_ref),
                (obs_in, obs_ref),
                (prec_in, prec_ref),
            )
        )
    ]
    for copy in copies:
        copy.start()
    steps, count = cell_ref.shape
    ntiles = out_ref.shape[0]
    tile_ids = lax.broadcasted_iota(jnp.int32, (ntiles, count), 0)
    before = (
        lax.broadcasted_iota(jnp.int32, (count, count), 0)
        < lax.broadcasted_iota(jnp.int32, (count, count), 1)
    ).astype(F32).astype(BF16)
    rank_ids = lax.broadcasted_iota(jnp.int32, (CAP, count), 0)
    pad = jnp.zeros((48 - CAP * WORDS, count), F32)
    empty = [jnp.zeros((n, count), BF16) for n in (64, 16)]
    copies[0].wait()
    mine, at_rank = [], []
    for s in range(steps):
        here = tile_ids == tile_ref[s]
        here_f = jnp.where(here, 1.0, 0.0)
        mine.append(here_f.astype(BF16))
        rank = jnp.sum(here_f * dot(mine[s], before), axis=0, keepdims=True).astype(jnp.int32)
        at_rank.append(rank_ids == rank)
    for copy in copies[1:]:
        copy.wait()
    for pair in range(steps // 2):
        total = None
        for side in range(2):
            s = 2 * pair + side
            code = (index_ref[s : s + 1, :] * 4096 + cell_ref[s : s + 1, :]).astype(F32)
            words = [code] + [obs_ref[t, s : s + 1, :] for t in range(3)] + [prec_ref[s : s + 1, :]]
            rows = jnp.concatenate([jnp.where(at_rank[s], w, 0.0) for w in words] + [pad], axis=0)
            for part in split3(rows):
                block = [part, empty[1], empty[0]] if side == 0 else [empty[0], part, empty[1]]
                term = dot_t(mine[s], jnp.concatenate(block, axis=0))
                total = term if total is None else total + term
        out_ref[:, pair, :] = total


def unpack_kernel(got_ref, out_ref):
    ntiles = got_ref.shape[0]
    for pair in range(2):
        turned = got_ref[:, pair, :].T
        for side in range(2):
            s = 2 * pair + side
            base = 64 * side
            code = turned[base : base + CAP, :].astype(jnp.int32)
            kidx = code // 4096
            cell = code - kidx * 4096
            row = cell // 128
            col = cell - row * 128
            hi = row // 16
            fields = [hi * 128 + col, row - hi * 16, kidx]
            fields = [f.astype(F32) for f in fields]
            fields += [turned[base + CAP * w : base + CAP * (w + 1), :] for w in range(1, WORDS)]
            for f, value in enumerate(fields):
                for r in range(CAP):
                    out_ref[s, f : f + 1, r * ntiles : (r + 1) * ntiles] = value[r : r + 1, :]
            out_ref[s, 7:8, :] = jnp.zeros((1, CAP * ntiles), F32)


def forcing_kernel(s, chunk, snd_ref, traj_ref, table_ref, *refs):
    if s == 0:
        out_ref, pick, weight = refs
    else:
        traj_in, out_ref, next_ref, pick, weight, sem = refs
        copy = pltpu.make_async_copy(traj_in.at[s - 1], next_ref, sem)
        copy.start()
    forcing_body(s, chunk, snd_ref, traj_ref, table_ref, out_ref, pick, weight)
    if s > 0:
        copy.wait()


def forcing_body(s, chunk, snd_ref, step_traj, table_ref, out_ref, pick, weight):
    tracers, layers = out_ref.shape[:2]
    slots = snd_ref.shape[2]
    nker = table_ref.shape[2]
    cell_ids = lax.broadcasted_iota(jnp.int32, (256, chunk), 0).astype(F32)
    low_ids = lax.broadcasted_iota(jnp.int32, (16, chunk), 0).astype(F32)
    ker_ids = lax.broadcasted_iota(jnp.int32, (nker, chunk), 0).astype(F32)
    for c in range(slots // chunk):
        at = pl.ds(c * chunk, chunk)
        pick[:, at] = jnp.where(cell_ids == snd_ref[s, 0:1, at], 1.0, 0.0).astype(BF16)
        low = jnp.where(low_ids == snd_ref[s, 1:2, at], 1.0, 0.0)
        ker = jnp.where(ker_ids == snd_ref[s, 2:3, at], 1.0, 0.0).astype(BF16)
        w = dot(table_ref[0], ker) + dot(table_ref[1], ker) + dot(table_ref[2], ker)
        for k in range(layers):
            weight[k, :, at] = w[k : k + 1, :] * low
    for t in range(tracers):
        lhs = jnp.concatenate(
            [
                step_traj[t, :, 0:16, :].reshape(layers * 16, 128),
                step_traj[t, :, 16:32, :].reshape(layers * 16, 128),
            ],
            axis=1,
        )
        force = None
        for c in range(slots // chunk):
            at = pl.ds(c * chunk, chunk)
            sampled = dot(lhs, pick[:, at]).reshape(layers, 16, chunk)
            model = jnp.sum(jnp.sum(sampled * weight[:, :, at], axis=0), axis=0, keepdims=True)
            sc = (model - snd_ref[s, 3 + t : 4 + t, at]) * snd_ref[s, 6:7, at]
            hi, lo = split2((weight[:, :, at] * sc).reshape(layers * 16, chunk))
            term = dot_t(hi, pick[:, at]) + dot_t(lo, pick[:, at])
            force = term if force is None else force + term
        out_ref[t, :, 0:16, :] = force[:, 0:128].reshape(layers, 16, 128)
        out_ref[t, :, 16:32, :] = force[:, 128:256].reshape(layers, 16, 128)


def end_rows():
    row = lax.broadcasted_iota(jnp.int32, (8, 256), 0)
    lane = lax.broadcasted_iota(jnp.int32, (8, 256), 1) % 128
    ends = ((row == 0) & (lane == 127)) | ((row == 1) & (lane == 0))
    return jnp.where(ends, 1.0, 0.0).astype(BF16)


def lane_shifts():
    src = lax.broadcasted_iota(jnp.int32, (256, 256), 0) % 128
    dst = lax.broadcasted_iota(jnp.int32, (256, 256), 1)
    dst = jnp.where(dst < 128, dst - 1, dst - 127)
    return jnp.where(src == dst, 1.0, 0.0).astype(BF16)


def columns(column_ref, layers):
    at = [0, layers - 1, 2 * layers - 1]
    sizes = [layers - 1, layers, layers - 1]
    return [column_ref.at[pl.ds(a, n)] for a, n in zip(at, sizes)]


def setup_kernel(
    mask_ref, mix_in, tr_in, traj_in, coef_out, column_ref, lat_w, lon_w, traj_ref,
    tr_ref, flat_ref, in_sems, out_sems,
):
    layers = tr_ref.shape[1]
    mix_ref, inv_ref, up_ref = columns(column_ref, layers)
    copies = [
        pltpu.make_async_copy(src, dst, in_sems.at[i])
        for i, (src, dst) in enumerate(((mix_in, mix_ref), (tr_in, tr_ref), (traj_in.at[traj_in.shape[0] - 1], traj_ref)))
    ]
    for copy in copies:
        copy.start()
    sent = []

    def send(src, dst):
        sent.append(pltpu.make_async_copy(src, dst, out_sems.at[len(sent)]))
        sent[-1].start()

    copies[0].wait()
    for k in range(layers):
        diag = jnp.ones_like(mix_ref[0])
        if k > 0:
            diag = diag + mix_ref[k - 1]
        if k < layers - 1:
            diag = diag + mix_ref[k]
        if k > 0:
            diag = diag + mix_ref[k - 1] * up
        inv = 1.0 / diag
        inv_ref[k] = inv
        if k < layers - 1:
            up = -mix_ref[k] * inv
            up_ref[k] = up
    copies[1].wait()
    lane = lax.broadcasted_iota(jnp.int32, (32, 128), 1)
    row = lax.broadcasted_iota(jnp.int32, (32, 128), 0)

    def coefs(k, _):
        te, tw, tn, ts = (tr_ref[i, k] for i in range(4))
        flat_ref[0 * layers + k] = jnp.where(lane == 0, 0.0, pltpu.roll(te, 1, axis=1))
        flat_ref[1 * layers + k] = jnp.where(lane == 127, 0.0, pltpu.roll(tw, 127, axis=1))
        flat_ref[2 * layers + k] = jnp.where(row == 0, 0.0, pltpu.roll(tn, 1, axis=0))
        flat_ref[3 * layers + k] = jnp.where(row == 31, 0.0, pltpu.roll(ts, 31, axis=0))
        flat_ref[4 * layers + k] = 1.0 - te - tw - tn - ts
        return 0

    group = layers // 3
    for g in range(3):
        lax.fori_loop(g * group, (g + 1) * group, coefs, 0, unroll=4)
        for i in range(5):
            at = pl.ds(i * layers + g * group, group)
            send(flat_ref.at[at], coef_out.at[at])
    to_north = tr_ref[3, :, 0, :] * mask_ref[0:1, :]
    to_south = tr_ref[2, :, 31, :] * mask_ref[1:2, :]
    odd = mask_ref[2:3, :]
    lat_w[0] = odd * to_north
    lat_w[1] = (1.0 - odd) * to_south
    lat_w[2] = (1.0 - odd) * to_north
    lat_w[3] = odd * to_south
    odd = mask_ref[3:4, 0:1]
    ends = end_rows()[:, 0:128]
    for side in range(2):
        flat = None
        for part in split3(tr_ref[side].reshape(layers * 32, 128)):
            term = dot_t(ends, part)
            flat = term if flat is None else flat + term
        flat = flat[side : side + 1, :]
        lon_w[side] = flat * (odd if side else 1.0 - odd)
        lon_w[2 + side] = flat * (1.0 - odd if side else odd)
    for copy in copies[2:] + sent:
        copy.wait()


def lon_spots(mask_ref, lon_a, lon_b, first, size, cols):
    row = lax.broadcasted_iota(jnp.int32, (4, cols), 0)
    lane = lax.broadcasted_iota(jnp.int32, (4, cols), 1)
    other = (row % 2).astype(F32)
    lon_odd = jnp.broadcast_to(mask_ref[3:4, :], (4, cols))
    spot = (other * lon_odd + (1.0 - other) * (1.0 - lon_odd)) * (cols - 1)
    place = jnp.where(lane.astype(F32) == spot, 1.0, 0.0).astype(BF16)
    at = slice(first, first + size)
    hi, lo = split2(jnp.concatenate([lon_a[:, at], lon_b[:, at]], axis=0))
    both = jnp.concatenate([hi, lo], axis=0)
    return lax.dot_general(both, place, (((0,), (0,)), ((), ())), preferred_element_type=F32)


def lat_rows(mask_ref, lat_a, lat_b, layers):
    odd = mask_ref[2:3, :] > 0.5
    a, b = lat_a[...].astype(F32), lat_b[...].astype(F32)
    north, south = jnp.where(odd, a, b), jnp.where(odd, b, a)
    return [(x[0:layers], x[layers : 2 * layers], x[2 * layers :]) for x in (north, south)]


def spread(mask_ref, lon_a, lon_b, lat_a, lat_b, halo):
    tracers, layers, rows, cols = halo.shape
    size = layers * rows
    north, south = lat_rows(mask_ref, lat_a, lat_b, layers)
    for t in range(tracers):
        halo[t] = lon_spots(mask_ref, lon_a, lon_b, t * size, size, cols).reshape(layers, rows, cols)
        halo[t, :, 0, :] += north[t]
        halo[t, :, rows - 1, :] += south[t]


def vertical(base, force_ref, column_ref, v):
    tracers, layers = v.shape[:2]
    mix_ref, inv_ref, up_ref = columns(column_ref, layers)
    d = tuple((force_ref[t, 0] + base(t, 0)) * inv_ref[0] for t in range(tracers))
    for t in range(tracers):
        v[t, 0] = d[t]

    def forward(k, d):
        m, inv = mix_ref[k - 1], inv_ref[k]
        d = tuple((force_ref[t, k] + base(t, k) + m * d[t]) * inv for t in range(tracers))
        for t in range(tracers):
            v[t, k] = d[t]
        return d

    d = lax.fori_loop(1, layers, forward, d, unroll=5)

    def backward(i, x):
        k = layers - 2 - i
        u = up_ref[k]
        x = tuple(v[t, k] - u * x[t] for t in range(tracers))
        for t in range(tracers):
            v[t, k] = x[t]
        return x

    lax.fori_loop(0, layers - 1, backward, d, unroll=5)


def horizontal(v, coef_ref=None, w_out=None, weights=None, edges=None):
    tracers, layers, rows, cols = v.shape
    shifts, end_lanes = lane_shifts(), end_rows()
    group = 12
    size = group * rows
    for t in range(tracers):
        for g in range(0, layers, group):
            x = v[t, g : g + group]
            both = jnp.concatenate(split2(x.reshape(size, cols)), axis=1)
            if edges is not None:
                (_, lon_w), (lon_a, lon_b) = weights, edges[:2]
                ends = dot_t(end_lanes, both)
                to = pl.ds((t * layers + g) * rows, size)
                at = pl.ds(g * rows, size)
                lon_a[:, to] = ends[0:1, :] * lon_w[0, :, at] + ends[1:2, :] * lon_w[1, :, at]
                lon_b[:, to] = ends[0:1, :] * lon_w[2, :, at] + ends[1:2, :] * lon_w[3, :, at]
            if w_out is not None:
                moved = dot(both, shifts)
                c = [coef_ref[i * layers + g : i * layers + g + group].reshape(size, cols) for i in range(5)]
                down = jnp.stack([pltpu.roll(x[i], 1, axis=0) for i in range(group)])
                up = jnp.stack([pltpu.roll(x[i], rows - 1, axis=0) for i in range(group)])
                out = c[4] * x.reshape(size, cols) + c[0] * moved[:, :cols] + c[1] * moved[:, cols:]
                out = out + c[2] * down.reshape(size, cols) + c[3] * up.reshape(size, cols)
                w_out[t, g : g + group] = out.reshape(group, rows, cols)
    if edges is not None:
        (lat_w, _), (lat_a, lat_b) = weights, edges[2:]
        ends = [(v[t, :, 0, :], v[t, :, rows - 1, :]) for t in range(tracers)]
        to_a = [top * lat_w[0] + low * lat_w[1] for top, low in ends]
        to_b = [top * lat_w[2] + low * lat_w[3] for top, low in ends]
        lat_a[...] = jnp.concatenate(to_a, axis=0).astype(BF16)
        lat_b[...] = jnp.concatenate(to_b, axis=0).astype(BF16)


def head_kernel(
    s, chunk, got_ref, traj_ref, table_in, traj_in, coef_in,
    out_ref, snd_ref, parts_ref, next_ref, coef_ref, pick, weight, table_ref, sems,
):
    pairs = ((table_in, table_ref), (traj_in.at[s - 1], next_ref), (coef_in, coef_ref))
    copies = [pltpu.make_async_copy(a, b, sems.at[i]) for i, (a, b) in enumerate(pairs)]
    for copy in copies:
        copy.start()
    unpack_kernel(got_ref, snd_ref)
    copies[0].wait()
    for i, part in enumerate(split3(table_ref[...])):
        parts_ref[i] = part
    forcing_body(s, chunk, snd_ref, traj_ref, parts_ref, out_ref, pick, weight)
    for copy in copies[1:]:
        copy.wait()


def first_step_kernel(force_ref, column_ref, coef_ref, lat_w, lon_w, w_out, *refs):
    edges, v = refs[:4], refs[4]
    vertical(lambda t, k: 0.0, force_ref, column_ref, v)
    horizontal(v, coef_ref, w_out, (lat_w, lon_w), edges)


def step_kernel(
    whole, mask_ref, w_in, lat_b, lat_a, lon_b, lon_a, flux_in, force_ref, column_ref, coef_ref, lat_w, lon_w,
    w_out, *refs,
):
    edges, flux_out, halo, v = refs[:4], refs[4], refs[5], refs[6] if whole else w_out
    spread(mask_ref, lon_a, lon_b, lat_a, lat_b, halo)

    def base(t, k):
        value = w_in[t, k] + halo[t, k]
        if isinstance(k, int):
            flux_out[t] = flux_in[t] + value
        return value

    vertical(base, force_ref, column_ref, v)
    horizontal(v, coef_ref if whole else None, w_out if whole else None, (lat_w, lon_w), edges)


def interior_kernel(v, coef_ref, w_out):
    horizontal(v, coef_ref, w_out)


def last_kernel(
    mask_ref, w_in, lat_b, lat_a, lon_b, lon_a, flux_in, adj_out, flux_out, done, sems
):
    tracers, layers, rows, cols = w_in.shape
    north, south = lat_rows(mask_ref, lat_a, lat_b, layers)
    group = layers // 3
    size = group * rows
    copies = []
    for t in range(tracers):
        for g in range(3):
            first = t * layers * rows + g * size
            at = (t, pl.ds(g * group, group))
            spots = lon_spots(mask_ref, lon_a, lon_b, first, size, cols)
            done[at] = w_in[at] + spots.reshape(group, rows, cols)
            done[t, g * group : (g + 1) * group, 0, :] += north[t][g * group : (g + 1) * group]
            done[t, g * group : (g + 1) * group, rows - 1, :] += south[t][g * group : (g + 1) * group]
            copies.append(pltpu.make_async_copy(done.at[at], adj_out.at[at], sems.at[3 * t + g]))
            copies[-1].start()
    flux_out[...] = flux_in[...] + done[:, 0]
    for copy in copies:
        copy.wait()


def swaps(axis):
    peers = lax.axis_size(axis)
    near = [(i, i + 1 - 2 * (i % 2)) for i in range(peers)]
    return near, [((i + 1) % peers, (j + 1) % peers) for i, j in near]


def exchange(lon_a, lon_b, lat_a, lat_b):
    lat_near, lat_far = swaps("lat")
    lon_near, lon_far = swaps("lon")
    lon_b = lax.ppermute(lon_b, "lon", lon_far)
    lat_b = lax.ppermute(lat_b, "lat", lat_far)
    lon_a = lax.ppermute(lon_a, "lon", lon_near)
    lat_a = lax.ppermute(lat_a, "lat", lat_near)
    return lat_b, lat_a, lon_b, lon_a


def body(
    transport, mixing, trajectory, kernel_table, track_tile, sound_cell, kernel_index, observed, precision
):
    ntiles = lax.axis_size(("lat", "lon"))
    steps, tracers, layers, rows, cols = trajectory.shape
    count = sound_cell.shape[1]
    field = sds(tracers, layers, rows, cols)
    plane = sds(tracers, rows, cols)
    lat_edge = sds(tracers * layers, cols, dtype=BF16)
    lon_edge = sds(1, 7168)
    slots = ntiles * CAP
    outgoing = call(
        route_kernel,
        sds(ntiles, 2, 128),
        track_tile.transpose(0, 2, 1),
        sound_cell,
        kernel_index,
        observed.transpose(1, 0, 2),
        precision,
        hbm=range(5),
        scratch=(
            pltpu.VMEM((steps, 1, count), jnp.int32),
            pltpu.VMEM((steps, count), jnp.int32),
            pltpu.VMEM((steps, count), jnp.int32),
            pltpu.VMEM((tracers, steps, count), F32),
            pltpu.VMEM((steps, count), F32),
            pltpu.SemaphoreType.DMA((5,)),
        ),
    )
    got = lax.all_to_all(outgoing, ("lat", "lon"), split_axis=0, concat_axis=0, tiled=True)
    lat, lon = lax.axis_index("lat"), lax.axis_index("lon")
    mask = jnp.stack([lat > 0, lat < lax.axis_size("lat") - 1, lat % 2 > 0, lon % 2 > 0]).astype(F32)
    mask = jnp.broadcast_to(mask[:, None], (4, cols))
    one_step = sds(*trajectory.shape[1:], dtype=BF16)
    coef, column, lat_w, lon_w, now = call(
        setup_kernel,
        (
            sds(5 * layers, rows, cols),
            sds(3 * layers - 2, rows, cols),
            sds(4, layers, cols),
            sds(4, 1, layers * rows),
            one_step,
        ),
        mask,
        mixing,
        transport,
        trajectory,
        hbm=(1, 2, 3),
        hbm_out=(0,),
        scratch=(
            pltpu.VMEM(transport.shape, F32),
            pltpu.VMEM((5 * layers, rows, cols), F32),
            pltpu.SemaphoreType.DMA((3,)),
            pltpu.SemaphoreType.DMA((15,)),
        ),
    )
    table = kernel_table.T
    work = (pltpu.VMEM((256, slots), BF16), pltpu.VMEM((layers, 16, slots), F32))
    force, snd, parts, now, coef = call(
        functools.partial(head_kernel, steps - 1, slots),
        (
            field,
            sds(steps, 8, slots),
            sds(3, *table.shape, dtype=BF16),
            one_step,
            sds(*coef.shape),
        ),
        got,
        now,
        table,
        trajectory,
        coef,
        hbm=(2, 3, 4),
        scratch=work + (pltpu.VMEM(table.shape, F32), pltpu.SemaphoreType.DMA((3,))),
    )
    fixed = (column, coef, lat_w, lon_w)

    def forcing(s, now):
        kernel = functools.partial(forcing_kernel, s, slots)
        if s == 0:
            return call(kernel, field, snd, now, parts, scratch=work), None
        return call(
            kernel,
            (field, one_step),
            snd,
            now,
            parts,
            trajectory,
            hbm=(3,),
            scratch=work + (pltpu.SemaphoreType.DMA,),
        )

    v = pltpu.VMEM(field.shape, F32)
    moved = (field, lon_edge, lon_edge, lat_edge, lat_edge)
    w, *edges = call(first_step_kernel, moved, force, *fixed, scratch=(v,))
    flux = jnp.zeros((tracers, rows, cols), F32)
    for s in range(steps - 2, -1, -1):
        halos = exchange(*edges)
        force, now = forcing(s, now)
        w, *edges, flux = call(
            functools.partial(step_kernel, s > 0),
            moved + (plane,),
            mask,
            w,
            *halos,
            flux,
            force,
            *fixed,
            scratch=(v, v) if s > 0 else (v,),
        )
    return call(
        last_kernel,
        (field, plane),
        mask,
        call(interior_kernel, field, w, coef),
        *exchange(*edges),
        flux,
        hbm_out=(0,),
        scratch=(v, pltpu.SemaphoreType.DMA((3 * tracers,))),
    )


def solution(mesh):
    return jax.shard_map(
        body,
        mesh=mesh,
        in_specs=(
            P(None, None, "lat", "lon"),
            P(None, "lat", "lon"),
            P(None, None, None, "lat", "lon"),
            P(),
            P(None, ("lat", "lon"), None),
            P(None, ("lat", "lon")),
            P(None, ("lat", "lon")),
            P(None, None, ("lat", "lon")),
            P(None, ("lat", "lon")),
        ),
        out_specs=(P(None, None, "lat", "lon"), P(None, "lat", "lon")),
        check_vma=False,
    )
```

```python
import functools

import jax
import jax.numpy as jnp
from jax import lax
from jax.experimental import pallas as pl
from jax.experimental.pallas import tpu as pltpu
from jax.sharding import PartitionSpec as P

CAP = 8
WORDS = 5
F32 = jnp.float32
BF16 = jnp.bfloat16
F8 = jnp.float8_e4m3fn
LOW = 256.0


def split3(x):
    hi = x.astype(BF16)
    rest = x - hi.astype(F32)
    mid = rest.astype(BF16)
    return hi, mid, (rest - mid.astype(F32)).astype(BF16)


def split2(x):
    hi = x.astype(BF16)
    return hi, (x - hi.astype(F32)).astype(BF16)


def dot(a, b):
    return jnp.dot(a, b, preferred_element_type=F32)


def dot_t(a, b):
    return lax.dot_general(a, b, (((1,), (1,)), ((), ())), preferred_element_type=F32)


VMEM = pl.BlockSpec(memory_space=pltpu.VMEM)
HBM = pl.BlockSpec(memory_space=pltpu.HBM)


def call(kernel, outs, *args, scratch=(), vmem=20 << 20, hbm=(), hbm_out=()):
    outs = tuple(outs) if isinstance(outs, (tuple, list)) else (outs,)
    args = [pltpu.with_memory_space_constraint(a, pltpu.HBM) if i in hbm else a for i, a in enumerate(args)]
    done = pl.pallas_call(
        kernel,
        out_shape=tuple(pltpu.HBM(o.shape, o.dtype) if i in hbm_out else o for i, o in enumerate(outs)),
        in_specs=[HBM if i in hbm else VMEM for i in range(len(args))],
        out_specs=tuple(HBM if i in hbm_out else VMEM for i in range(len(outs))),
        scratch_shapes=list(scratch),
        compiler_params=pltpu.CompilerParams(vmem_limit_bytes=vmem),
    )(*args)
    return done if len(outs) > 1 else done[0]


def sds(*shape, dtype=F32):
    return jax.ShapeDtypeStruct(shape, dtype)


def route_kernel(
    tile_in, cell_in, index_in, obs_in, prec_in, out_ref, tile_ref, cell_ref, index_ref, obs_ref, prec_ref, sems
):
    copies = [
        pltpu.make_async_copy(src, dst, sems.at[i])
        for i, (src, dst) in enumerate(
            (
                (tile_in, tile_ref),
                (cell_in, cell_ref),
                (index_in, index_ref),
                (obs_in, obs_ref),
                (prec_in, prec_ref),
            )
        )
    ]
    for copy in copies:
        copy.start()
    steps, count = cell_ref.shape
    ntiles = out_ref.shape[0]
    tile_ids = lax.broadcasted_iota(jnp.int32, (ntiles, count), 0)
    before = (
        lax.broadcasted_iota(jnp.int32, (count, count), 0)
        < lax.broadcasted_iota(jnp.int32, (count, count), 1)
    ).astype(F32).astype(BF16)
    rank_ids = lax.broadcasted_iota(jnp.int32, (CAP, count), 0)
    pad = jnp.zeros((48 - CAP * WORDS, count), F32)
    empty = [jnp.zeros((n, count), BF16) for n in (64, 16)]
    copies[0].wait()
    mine, at_rank = [], []
    for s in range(steps):
        here = tile_ids == tile_ref[s]
        here_f = jnp.where(here, 1.0, 0.0)
        mine.append(here_f.astype(BF16))
        rank = jnp.sum(here_f * dot(mine[s], before), axis=0, keepdims=True).astype(jnp.int32)
        at_rank.append(rank_ids == rank)
    for copy in copies[1:]:
        copy.wait()
    for pair in range(steps // 2):
        total = None
        for side in range(2):
            s = 2 * pair + side
            code = (index_ref[s : s + 1, :] * 4096 + cell_ref[s : s + 1, :]).astype(F32)
            words = [code] + [obs_ref[t, s : s + 1, :] for t in range(3)] + [prec_ref[s : s + 1, :]]
            rows = jnp.concatenate([jnp.where(at_rank[s], w, 0.0) for w in words] + [pad], axis=0)
            for part in split3(rows):
                block = [part, empty[1], empty[0]] if side == 0 else [empty[0], part, empty[1]]
                term = dot_t(mine[s], jnp.concatenate(block, axis=0))
                total = term if total is None else total + term
        out_ref[:, pair, :] = total


def unpack_kernel(got_ref, out_ref):
    ntiles = got_ref.shape[0]
    for pair in range(2):
        turned = got_ref[:, pair, :].T
        for side in range(2):
            s = 2 * pair + side
            base = 64 * side
            code = turned[base : base + CAP, :].astype(jnp.int32)
            kidx = code // 4096
            cell = code - kidx * 4096
            row = cell // 128
            col = cell - row * 128
            hi = row // 16
            fields = [hi * 128 + col, row - hi * 16, kidx]
            fields = [f.astype(F32) for f in fields]
            fields += [turned[base + CAP * w : base + CAP * (w + 1), :] for w in range(1, WORDS)]
            for f, value in enumerate(fields):
                for r in range(CAP):
                    out_ref[s, f : f + 1, r * ntiles : (r + 1) * ntiles] = value[r : r + 1, :]
            out_ref[s, 7:8, :] = jnp.zeros((1, CAP * ntiles), F32)


def forcing_kernel(s, chunk, snd_ref, traj_ref, table_ref, *refs):
    if s == 0:
        out_ref, pick, pick8, weight = refs
    else:
        traj_in, out_ref, next_ref, pick, pick8, weight, sem = refs
        copy = pltpu.make_async_copy(traj_in.at[s - 1], next_ref, sem)
        copy.start()
    forcing_body(s, chunk, snd_ref, traj_ref, table_ref, out_ref, pick, pick8, weight)
    if s > 0:
        copy.wait()


def forcing_body(s, chunk, snd_ref, step_traj, table_ref, out_ref, pick, pick8, weight):
    tracers, layers = out_ref.shape[:2]
    slots = snd_ref.shape[2]
    nker = table_ref.shape[2]
    cell_ids = lax.broadcasted_iota(jnp.int32, (256, chunk), 0).astype(F32)
    low_ids = lax.broadcasted_iota(jnp.int32, (16, chunk), 0).astype(F32)
    ker_ids = lax.broadcasted_iota(jnp.int32, (nker, chunk), 0).astype(F32)
    for c in range(slots // chunk):
        at = pl.ds(c * chunk, chunk)
        here = jnp.where(cell_ids == snd_ref[s, 0:1, at], 1.0, 0.0)
        pick[:, at] = here.astype(BF16)
        pick8[:, at] = here.astype(F8)
        low = jnp.where(low_ids == snd_ref[s, 1:2, at], 1.0, 0.0)
        ker = jnp.where(ker_ids == snd_ref[s, 2:3, at], 1.0, 0.0).astype(BF16)
        w = dot(table_ref[0], ker) + dot(table_ref[1], ker) + dot(table_ref[2], ker)
        for k in range(layers):
            weight[k, :, at] = w[k : k + 1, :] * low
    for t in range(tracers):
        lhs = jnp.concatenate(
            [
                step_traj[t, :, 0:16, :].reshape(layers * 16, 128),
                step_traj[t, :, 16:32, :].reshape(layers * 16, 128),
            ],
            axis=1,
        )
        force = None
        for c in range(slots // chunk):
            at = pl.ds(c * chunk, chunk)
            sampled = dot(lhs, pick[:, at]).reshape(layers, 16, chunk)
            model = jnp.sum(jnp.sum(sampled * weight[:, :, at], axis=0), axis=0, keepdims=True)
            sc = (model - snd_ref[s, 3 + t : 4 + t, at]) * snd_ref[s, 6:7, at]
            value = (weight[:, :, at] * sc).reshape(layers * 16, chunk)
            hi = value.astype(BF16)
            lo = ((value - hi.astype(F32)) * LOW).astype(F8)
            term = dot_t(hi, pick[:, at]) + dot_t(lo, pick8[:, at]) * (1.0 / LOW)
            force = term if force is None else force + term
        out_ref[t, :, 0:16, :] = force[:, 0:128].reshape(layers, 16, 128)
        out_ref[t, :, 16:32, :] = force[:, 128:256].reshape(layers, 16, 128)


def end_rows():
    row = lax.broadcasted_iota(jnp.int32, (8, 256), 0)
    lane = lax.broadcasted_iota(jnp.int32, (8, 256), 1) % 128
    ends = ((row == 0) & (lane == 127)) | ((row == 1) & (lane == 0))
    return jnp.where(ends, 1.0, 0.0).astype(BF16)


def lane_shifts():
    src = lax.broadcasted_iota(jnp.int32, (256, 256), 0) % 128
    dst = lax.broadcasted_iota(jnp.int32, (256, 256), 1)
    dst = jnp.where(dst < 128, dst - 1, dst - 127)
    return jnp.where(src == dst, 1.0, 0.0).astype(BF16)


def columns(column_ref, layers):
    at = [0, layers - 1, 2 * layers - 1]
    sizes = [layers - 1, layers, layers - 1]
    return [column_ref.at[pl.ds(a, n)] for a, n in zip(at, sizes)]


def setup_kernel(
    mask_ref, mix_in, tr_in, traj_in, coef_out, column_ref, lat_w, lon_w, traj_ref,
    tr_ref, flat_ref, in_sems, out_sems,
):
    layers = tr_ref.shape[1]
    mix_ref, inv_ref, up_ref = columns(column_ref, layers)
    copies = [
        pltpu.make_async_copy(src, dst, in_sems.at[i])
        for i, (src, dst) in enumerate(((mix_in, mix_ref), (tr_in, tr_ref), (traj_in.at[traj_in.shape[0] - 1], traj_ref)))
    ]
    for copy in copies:
        copy.start()
    sent = []

    def send(src, dst):
        sent.append(pltpu.make_async_copy(src, dst, out_sems.at[len(sent)]))
        sent[-1].start()

    copies[0].wait()
    for k in range(layers):
        diag = jnp.ones_like(mix_ref[0])
        if k > 0:
            diag = diag + mix_ref[k - 1]
        if k < layers - 1:
            diag = diag + mix_ref[k]
        if k > 0:
            diag = diag + mix_ref[k - 1] * up
        inv = 1.0 / diag
        inv_ref[k] = inv
        if k < layers - 1:
            up = -mix_ref[k] * inv
            up_ref[k] = up
    copies[1].wait()
    lane = lax.broadcasted_iota(jnp.int32, (32, 128), 1)
    row = lax.broadcasted_iota(jnp.int32, (32, 128), 0)

    def coefs(k, _):
        te, tw, tn, ts = (tr_ref[i, k] for i in range(4))
        flat_ref[0 * layers + k] = jnp.where(lane == 0, 0.0, pltpu.roll(te, 1, axis=1))
        flat_ref[1 * layers + k] = jnp.where(lane == 127, 0.0, pltpu.roll(tw, 127, axis=1))
        flat_ref[2 * layers + k] = jnp.where(row == 0, 0.0, pltpu.roll(tn, 1, axis=0))
        flat_ref[3 * layers + k] = jnp.where(row == 31, 0.0, pltpu.roll(ts, 31, axis=0))
        flat_ref[4 * layers + k] = 1.0 - te - tw - tn - ts
        return 0

    group = layers // 3
    for g in range(3):
        lax.fori_loop(g * group, (g + 1) * group, coefs, 0, unroll=4)
        for i in range(5):
            at = pl.ds(i * layers + g * group, group)
            send(flat_ref.at[at], coef_out.at[at])
    to_north = tr_ref[3, :, 0, :] * mask_ref[0:1, :]
    to_south = tr_ref[2, :, 31, :] * mask_ref[1:2, :]
    odd = mask_ref[2:3, :]
    lat_w[0] = odd * to_north
    lat_w[1] = (1.0 - odd) * to_south
    lat_w[2] = (1.0 - odd) * to_north
    lat_w[3] = odd * to_south
    odd = mask_ref[3:4, 0:1]
    ends = end_rows()[:, 0:128]
    for side in range(2):
        flat = None
        for part in split3(tr_ref[side].reshape(layers * 32, 128)):
            term = dot_t(ends, part)
            flat = term if flat is None else flat + term
        flat = flat[side : side + 1, :]
        lon_w[side] = flat * (odd if side else 1.0 - odd)
        lon_w[2 + side] = flat * (1.0 - odd if side else odd)
    for copy in copies[2:] + sent:
        copy.wait()


def lon_spots(mask_ref, lon_a, lon_b, first, size, cols):
    row = lax.broadcasted_iota(jnp.int32, (4, cols), 0)
    lane = lax.broadcasted_iota(jnp.int32, (4, cols), 1)
    other = (row % 2).astype(F32)
    lon_odd = jnp.broadcast_to(mask_ref[3:4, :], (4, cols))
    spot = (other * lon_odd + (1.0 - other) * (1.0 - lon_odd)) * (cols - 1)
    place = jnp.where(lane.astype(F32) == spot, 1.0, 0.0).astype(BF16)
    at = slice(first, first + size)
    hi, lo = split2(jnp.concatenate([lon_a[:, at], lon_b[:, at]], axis=0))
    both = jnp.concatenate([hi, lo], axis=0)
    return lax.dot_general(both, place, (((0,), (0,)), ((), ())), preferred_element_type=F32)


def lat_rows(mask_ref, lat_a, lat_b, layers):
    odd = mask_ref[2:3, :] > 0.5
    rows = [(lat_a[at, :], lat_b[at, :]) for at in (slice(t * layers, (t + 1) * layers) for t in range(3))]
    return [jnp.where(odd, a, b) for a, b in rows], [jnp.where(odd, b, a) for a, b in rows]


def spread(mask_ref, lon_a, lon_b, lat_a, lat_b, halo):
    tracers, layers, rows, cols = halo.shape
    size = layers * rows
    north, south = lat_rows(mask_ref, lat_a, lat_b, layers)
    for t in range(tracers):
        halo[t] = lon_spots(mask_ref, lon_a, lon_b, t * size, size, cols).reshape(layers, rows, cols)
        halo[t, :, 0, :] += north[t]
        halo[t, :, rows - 1, :] += south[t]


def vertical(base, force_ref, column_ref, v):
    tracers, layers = v.shape[:2]
    mix_ref, inv_ref, up_ref = columns(column_ref, layers)
    d = tuple((force_ref[t, 0] + base(t, 0)) * inv_ref[0] for t in range(tracers))
    for t in range(tracers):
        v[t, 0] = d[t]

    def forward(k, d):
        m, inv = mix_ref[k - 1], inv_ref[k]
        d = tuple((force_ref[t, k] + base(t, k) + m * d[t]) * inv for t in range(tracers))
        for t in range(tracers):
            v[t, k] = d[t]
        return d

    d = lax.fori_loop(1, layers, forward, d, unroll=5)

    def backward(i, x):
        k = layers - 2 - i
        u = up_ref[k]
        x = tuple(v[t, k] - u * x[t] for t in range(tracers))
        for t in range(tracers):
            v[t, k] = x[t]
        return x

    lax.fori_loop(0, layers - 1, backward, d, unroll=5)


def horizontal(v, coef_ref=None, w_out=None, weights=None, edges=None):
    tracers, layers, rows, cols = v.shape
    shifts, end_lanes = lane_shifts(), end_rows()
    group = 12
    size = group * rows
    for t in range(tracers):
        for g in range(0, layers, group):
            x = v[t, g : g + group]
            both = jnp.concatenate(split2(x.reshape(size, cols)), axis=1)
            if edges is not None:
                (_, lon_w), (lon_a, lon_b) = weights, edges[:2]
                ends = dot_t(end_lanes, both)
                to = pl.ds((t * layers + g) * rows, size)
                at = pl.ds(g * rows, size)
                lon_a[:, to] = ends[0:1, :] * lon_w[0, :, at] + ends[1:2, :] * lon_w[1, :, at]
                lon_b[:, to] = ends[0:1, :] * lon_w[2, :, at] + ends[1:2, :] * lon_w[3, :, at]
            if w_out is not None:
                moved = dot(both, shifts)
                c = [coef_ref[i * layers + g : i * layers + g + group].reshape(size, cols) for i in range(5)]
                down = jnp.stack([pltpu.roll(x[i], 1, axis=0) for i in range(group)])
                up = jnp.stack([pltpu.roll(x[i], rows - 1, axis=0) for i in range(group)])
                out = c[4] * x.reshape(size, cols) + c[0] * moved[:, :cols] + c[1] * moved[:, cols:]
                out = out + c[2] * down.reshape(size, cols) + c[3] * up.reshape(size, cols)
                w_out[t, g : g + group] = out.reshape(group, rows, cols)
    if edges is not None:
        (lat_w, _), (lat_a, lat_b) = weights, edges[2:]
        ends = [(v[t, :, 0, :], v[t, :, rows - 1, :]) for t in range(tracers)]
        to_a = [top * lat_w[0] + low * lat_w[1] for top, low in ends]
        to_b = [top * lat_w[2] + low * lat_w[3] for top, low in ends]
        for t in range(tracers):
            at = slice(t * layers, (t + 1) * layers)
            lat_a[at, :] = to_a[t]
            lat_b[at, :] = to_b[t]


def head_kernel(
    s, chunk, got_ref, traj_ref, table_in, traj_in, coef_in,
    out_ref, snd_ref, parts_ref, next_ref, coef_ref, pick, pick8, weight, table_ref, sems,
):
    pairs = ((table_in, table_ref), (traj_in.at[s - 1], next_ref), (coef_in, coef_ref))
    copies = [pltpu.make_async_copy(a, b, sems.at[i]) for i, (a, b) in enumerate(pairs)]
    for copy in copies:
        copy.start()
    unpack_kernel(got_ref, snd_ref)
    copies[0].wait()
    for i, part in enumerate(split3(table_ref[...])):
        parts_ref[i] = part
    forcing_body(s, chunk, snd_ref, traj_ref, parts_ref, out_ref, pick, pick8, weight)
    for copy in copies[1:]:
        copy.wait()


def first_step_kernel(force_ref, column_ref, coef_ref, lat_w, lon_w, w_out, *refs):
    edges, v = refs[:4], refs[4]
    vertical(lambda t, k: 0.0, force_ref, column_ref, v)
    horizontal(v, coef_ref, w_out, (lat_w, lon_w), edges)


def step_kernel(
    start, whole, mask_ref, w_in, lat_b, lat_a, lon_b, lon_a, *refs
):
    flux_in, refs = (None, refs) if start else (refs[0], refs[1:])
    force_ref, column_ref, coef_ref, lat_w, lon_w, w_out = refs[:6]
    refs = refs[6:]
    edges, flux_out, halo, v = refs[:4], refs[4], refs[5], refs[6] if whole else w_out
    spread(mask_ref, lon_a, lon_b, lat_a, lat_b, halo)

    def base(t, k):
        value = w_in[t, k] + halo[t, k]
        if isinstance(k, int):
            flux_out[t] = value if start else flux_in[t] + value
        return value

    vertical(base, force_ref, column_ref, v)
    horizontal(v, coef_ref if whole else None, w_out if whole else None, (lat_w, lon_w), edges)


def interior_kernel(v, coef_ref, w_out):
    horizontal(v, coef_ref, w_out)


def last_kernel(
    mask_ref, w_in, lat_b, lat_a, lon_b, lon_a, flux_in, adj_out, flux_out, done, sems
):
    tracers, layers, rows, cols = w_in.shape
    north, south = lat_rows(mask_ref, lat_a, lat_b, layers)
    group = layers // 3
    size = group * rows
    copies = []
    for t in range(tracers):
        for g in range(3):
            first = t * layers * rows + g * size
            at = (t, pl.ds(g * group, group))
            spots = lon_spots(mask_ref, lon_a, lon_b, first, size, cols)
            done[at] = w_in[at] + spots.reshape(group, rows, cols)
            done[t, g * group : (g + 1) * group, 0, :] += north[t][g * group : (g + 1) * group]
            done[t, g * group : (g + 1) * group, rows - 1, :] += south[t][g * group : (g + 1) * group]
            copies.append(pltpu.make_async_copy(done.at[at], adj_out.at[at], sems.at[3 * t + g]))
            copies[-1].start()
    flux_out[...] = flux_in[...] + done[:, 0]
    for copy in copies:
        copy.wait()


def swaps(axis):
    peers = lax.axis_size(axis)
    near = [(i, i + 1 - 2 * (i % 2)) for i in range(peers)]
    return near, [((i + 1) % peers, (j + 1) % peers) for i, j in near]


def exchange(lon_a, lon_b, lat_a, lat_b):
    lat_near, lat_far = swaps("lat")
    lon_near, lon_far = swaps("lon")
    lon_b = lax.ppermute(lon_b, "lon", lon_far)
    lat_b = lax.ppermute(lat_b, "lat", lat_far)
    lon_a = lax.ppermute(lon_a, "lon", lon_near)
    lat_a = lax.ppermute(lat_a, "lat", lat_near)
    return lat_b, lat_a, lon_b, lon_a


def body(
    transport, mixing, trajectory, kernel_table, track_tile, sound_cell, kernel_index, observed, precision
):
    ntiles = lax.axis_size(("lat", "lon"))
    steps, tracers, layers, rows, cols = trajectory.shape
    count = sound_cell.shape[1]
    field = sds(tracers, layers, rows, cols)
    plane = sds(tracers, rows, cols)
    lat_edge = sds(tracers * layers, cols)
    lon_edge = sds(1, 14336)
    slots = ntiles * CAP
    outgoing = call(
        route_kernel,
        sds(ntiles, 2, 128),
        track_tile.transpose(0, 2, 1),
        sound_cell,
        kernel_index,
        observed.transpose(1, 0, 2),
        precision,
        hbm=range(5),
        scratch=(
            pltpu.VMEM((steps, 1, count), jnp.int32),
            pltpu.VMEM((steps, count), jnp.int32),
            pltpu.VMEM((steps, count), jnp.int32),
            pltpu.VMEM((tracers, steps, count), F32),
            pltpu.VMEM((steps, count), F32),
            pltpu.SemaphoreType.DMA((5,)),
        ),
    )
    got = lax.all_to_all(outgoing, ("lat", "lon"), split_axis=0, concat_axis=0, tiled=True)
    lat, lon = lax.axis_index("lat"), lax.axis_index("lon")
    mask = jnp.stack([lat > 0, lat < lax.axis_size("lat") - 1, lat % 2 > 0, lon % 2 > 0]).astype(F32)
    mask = jnp.broadcast_to(mask[:, None], (4, cols))
    one_step = sds(*trajectory.shape[1:], dtype=BF16)
    coef, column, lat_w, lon_w, now = call(
        setup_kernel,
        (
            sds(5 * layers, rows, cols),
            sds(3 * layers - 2, rows, cols),
            sds(4, layers, cols),
            sds(4, 1, layers * rows),
            one_step,
        ),
        mask,
        mixing,
        transport,
        trajectory,
        hbm=(1, 2, 3),
        hbm_out=(0,),
        scratch=(
            pltpu.VMEM(transport.shape, F32),
            pltpu.VMEM((5 * layers, rows, cols), F32),
            pltpu.SemaphoreType.DMA((3,)),
            pltpu.SemaphoreType.DMA((15,)),
        ),
    )
    table = kernel_table.T
    work = (
        pltpu.VMEM((256, slots), BF16),
        pltpu.VMEM((256, slots), F8),
        pltpu.VMEM((layers, 16, slots), F32),
    )
    force, snd, parts, now, coef = call(
        functools.partial(head_kernel, steps - 1, slots),
        (
            field,
            sds(steps, 8, slots),
            sds(3, *table.shape, dtype=BF16),
            one_step,
            sds(*coef.shape),
        ),
        got,
        now,
        table,
        trajectory,
        coef,
        hbm=(2, 3, 4),
        scratch=work + (pltpu.VMEM(table.shape, F32), pltpu.SemaphoreType.DMA((3,))),
    )
    fixed = (column, coef, lat_w, lon_w)

    def forcing(s, now):
        kernel = functools.partial(forcing_kernel, s, slots)
        if s == 0:
            return call(kernel, field, snd, now, parts, scratch=work), None
        return call(
            kernel,
            (field, one_step),
            snd,
            now,
            parts,
            trajectory,
            hbm=(3,),
            scratch=work + (pltpu.SemaphoreType.DMA,),
        )

    v = pltpu.VMEM(field.shape, F32)
    moved = (field, lon_edge, lon_edge, lat_edge, lat_edge)
    w, *edges = call(first_step_kernel, moved, force, *fixed, scratch=(v,))
    flux = []
    for s in range(steps - 2, -1, -1):
        halos = exchange(*edges)
        force, now = forcing(s, now)
        *done, flux = call(
            functools.partial(step_kernel, s == steps - 2, s > 0),
            moved + (plane,),
            mask,
            w,
            *halos,
            *flux,
            force,
            *fixed,
            scratch=(v, v) if s > 0 else (v,),
        )
        (w, *edges), flux = done, [flux]
    return call(
        last_kernel,
        (field, plane),
        mask,
        call(interior_kernel, field, w, coef),
        *exchange(*edges),
        *flux,
        hbm_out=(0,),
        scratch=(v, pltpu.SemaphoreType.DMA((3 * tracers,))),
    )


def solution(mesh):
    return jax.shard_map(
        body,
        mesh=mesh,
        in_specs=(
            P(None, None, "lat", "lon"),
            P(None, "lat", "lon"),
            P(None, None, None, "lat", "lon"),
            P(),
            P(None, ("lat", "lon"), None),
            P(None, ("lat", "lon")),
            P(None, ("lat", "lon")),
            P(None, None, ("lat", "lon")),
            P(None, ("lat", "lon")),
        ),
        out_specs=(P(None, None, "lat", "lon"), P(None, "lat", "lon")),
        check_vma=False,
    )
```

```python
import functools

import jax
import jax.numpy as jnp
from jax import lax
from jax.experimental import pallas as pl
from jax.experimental.pallas import tpu as pltpu
from jax.sharding import PartitionSpec as P

CAP = 8
WORDS = 5
F32 = jnp.float32
BF16 = jnp.bfloat16
F8 = jnp.float8_e4m3fn
LOW = 256.0


def split3(x):
    hi = x.astype(BF16)
    rest = x - hi.astype(F32)
    mid = rest.astype(BF16)
    return hi, mid, (rest - mid.astype(F32)).astype(BF16)


def split2(x):
    hi = x.astype(BF16)
    return hi, (x - hi.astype(F32)).astype(BF16)


def dot(a, b):
    return jnp.dot(a, b, preferred_element_type=F32)


def dot_t(a, b):
    return lax.dot_general(a, b, (((1,), (1,)), ((), ())), preferred_element_type=F32)


VMEM = pl.BlockSpec(memory_space=pltpu.VMEM)
HBM = pl.BlockSpec(memory_space=pltpu.HBM)


def call(kernel, outs, *args, scratch=(), vmem=20 << 20, hbm=(), hbm_out=()):
    outs = tuple(outs) if isinstance(outs, (tuple, list)) else (outs,)
    args = [pltpu.with_memory_space_constraint(a, pltpu.HBM) if i in hbm else a for i, a in enumerate(args)]
    done = pl.pallas_call(
        kernel,
        out_shape=tuple(pltpu.HBM(o.shape, o.dtype) if i in hbm_out else o for i, o in enumerate(outs)),
        in_specs=[HBM if i in hbm else VMEM for i in range(len(args))],
        out_specs=tuple(HBM if i in hbm_out else VMEM for i in range(len(outs))),
        scratch_shapes=list(scratch),
        compiler_params=pltpu.CompilerParams(vmem_limit_bytes=vmem),
    )(*args)
    return done if len(outs) > 1 else done[0]


def sds(*shape, dtype=F32):
    return jax.ShapeDtypeStruct(shape, dtype)


def route_kernel(
    tile_in, cell_in, index_in, obs_in, prec_in, out_ref, tile_ref, cell_ref, index_ref, obs_ref, prec_ref, sems
):
    copies = [
        pltpu.make_async_copy(src, dst, sems.at[i])
        for i, (src, dst) in enumerate(
            (
                (tile_in, tile_ref),
                (cell_in, cell_ref),
                (index_in, index_ref),
                (obs_in, obs_ref),
                (prec_in, prec_ref),
            )
        )
    ]
    for copy in copies:
        copy.start()
    steps, count = cell_ref.shape
    ntiles = out_ref.shape[0]
    tile_ids = lax.broadcasted_iota(jnp.int32, (ntiles, count), 0)
    before = (
        lax.broadcasted_iota(jnp.int32, (count, count), 0)
        < lax.broadcasted_iota(jnp.int32, (count, count), 1)
    ).astype(F32).astype(BF16)
    rank_ids = lax.broadcasted_iota(jnp.int32, (CAP, count), 0)
    pad = jnp.zeros((48 - CAP * WORDS, count), F32)
    empty = [jnp.zeros((n, count), BF16) for n in (64, 16)]
    copies[0].wait()
    mine, at_rank = [], []
    for s in range(steps):
        here = tile_ids == tile_ref[s]
        here_f = jnp.where(here, 1.0, 0.0)
        mine.append(here_f.astype(BF16))
        rank = jnp.sum(here_f * dot(mine[s], before), axis=0, keepdims=True).astype(jnp.int32)
        at_rank.append(rank_ids == rank)
    for copy in copies[1:]:
        copy.wait()
    for pair in range(steps // 2):
        total = None
        for side in range(2):
            s = 2 * pair + side
            code = (index_ref[s : s + 1, :] * 4096 + cell_ref[s : s + 1, :]).astype(F32)
            words = [code] + [obs_ref[t, s : s + 1, :] for t in range(3)] + [prec_ref[s : s + 1, :]]
            rows = jnp.concatenate([jnp.where(at_rank[s], w, 0.0) for w in words] + [pad], axis=0)
            for part in split3(rows):
                block = [part, empty[1], empty[0]] if side == 0 else [empty[0], part, empty[1]]
                term = dot_t(mine[s], jnp.concatenate(block, axis=0))
                total = term if total is None else total + term
        out_ref[:, pair, :] = total


def unpack_kernel(got_ref, out_ref):
    ntiles = got_ref.shape[0]
    for pair in range(2):
        turned = got_ref[:, pair, :].T
        for side in range(2):
            s = 2 * pair + side
            base = 64 * side
            code = turned[base : base + CAP, :].astype(jnp.int32)
            kidx = code // 4096
            cell = code - kidx * 4096
            row = cell // 128
            col = cell - row * 128
            hi = row // 16
            fields = [hi * 128 + col, row - hi * 16, kidx]
            fields = [f.astype(F32) for f in fields]
            fields += [turned[base + CAP * w : base + CAP * (w + 1), :] for w in range(1, WORDS)]
            for f, value in enumerate(fields):
                for r in range(CAP):
                    out_ref[s, f : f + 1, r * ntiles : (r + 1) * ntiles] = value[r : r + 1, :]
            out_ref[s, 7:8, :] = jnp.zeros((1, CAP * ntiles), F32)


def forcing_kernel(s, chunk, snd_ref, traj_ref, table_ref, *refs):
    if s == 0:
        out_ref, pick, pick8, weight = refs
    else:
        traj_in, out_ref, next_ref, pick, pick8, weight, sem = refs
        copy = pltpu.make_async_copy(traj_in.at[s - 1], next_ref, sem)
        copy.start()
    forcing_body(s, chunk, snd_ref, traj_ref, table_ref, out_ref, pick, pick8, weight)
    if s > 0:
        copy.wait()


def forcing_body(s, chunk, snd_ref, step_traj, table_ref, out_ref, pick, pick8, weight):
    tracers, layers = out_ref.shape[:2]
    slots = snd_ref.shape[2]
    nker = table_ref.shape[2]
    cell_ids = lax.broadcasted_iota(jnp.int32, (256, chunk), 0).astype(F32)
    low_ids = lax.broadcasted_iota(jnp.int32, (16, chunk), 0).astype(F32)
    ker_ids = lax.broadcasted_iota(jnp.int32, (nker, chunk), 0).astype(F32)
    for c in range(slots // chunk):
        at = pl.ds(c * chunk, chunk)
        here = jnp.where(cell_ids == snd_ref[s, 0:1, at], 1.0, 0.0)
        pick[:, at] = here.astype(BF16)
        pick8[:, at] = here.astype(F8)
        low = jnp.where(low_ids == snd_ref[s, 1:2, at], 1.0, 0.0)
        ker = jnp.where(ker_ids == snd_ref[s, 2:3, at], 1.0, 0.0).astype(BF16)
        w = dot(table_ref[0], ker) + dot(table_ref[1], ker) + dot(table_ref[2], ker)
        for k in range(layers):
            weight[k, :, at] = w[k : k + 1, :] * low
    for t in range(tracers):
        lhs = jnp.concatenate(
            [
                step_traj[t, :, 0:16, :].reshape(layers * 16, 128),
                step_traj[t, :, 16:32, :].reshape(layers * 16, 128),
            ],
            axis=1,
        )
        force = None
        for c in range(slots // chunk):
            at = pl.ds(c * chunk, chunk)
            sampled = dot(lhs, pick[:, at]).reshape(layers, 16, chunk)
            model = jnp.sum(jnp.sum(sampled * weight[:, :, at], axis=0), axis=0, keepdims=True)
            sc = (model - snd_ref[s, 3 + t : 4 + t, at]) * snd_ref[s, 6:7, at]
            value = (weight[:, :, at] * sc).reshape(layers * 16, chunk)
            hi = value.astype(BF16)
            lo = ((value - hi.astype(F32)) * LOW).astype(F8)
            term = dot_t(hi, pick[:, at]) + dot_t(lo, pick8[:, at]) * (1.0 / LOW)
            force = term if force is None else force + term
        out_ref[t, :, 0:16, :] = force[:, 0:128].reshape(layers, 16, 128)
        out_ref[t, :, 16:32, :] = force[:, 128:256].reshape(layers, 16, 128)


def end_rows():
    row = lax.broadcasted_iota(jnp.int32, (8, 256), 0)
    lane = lax.broadcasted_iota(jnp.int32, (8, 256), 1) % 128
    ends = ((row == 0) & (lane == 127)) | ((row == 1) & (lane == 0))
    return jnp.where(ends, 1.0, 0.0).astype(BF16)


def lane_shifts():
    src = lax.broadcasted_iota(jnp.int32, (256, 256), 0) % 128
    dst = lax.broadcasted_iota(jnp.int32, (256, 256), 1)
    dst = jnp.where(dst < 128, dst - 1, dst - 127)
    return jnp.where(src == dst, 1.0, 0.0).astype(BF16)


def columns(column_ref, layers):
    at = [0, layers - 1, 2 * layers - 1]
    sizes = [layers - 1, layers, layers - 1]
    return [column_ref.at[pl.ds(a, n)] for a, n in zip(at, sizes)]


def setup_kernel(
    mask_ref, mix_in, tr_in, traj_in, coef_out, column_ref, lat_w, lon_w, traj_ref,
    tr_ref, flat_ref, in_sems, out_sems,
):
    layers = tr_ref.shape[1]
    mix_ref, inv_ref, up_ref = columns(column_ref, layers)
    copies = [
        pltpu.make_async_copy(src, dst, in_sems.at[i])
        for i, (src, dst) in enumerate(((mix_in, mix_ref), (tr_in, tr_ref), (traj_in.at[traj_in.shape[0] - 1], traj_ref)))
    ]
    for copy in copies:
        copy.start()
    sent = []

    def send(src, dst):
        sent.append(pltpu.make_async_copy(src, dst, out_sems.at[len(sent)]))
        sent[-1].start()

    copies[0].wait()
    for k in range(layers):
        diag = jnp.ones_like(mix_ref[0])
        if k > 0:
            diag = diag + mix_ref[k - 1]
        if k < layers - 1:
            diag = diag + mix_ref[k]
        if k > 0:
            diag = diag + mix_ref[k - 1] * up
        inv = 1.0 / diag
        inv_ref[k] = inv
        if k < layers - 1:
            up = -mix_ref[k] * inv
            up_ref[k] = up
    copies[1].wait()
    lane = lax.broadcasted_iota(jnp.int32, (32, 128), 1)
    row = lax.broadcasted_iota(jnp.int32, (32, 128), 0)

    def coefs(k, _):
        te, tw, tn, ts = (tr_ref[i, k] for i in range(4))
        flat_ref[0 * layers + k] = jnp.where(lane == 0, 0.0, pltpu.roll(te, 1, axis=1))
        flat_ref[1 * layers + k] = jnp.where(lane == 127, 0.0, pltpu.roll(tw, 127, axis=1))
        flat_ref[2 * layers + k] = jnp.where(row == 0, 0.0, pltpu.roll(tn, 1, axis=0))
        flat_ref[3 * layers + k] = jnp.where(row == 31, 0.0, pltpu.roll(ts, 31, axis=0))
        flat_ref[4 * layers + k] = 1.0 - te - tw - tn - ts
        return 0

    group = layers // 3
    for g in range(3):
        lax.fori_loop(g * group, (g + 1) * group, coefs, 0, unroll=4)
        for i in range(5):
            at = pl.ds(i * layers + g * group, group)
            send(flat_ref.at[at], coef_out.at[at])
    to_north = tr_ref[3, :, 0, :] * mask_ref[0:1, :]
    to_south = tr_ref[2, :, 31, :] * mask_ref[1:2, :]
    odd = mask_ref[2:3, :]
    lat_w[0] = odd * to_north
    lat_w[1] = (1.0 - odd) * to_south
    lat_w[2] = (1.0 - odd) * to_north
    lat_w[3] = odd * to_south
    odd = mask_ref[3:4, 0:1]
    ends = end_rows()[:, 0:128]
    for side in range(2):
        flat = None
        for part in split3(tr_ref[side].reshape(layers * 32, 128)):
            term = dot_t(ends, part)
            flat = term if flat is None else flat + term
        flat = flat[side : side + 1, :]
        lon_w[side] = flat * (odd if side else 1.0 - odd)
        lon_w[2 + side] = flat * (1.0 - odd if side else odd)
    for copy in copies[2:] + sent:
        copy.wait()


def lon_spots(mask_ref, lon_a, lon_b, first, size, cols):
    row = lax.broadcasted_iota(jnp.int32, (4, cols), 0)
    lane = lax.broadcasted_iota(jnp.int32, (4, cols), 1)
    other = (row % 2).astype(F32)
    lon_odd = jnp.broadcast_to(mask_ref[3:4, :], (4, cols))
    spot = (other * lon_odd + (1.0 - other) * (1.0 - lon_odd)) * (cols - 1)
    place = jnp.where(lane.astype(F32) == spot, 1.0, 0.0).astype(BF16)
    at = slice(first, first + size)
    hi, lo = split2(jnp.concatenate([lon_a[:, at], lon_b[:, at]], axis=0))
    both = jnp.concatenate([hi, lo], axis=0)
    return lax.dot_general(both, place, (((0,), (0,)), ((), ())), preferred_element_type=F32)


def lat_rows(mask_ref, lat_a, lat_b, layers):
    odd = mask_ref[2:3, :] > 0.5
    a, b = lat_a[...].astype(F32), lat_b[...].astype(F32)
    north, south = jnp.where(odd, a, b), jnp.where(odd, b, a)
    return [(x[0:layers], x[layers : 2 * layers], x[2 * layers :]) for x in (north, south)]


def spread(mask_ref, lon_a, lon_b, lat_a, lat_b, halo):
    tracers, layers, rows, cols = halo.shape
    size = layers * rows
    north, south = lat_rows(mask_ref, lat_a, lat_b, layers)
    for t in range(tracers):
        halo[t] = lon_spots(mask_ref, lon_a, lon_b, t * size, size, cols).reshape(layers, rows, cols)
        halo[t, :, 0, :] += north[t]
        halo[t, :, rows - 1, :] += south[t]


def vertical(base, force_ref, column_ref, v):
    tracers, layers = v.shape[:2]
    mix_ref, inv_ref, up_ref = columns(column_ref, layers)
    d = tuple((force_ref[t, 0] + base(t, 0)) * inv_ref[0] for t in range(tracers))
    for t in range(tracers):
        v[t, 0] = d[t]

    def forward(k, d):
        m, inv = mix_ref[k - 1], inv_ref[k]
        d = tuple((force_ref[t, k] + base(t, k) + m * d[t]) * inv for t in range(tracers))
        for t in range(tracers):
            v[t, k] = d[t]
        return d

    d = lax.fori_loop(1, layers, forward, d, unroll=5)

    def backward(i, x):
        k = layers - 2 - i
        u = up_ref[k]
        x = tuple(v[t, k] - u * x[t] for t in range(tracers))
        for t in range(tracers):
            v[t, k] = x[t]
        return x

    lax.fori_loop(0, layers - 1, backward, d, unroll=5)


def horizontal(v, coef_ref=None, w_out=None, weights=None, edges=None):
    tracers, layers, rows, cols = v.shape
    shifts, end_lanes = lane_shifts(), end_rows()
    group = 12
    size = group * rows
    for t in range(tracers):
        for g in range(0, layers, group):
            x = v[t, g : g + group]
            both = jnp.concatenate(split2(x.reshape(size, cols)), axis=1)
            if edges is not None:
                (_, lon_w), (lon_a, lon_b) = weights, edges[:2]
                ends = dot_t(end_lanes, both)
                to = pl.ds((t * layers + g) * rows, size)
                at = pl.ds(g * rows, size)
                lon_a[:, to] = ends[0:1, :] * lon_w[0, :, at] + ends[1:2, :] * lon_w[1, :, at]
                lon_b[:, to] = ends[0:1, :] * lon_w[2, :, at] + ends[1:2, :] * lon_w[3, :, at]
            if w_out is not None:
                moved = dot(both, shifts)
                c = [coef_ref[i * layers + g : i * layers + g + group].reshape(size, cols) for i in range(5)]
                down = jnp.stack([pltpu.roll(x[i], 1, axis=0) for i in range(group)])
                up = jnp.stack([pltpu.roll(x[i], rows - 1, axis=0) for i in range(group)])
                out = c[4] * x.reshape(size, cols) + c[0] * moved[:, :cols] + c[1] * moved[:, cols:]
                out = out + c[2] * down.reshape(size, cols) + c[3] * up.reshape(size, cols)
                w_out[t, g : g + group] = out.reshape(group, rows, cols)
    if edges is not None:
        (lat_w, _), (lat_a, lat_b) = weights, edges[2:]
        ends = [(v[t, :, 0, :], v[t, :, rows - 1, :]) for t in range(tracers)]
        to_a = [top * lat_w[0] + low * lat_w[1] for top, low in ends]
        to_b = [top * lat_w[2] + low * lat_w[3] for top, low in ends]
        lat_a[...] = jnp.concatenate(to_a, axis=0).astype(BF16)
        lat_b[...] = jnp.concatenate(to_b, axis=0).astype(BF16)


def head_kernel(
    s, chunk, got_ref, traj_ref, table_in, traj_in, coef_in,
    out_ref, snd_ref, parts_ref, next_ref, coef_ref, pick, pick8, weight, table_ref, sems,
):
    pairs = ((table_in, table_ref), (traj_in.at[s - 1], next_ref), (coef_in, coef_ref))
    copies = [pltpu.make_async_copy(a, b, sems.at[i]) for i, (a, b) in enumerate(pairs)]
    for copy in copies:
        copy.start()
    unpack_kernel(got_ref, snd_ref)
    copies[0].wait()
    for i, part in enumerate(split3(table_ref[...])):
        parts_ref[i] = part
    forcing_body(s, chunk, snd_ref, traj_ref, parts_ref, out_ref, pick, pick8, weight)
    for copy in copies[1:]:
        copy.wait()


def first_step_kernel(force_ref, column_ref, coef_ref, lat_w, lon_w, w_out, *refs):
    edges, v = refs[:4], refs[4]
    vertical(lambda t, k: 0.0, force_ref, column_ref, v)
    horizontal(v, coef_ref, w_out, (lat_w, lon_w), edges)


def step_kernel(
    start, whole, mask_ref, w_in, lat_b, lat_a, lon_b, lon_a, *refs
):
    flux_in, refs = (None, refs) if start else (refs[0], refs[1:])
    force_ref, column_ref, coef_ref, lat_w, lon_w, w_out = refs[:6]
    refs = refs[6:]
    edges, flux_out, halo, v = refs[:4], refs[4], refs[5], refs[6] if whole else w_out
    spread(mask_ref, lon_a, lon_b, lat_a, lat_b, halo)

    def base(t, k):
        value = w_in[t, k] + halo[t, k]
        if isinstance(k, int):
            flux_out[t] = value if start else flux_in[t] + value
        return value

    vertical(base, force_ref, column_ref, v)
    horizontal(v, coef_ref if whole else None, w_out if whole else None, (lat_w, lon_w), edges)


def interior_kernel(v, coef_ref, w_out):
    horizontal(v, coef_ref, w_out)


def last_kernel(
    mask_ref, w_in, lat_b, lat_a, lon_b, lon_a, flux_in, adj_out, flux_out, done, sems
):
    tracers, layers, rows, cols = w_in.shape
    north, south = lat_rows(mask_ref, lat_a, lat_b, layers)
    group = layers // 3
    size = group * rows
    copies = []
    for t in range(tracers):
        for g in range(3):
            first = t * layers * rows + g * size
            at = (t, pl.ds(g * group, group))
            spots = lon_spots(mask_ref, lon_a, lon_b, first, size, cols)
            done[at] = w_in[at] + spots.reshape(group, rows, cols)
            done[t, g * group : (g + 1) * group, 0, :] += north[t][g * group : (g + 1) * group]
            done[t, g * group : (g + 1) * group, rows - 1, :] += south[t][g * group : (g + 1) * group]
            copies.append(pltpu.make_async_copy(done.at[at], adj_out.at[at], sems.at[3 * t + g]))
            copies[-1].start()
    flux_out[...] = flux_in[...] + done[:, 0]
    for copy in copies:
        copy.wait()


def swaps(axis):
    peers = lax.axis_size(axis)
    near = [(i, i + 1 - 2 * (i % 2)) for i in range(peers)]
    return near, [((i + 1) % peers, (j + 1) % peers) for i, j in near]


def exchange(lon_a, lon_b, lat_a, lat_b):
    lat_near, lat_far = swaps("lat")
    lon_near, lon_far = swaps("lon")
    lon_b = lax.ppermute(lon_b, "lon", lon_far)
    lat_b = lax.ppermute(lat_b, "lat", lat_far)
    lon_a = lax.ppermute(lon_a, "lon", lon_near)
    lat_a = lax.ppermute(lat_a, "lat", lat_near)
    return lat_b, lat_a, lon_b, lon_a


def body(
    transport, mixing, trajectory, kernel_table, track_tile, sound_cell, kernel_index, observed, precision
):
    ntiles = lax.axis_size(("lat", "lon"))
    steps, tracers, layers, rows, cols = trajectory.shape
    count = sound_cell.shape[1]
    field = sds(tracers, layers, rows, cols)
    plane = sds(tracers, rows, cols)
    lat_edge = sds(tracers * layers, cols, dtype=BF16)
    lon_edge = sds(1, 7168)
    slots = ntiles * CAP
    outgoing = call(
        route_kernel,
        sds(ntiles, 2, 128),
        track_tile.transpose(0, 2, 1),
        sound_cell,
        kernel_index,
        observed.transpose(1, 0, 2),
        precision,
        hbm=range(5),
        scratch=(
            pltpu.VMEM((steps, 1, count), jnp.int32),
            pltpu.VMEM((steps, count), jnp.int32),
            pltpu.VMEM((steps, count), jnp.int32),
            pltpu.VMEM((tracers, steps, count), F32),
            pltpu.VMEM((steps, count), F32),
            pltpu.SemaphoreType.DMA((5,)),
        ),
    )
    got = lax.all_to_all(outgoing, ("lat", "lon"), split_axis=0, concat_axis=0, tiled=True)
    lat, lon = lax.axis_index("lat"), lax.axis_index("lon")
    mask = jnp.stack([lat > 0, lat < lax.axis_size("lat") - 1, lat % 2 > 0, lon % 2 > 0]).astype(F32)
    mask = jnp.broadcast_to(mask[:, None], (4, cols))
    one_step = sds(*trajectory.shape[1:], dtype=BF16)
    coef, column, lat_w, lon_w, now = call(
        setup_kernel,
        (
            sds(5 * layers, rows, cols),
            sds(3 * layers - 2, rows, cols),
            sds(4, layers, cols),
            sds(4, 1, layers * rows),
            one_step,
        ),
        mask,
        mixing,
        transport,
        trajectory,
        hbm=(1, 2, 3),
        hbm_out=(0,),
        scratch=(
            pltpu.VMEM(transport.shape, F32),
            pltpu.VMEM((5 * layers, rows, cols), F32),
            pltpu.SemaphoreType.DMA((3,)),
            pltpu.SemaphoreType.DMA((15,)),
        ),
    )
    table = kernel_table.T
    work = (
        pltpu.VMEM((256, slots), BF16),
        pltpu.VMEM((256, slots), F8),
        pltpu.VMEM((layers, 16, slots), F32),
    )
    force, snd, parts, now, coef = call(
        functools.partial(head_kernel, steps - 1, slots),
        (
            field,
            sds(steps, 8, slots),
            sds(3, *table.shape, dtype=BF16),
            one_step,
            sds(*coef.shape),
        ),
        got,
        now,
        table,
        trajectory,
        coef,
        hbm=(2, 3, 4),
        scratch=work + (pltpu.VMEM(table.shape, F32), pltpu.SemaphoreType.DMA((3,))),
    )
    fixed = (column, coef, lat_w, lon_w)

    def forcing(s, now):
        kernel = functools.partial(forcing_kernel, s, slots)
        if s == 0:
            return call(kernel, field, snd, now, parts, scratch=work), None
        return call(
            kernel,
            (field, one_step),
            snd,
            now,
            parts,
            trajectory,
            hbm=(3,),
            scratch=work + (pltpu.SemaphoreType.DMA,),
        )

    v = pltpu.VMEM(field.shape, F32)
    moved = (field, lon_edge, lon_edge, lat_edge, lat_edge)
    w, *edges = call(first_step_kernel, moved, force, *fixed, scratch=(v,))
    flux = []
    for s in range(steps - 2, -1, -1):
        halos = exchange(*edges)
        force, now = forcing(s, now)
        *done, flux = call(
            functools.partial(step_kernel, s == steps - 2, s > 0),
            moved + (plane,),
            mask,
            w,
            *halos,
            *flux,
            force,
            *fixed,
            scratch=(v, v) if s > 0 else (v,),
        )
        (w, *edges), flux = done, [flux]
    return call(
        last_kernel,
        (field, plane),
        mask,
        call(interior_kernel, field, w, coef),
        *exchange(*edges),
        *flux,
        hbm_out=(0,),
        scratch=(v, pltpu.SemaphoreType.DMA((3 * tracers,))),
    )


def solution(mesh):
    return jax.shard_map(
        body,
        mesh=mesh,
        in_specs=(
            P(None, None, "lat", "lon"),
            P(None, "lat", "lon"),
            P(None, None, None, "lat", "lon"),
            P(),
            P(None, ("lat", "lon"), None),
            P(None, ("lat", "lon")),
            P(None, ("lat", "lon")),
            P(None, None, ("lat", "lon")),
            P(None, ("lat", "lon")),
        ),
        out_specs=(P(None, None, "lat", "lon"), P(None, "lat", "lon")),
        check_vma=False,
    )
```

```python
import functools

import jax
import jax.numpy as jnp
from jax import lax
from jax.experimental import pallas as pl
from jax.experimental.pallas import tpu as pltpu
from jax.sharding import PartitionSpec as P

CAP = 8
WORDS = 5
F32 = jnp.float32
BF16 = jnp.bfloat16
F8 = jnp.float8_e4m3fn
LOW = 256.0


def split3(x):
    hi = x.astype(BF16)
    rest = x - hi.astype(F32)
    mid = rest.astype(BF16)
    return hi, mid, (rest - mid.astype(F32)).astype(BF16)


def split2(x):
    hi = x.astype(BF16)
    return hi, (x - hi.astype(F32)).astype(BF16)


def dot(a, b):
    return jnp.dot(a, b, preferred_element_type=F32)


def dot_t(a, b):
    return lax.dot_general(a, b, (((1,), (1,)), ((), ())), preferred_element_type=F32)


VMEM = pl.BlockSpec(memory_space=pltpu.VMEM)
HBM = pl.BlockSpec(memory_space=pltpu.HBM)


def call(kernel, outs, *args, scratch=(), vmem=20 << 20, hbm=(), hbm_out=()):
    outs = tuple(outs) if isinstance(outs, (tuple, list)) else (outs,)
    args = [pltpu.with_memory_space_constraint(a, pltpu.HBM) if i in hbm else a for i, a in enumerate(args)]
    done = pl.pallas_call(
        kernel,
        out_shape=tuple(pltpu.HBM(o.shape, o.dtype) if i in hbm_out else o for i, o in enumerate(outs)),
        in_specs=[HBM if i in hbm else VMEM for i in range(len(args))],
        out_specs=tuple(HBM if i in hbm_out else VMEM for i in range(len(outs))),
        scratch_shapes=list(scratch),
        compiler_params=pltpu.CompilerParams(vmem_limit_bytes=vmem),
    )(*args)
    return done if len(outs) > 1 else done[0]


def sds(*shape, dtype=F32):
    return jax.ShapeDtypeStruct(shape, dtype)


def route_kernel(
    tile_in, cell_in, index_in, obs_in, prec_in, out_ref, tile_ref, cell_ref, index_ref, obs_ref, prec_ref, sems
):
    copies = [
        pltpu.make_async_copy(src, dst, sems.at[i])
        for i, (src, dst) in enumerate(
            (
                (tile_in, tile_ref),
                (cell_in, cell_ref),
                (index_in, index_ref),
                (obs_in, obs_ref),
                (prec_in, prec_ref),
            )
        )
    ]
    for copy in copies:
        copy.start()
    steps, count = cell_ref.shape
    ntiles = out_ref.shape[0]
    tile_ids = lax.broadcasted_iota(jnp.int32, (ntiles, count), 0)
    before = (
        lax.broadcasted_iota(jnp.int32, (count, count), 0)
        < lax.broadcasted_iota(jnp.int32, (count, count), 1)
    ).astype(F32).astype(BF16)
    rank_ids = lax.broadcasted_iota(jnp.int32, (CAP, count), 0)
    pad = jnp.zeros((48 - CAP * WORDS, count), F32)
    empty = [jnp.zeros((n, count), BF16) for n in (64, 16)]
    copies[0].wait()
    mine, at_rank = [], []
    for s in range(steps):
        here = tile_ids == tile_ref[s]
        here_f = jnp.where(here, 1.0, 0.0)
        mine.append(here_f.astype(BF16))
        rank = jnp.sum(here_f * dot(mine[s], before), axis=0, keepdims=True).astype(jnp.int32)
        at_rank.append(rank_ids == rank)
    for copy in copies[1:]:
        copy.wait()
    for pair in range(steps // 2):
        total = None
        for side in range(2):
            s = 2 * pair + side
            code = (index_ref[s : s + 1, :] * 4096 + cell_ref[s : s + 1, :]).astype(F32)
            words = [code] + [obs_ref[t, s : s + 1, :] for t in range(3)] + [prec_ref[s : s + 1, :]]
            rows = jnp.concatenate([jnp.where(at_rank[s], w, 0.0) for w in words] + [pad], axis=0)
            for part in split3(rows):
                block = [part, empty[1], empty[0]] if side == 0 else [empty[0], part, empty[1]]
                term = dot_t(mine[s], jnp.concatenate(block, axis=0))
                total = term if total is None else total + term
        out_ref[:, pair, :] = total


def unpack_kernel(got_ref, out_ref):
    ntiles = got_ref.shape[0]
    for pair in range(2):
        turned = got_ref[:, pair, :].T
        for side in range(2):
            s = 2 * pair + side
            base = 64 * side
            code = turned[base : base + CAP, :].astype(jnp.int32)
            kidx = code // 4096
            cell = code - kidx * 4096
            row = cell // 128
            col = cell - row * 128
            hi = row // 16
            fields = [hi * 128 + col, row - hi * 16, kidx]
            fields = [f.astype(F32) for f in fields]
            fields += [turned[base + CAP * w : base + CAP * (w + 1), :] for w in range(1, WORDS)]
            for f, value in enumerate(fields):
                for r in range(CAP):
                    out_ref[s, f : f + 1, r * ntiles : (r + 1) * ntiles] = value[r : r + 1, :]
            out_ref[s, 7:8, :] = jnp.zeros((1, CAP * ntiles), F32)


def forcing_kernel(s, chunk, snd_ref, traj_ref, table_ref, *refs):
    if s == 0:
        out_ref, pick, pick8, weight = refs
    else:
        traj_in, out_ref, next_ref, pick, pick8, weight, sem = refs
        copy = pltpu.make_async_copy(traj_in.at[s - 1], next_ref, sem)
        copy.start()
    forcing_body(s, chunk, snd_ref, traj_ref, table_ref, out_ref, pick, pick8, weight)
    if s > 0:
        copy.wait()


def forcing_body(s, chunk, snd_ref, step_traj, table_ref, out_ref, pick, pick8, weight):
    tracers, layers = out_ref.shape[:2]
    slots = snd_ref.shape[2]
    nker = table_ref.shape[2]
    cell_ids = lax.broadcasted_iota(jnp.int32, (256, chunk), 0).astype(F32)
    low_ids = lax.broadcasted_iota(jnp.int32, (16, chunk), 0).astype(F32)
    ker_ids = lax.broadcasted_iota(jnp.int32, (nker, chunk), 0).astype(F32)
    for c in range(slots // chunk):
        at = pl.ds(c * chunk, chunk)
        here = jnp.where(cell_ids == snd_ref[s, 0:1, at], 1.0, 0.0)
        pick[:, at] = here.astype(BF16)
        pick8[:, at] = here.astype(F8)
        low = jnp.where(low_ids == snd_ref[s, 1:2, at], 1.0, 0.0)
        ker = jnp.where(ker_ids == snd_ref[s, 2:3, at], 1.0, 0.0).astype(BF16)
        w = dot(table_ref[0], ker) + dot(table_ref[1], ker) + dot(table_ref[2], ker)
        for k in range(layers):
            weight[k, :, at] = w[k : k + 1, :] * low
    for t in range(tracers):
        lhs = jnp.concatenate(
            [
                step_traj[t, :, 0:16, :].reshape(layers * 16, 128),
                step_traj[t, :, 16:32, :].reshape(layers * 16, 128),
            ],
            axis=1,
        )
        force = None
        for c in range(slots // chunk):
            at = pl.ds(c * chunk, chunk)
            sampled = dot(lhs, pick[:, at]).reshape(layers, 16, chunk)
            model = jnp.sum(jnp.sum(sampled * weight[:, :, at], axis=0), axis=0, keepdims=True)
            sc = (model - snd_ref[s, 3 + t : 4 + t, at]) * snd_ref[s, 6:7, at]
            value = (weight[:, :, at] * sc).reshape(layers * 16, chunk)
            hi = value.astype(BF16)
            lo = ((value - hi.astype(F32)) * LOW).astype(F8)
            term = dot_t(hi, pick[:, at]) + dot_t(lo, pick8[:, at]) * (1.0 / LOW)
            force = term if force is None else force + term
        out_ref[t, :, 0:16, :] = force[:, 0:128].reshape(layers, 16, 128)
        out_ref[t, :, 16:32, :] = force[:, 128:256].reshape(layers, 16, 128)


def end_rows():
    row = lax.broadcasted_iota(jnp.int32, (8, 256), 0)
    lane = lax.broadcasted_iota(jnp.int32, (8, 256), 1) % 128
    ends = ((row == 0) & (lane == 127)) | ((row == 1) & (lane == 0))
    return jnp.where(ends, 1.0, 0.0).astype(BF16)


def lane_shifts():
    src = lax.broadcasted_iota(jnp.int32, (256, 256), 0) % 128
    dst = lax.broadcasted_iota(jnp.int32, (256, 256), 1)
    dst = jnp.where(dst < 128, dst - 1, dst - 127)
    return jnp.where(src == dst, 1.0, 0.0).astype(BF16)


def columns(column_ref, layers):
    at = [0, layers - 1, 2 * layers - 1]
    sizes = [layers - 1, layers, layers - 1]
    return [column_ref.at[pl.ds(a, n)] for a, n in zip(at, sizes)]


def setup_kernel(
    mask_ref, mix_in, tr_in, traj_in, coef_out, column_ref, lat_w, lon_w, traj_ref,
    tr_ref, flat_ref, in_sems, out_sems,
):
    layers = tr_ref.shape[1]
    mix_ref, inv_ref, up_ref = columns(column_ref, layers)
    copies = [
        pltpu.make_async_copy(src, dst, in_sems.at[i])
        for i, (src, dst) in enumerate(((mix_in, mix_ref), (tr_in, tr_ref), (traj_in.at[traj_in.shape[0] - 1], traj_ref)))
    ]
    for copy in copies:
        copy.start()
    sent = []

    def send(src, dst):
        sent.append(pltpu.make_async_copy(src, dst, out_sems.at[len(sent)]))
        sent[-1].start()

    copies[0].wait()
    for k in range(layers):
        diag = jnp.ones_like(mix_ref[0])
        if k > 0:
            diag = diag + mix_ref[k - 1]
        if k < layers - 1:
            diag = diag + mix_ref[k]
        if k > 0:
            diag = diag + mix_ref[k - 1] * up
        inv = 1.0 / diag
        inv_ref[k] = inv
        if k < layers - 1:
            up = -mix_ref[k] * inv
            up_ref[k] = up
    copies[1].wait()
    lane = lax.broadcasted_iota(jnp.int32, (32, 128), 1)
    row = lax.broadcasted_iota(jnp.int32, (32, 128), 0)

    def coefs(k, _):
        te, tw, tn, ts = (tr_ref[i, k] for i in range(4))
        flat_ref[0 * layers + k] = jnp.where(lane == 0, 0.0, pltpu.roll(te, 1, axis=1))
        flat_ref[1 * layers + k] = jnp.where(lane == 127, 0.0, pltpu.roll(tw, 127, axis=1))
        flat_ref[2 * layers + k] = jnp.where(row == 0, 0.0, pltpu.roll(tn, 1, axis=0))
        flat_ref[3 * layers + k] = jnp.where(row == 31, 0.0, pltpu.roll(ts, 31, axis=0))
        flat_ref[4 * layers + k] = 1.0 - te - tw - tn - ts
        return 0

    group = layers // 3
    for g in range(3):
        lax.fori_loop(g * group, (g + 1) * group, coefs, 0, unroll=4)
        for i in range(5):
            at = pl.ds(i * layers + g * group, group)
            send(flat_ref.at[at], coef_out.at[at])
    to_north = tr_ref[3, :, 0, :] * mask_ref[0:1, :]
    to_south = tr_ref[2, :, 31, :] * mask_ref[1:2, :]
    odd = mask_ref[2:3, :]
    lat_w[0] = odd * to_north
    lat_w[1] = (1.0 - odd) * to_south
    lat_w[2] = (1.0 - odd) * to_north
    lat_w[3] = odd * to_south
    odd = mask_ref[3:4, 0:1]
    ends = end_rows()[:, 0:128]
    for side in range(2):
        flat = None
        for part in split3(tr_ref[side].reshape(layers * 32, 128)):
            term = dot_t(ends, part)
            flat = term if flat is None else flat + term
        flat = flat[side : side + 1, :]
        lon_w[side] = flat * (odd if side else 1.0 - odd)
        lon_w[2 + side] = flat * (1.0 - odd if side else odd)
    for copy in copies[2:] + sent:
        copy.wait()


def lon_spots(mask_ref, lon_a, lon_b, first, size, cols):
    row = lax.broadcasted_iota(jnp.int32, (4, cols), 0)
    lane = lax.broadcasted_iota(jnp.int32, (4, cols), 1)
    other = (row % 2).astype(F32)
    lon_odd = jnp.broadcast_to(mask_ref[3:4, :], (4, cols))
    spot = (other * lon_odd + (1.0 - other) * (1.0 - lon_odd)) * (cols - 1)
    place = jnp.where(lane.astype(F32) == spot, 1.0, 0.0).astype(BF16)
    at = slice(first, first + size)
    hi, lo = split2(jnp.concatenate([lon_a[:, at], lon_b[:, at]], axis=0))
    both = jnp.concatenate([hi, lo], axis=0)
    return lax.dot_general(both, place, (((0,), (0,)), ((), ())), preferred_element_type=F32)


def lat_rows(mask_ref, lat_a, lat_b, layers):
    odd = mask_ref[2:3, :] > 0.5
    a, b = lat_a[...].astype(F32), lat_b[...].astype(F32)
    north, south = jnp.where(odd, a, b), jnp.where(odd, b, a)
    return [(x[0:layers], x[layers : 2 * layers], x[2 * layers :]) for x in (north, south)]


def spread(mask_ref, lon_a, lon_b, lat_a, lat_b, halo):
    tracers, layers, rows, cols = halo.shape
    size = layers * rows
    north, south = lat_rows(mask_ref, lat_a, lat_b, layers)
    for t in range(tracers):
        halo[t] = lon_spots(mask_ref, lon_a, lon_b, t * size, size, cols).reshape(layers, rows, cols)
        halo[t, :, 0, :] += north[t]
        halo[t, :, rows - 1, :] += south[t]


def vertical(base, force_ref, column_ref, v):
    tracers, layers = v.shape[:2]
    mix_ref, inv_ref, up_ref = columns(column_ref, layers)
    d = tuple((force_ref[t, 0] + base(t, 0)) * inv_ref[0] for t in range(tracers))
    for t in range(tracers):
        v[t, 0] = d[t]

    def forward(k, d):
        m, inv = mix_ref[k - 1], inv_ref[k]
        d = tuple((force_ref[t, k] + base(t, k) + m * d[t]) * inv for t in range(tracers))
        for t in range(tracers):
            v[t, k] = d[t]
        return d

    d = lax.fori_loop(1, layers, forward, d, unroll=5)

    def backward(i, x):
        k = layers - 2 - i
        u = up_ref[k]
        x = tuple(v[t, k] - u * x[t] for t in range(tracers))
        for t in range(tracers):
            v[t, k] = x[t]
        return x

    lax.fori_loop(0, layers - 1, backward, d, unroll=5)


def horizontal(v, coef_ref=None, w_out=None, weights=None, edges=None):
    tracers, layers, rows, cols = v.shape
    shifts, end_lanes = lane_shifts(), end_rows()
    group = 12
    size = group * rows
    for t in range(tracers):
        for g in range(0, layers, group):
            x = v[t, g : g + group]
            both = jnp.concatenate(split2(x.reshape(size, cols)), axis=1)
            if edges is not None:
                (_, lon_w), (lon_a, lon_b) = weights, edges[:2]
                ends = dot_t(end_lanes, both)
                to = pl.ds((t * layers + g) * rows, size)
                at = pl.ds(g * rows, size)
                lon_a[:, to] = ends[0:1, :] * lon_w[0, :, at] + ends[1:2, :] * lon_w[1, :, at]
                lon_b[:, to] = ends[0:1, :] * lon_w[2, :, at] + ends[1:2, :] * lon_w[3, :, at]
            if w_out is not None:
                moved = dot(both, shifts)
                c = [coef_ref[i * layers + g : i * layers + g + group].reshape(size, cols) for i in range(5)]
                down = jnp.stack([pltpu.roll(x[i], 1, axis=0) for i in range(group)])
                up = jnp.stack([pltpu.roll(x[i], rows - 1, axis=0) for i in range(group)])
                out = c[4] * x.reshape(size, cols) + c[0] * moved[:, :cols] + c[1] * moved[:, cols:]
                out = out + c[2] * down.reshape(size, cols) + c[3] * up.reshape(size, cols)
                w_out[t, g : g + group] = out.reshape(group, rows, cols)
    if edges is not None:
        (lat_w, _), (lat_a, lat_b) = weights, edges[2:]
        ends = [(v[t, :, 0, :], v[t, :, rows - 1, :]) for t in range(tracers)]
        to_a = [top * lat_w[0] + low * lat_w[1] for top, low in ends]
        to_b = [top * lat_w[2] + low * lat_w[3] for top, low in ends]
        lat_a[...] = jnp.concatenate(to_a, axis=0).astype(BF16)
        lat_b[...] = jnp.concatenate(to_b, axis=0).astype(BF16)


def head_kernel(
    s, chunk, got_ref, traj_ref, table_in, traj_in, coef_in,
    out_ref, snd_ref, parts_ref, next_ref, coef_ref, pick, pick8, weight, table_ref, sems,
):
    pairs = ((table_in, table_ref), (traj_in.at[s - 1], next_ref), (coef_in, coef_ref))
    copies = [pltpu.make_async_copy(a, b, sems.at[i]) for i, (a, b) in enumerate(pairs)]
    for copy in copies:
        copy.start()
    unpack_kernel(got_ref, snd_ref)
    copies[0].wait()
    for i, part in enumerate(split3(table_ref[...])):
        parts_ref[i] = part
    forcing_body(s, chunk, snd_ref, traj_ref, parts_ref, out_ref, pick, pick8, weight)
    for copy in copies[1:]:
        copy.wait()


def first_step_kernel(force_ref, column_ref, lat_w, lon_w, v, *edges):
    vertical(lambda t, k: 0.0, force_ref, column_ref, v)
    horizontal(v, None, None, (lat_w, lon_w), edges)


def step_kernel(
    start, whole, mask_ref, w_in, lat_b, lat_a, lon_b, lon_a, *refs
):
    flux_in, refs = (None, refs) if start else (refs[0], refs[1:])
    force_ref, column_ref, coef_ref, lat_w, lon_w, w_out = refs[:6]
    refs = refs[6:]
    edges, flux_out, halo, v = refs[:4], refs[4], refs[5], refs[6] if whole else w_out
    spread(mask_ref, lon_a, lon_b, lat_a, lat_b, halo)

    def base(t, k):
        value = w_in[t, k] + halo[t, k]
        if isinstance(k, int):
            flux_out[t] = value if start else flux_in[t] + value
        return value

    vertical(base, force_ref, column_ref, v)
    horizontal(v, coef_ref if whole else None, w_out if whole else None, (lat_w, lon_w), edges)


def interior_kernel(v, coef_ref, w_out):
    horizontal(v, coef_ref, w_out)


def last_kernel(
    mask_ref, w_in, lat_b, lat_a, lon_b, lon_a, flux_in, adj_out, flux_out, done, sems
):
    tracers, layers, rows, cols = w_in.shape
    north, south = lat_rows(mask_ref, lat_a, lat_b, layers)
    group = layers // 3
    size = group * rows
    copies = []
    for t in range(tracers):
        for g in range(3):
            first = t * layers * rows + g * size
            at = (t, pl.ds(g * group, group))
            spots = lon_spots(mask_ref, lon_a, lon_b, first, size, cols)
            done[at] = w_in[at] + spots.reshape(group, rows, cols)
            done[t, g * group : (g + 1) * group, 0, :] += north[t][g * group : (g + 1) * group]
            done[t, g * group : (g + 1) * group, rows - 1, :] += south[t][g * group : (g + 1) * group]
            copies.append(pltpu.make_async_copy(done.at[at], adj_out.at[at], sems.at[3 * t + g]))
            copies[-1].start()
    flux_out[...] = flux_in[...] + done[:, 0]
    for copy in copies:
        copy.wait()


def swaps(axis):
    peers = lax.axis_size(axis)
    near = [(i, i + 1 - 2 * (i % 2)) for i in range(peers)]
    return near, [((i + 1) % peers, (j + 1) % peers) for i, j in near]


def exchange(lon_a, lon_b, lat_a, lat_b):
    lat_near, lat_far = swaps("lat")
    lon_near, lon_far = swaps("lon")
    lon_b = lax.ppermute(lon_b, "lon", lon_far)
    lat_b = lax.ppermute(lat_b, "lat", lat_far)
    lon_a = lax.ppermute(lon_a, "lon", lon_near)
    lat_a = lax.ppermute(lat_a, "lat", lat_near)
    return lat_b, lat_a, lon_b, lon_a


def body(
    transport, mixing, trajectory, kernel_table, track_tile, sound_cell, kernel_index, observed, precision
):
    ntiles = lax.axis_size(("lat", "lon"))
    steps, tracers, layers, rows, cols = trajectory.shape
    count = sound_cell.shape[1]
    field = sds(tracers, layers, rows, cols)
    plane = sds(tracers, rows, cols)
    lat_edge = sds(tracers * layers, cols, dtype=BF16)
    lon_edge = sds(1, 7168)
    slots = ntiles * CAP
    outgoing = call(
        route_kernel,
        sds(ntiles, 2, 128),
        track_tile.transpose(0, 2, 1),
        sound_cell,
        kernel_index,
        observed.transpose(1, 0, 2),
        precision,
        hbm=range(5),
        scratch=(
            pltpu.VMEM((steps, 1, count), jnp.int32),
            pltpu.VMEM((steps, count), jnp.int32),
            pltpu.VMEM((steps, count), jnp.int32),
            pltpu.VMEM((tracers, steps, count), F32),
            pltpu.VMEM((steps, count), F32),
            pltpu.SemaphoreType.DMA((5,)),
        ),
    )
    got = lax.all_to_all(outgoing, ("lat", "lon"), split_axis=0, concat_axis=0, tiled=True)
    lat, lon = lax.axis_index("lat"), lax.axis_index("lon")
    mask = jnp.stack([lat > 0, lat < lax.axis_size("lat") - 1, lat % 2 > 0, lon % 2 > 0]).astype(F32)
    mask = jnp.broadcast_to(mask[:, None], (4, cols))
    one_step = sds(*trajectory.shape[1:], dtype=BF16)
    coef, column, lat_w, lon_w, now = call(
        setup_kernel,
        (
            sds(5 * layers, rows, cols),
            sds(3 * layers - 2, rows, cols),
            sds(4, layers, cols),
            sds(4, 1, layers * rows),
            one_step,
        ),
        mask,
        mixing,
        transport,
        trajectory,
        hbm=(1, 2, 3),
        hbm_out=(0,),
        scratch=(
            pltpu.VMEM(transport.shape, F32),
            pltpu.VMEM((5 * layers, rows, cols), F32),
            pltpu.SemaphoreType.DMA((3,)),
            pltpu.SemaphoreType.DMA((15,)),
        ),
    )
    table = kernel_table.T
    work = (
        pltpu.VMEM((256, slots), BF16),
        pltpu.VMEM((256, slots), F8),
        pltpu.VMEM((layers, 16, slots), F32),
    )
    force, snd, parts, now, coef = call(
        functools.partial(head_kernel, steps - 1, slots),
        (
            field,
            sds(steps, 8, slots),
            sds(3, *table.shape, dtype=BF16),
            one_step,
            sds(*coef.shape),
        ),
        got,
        now,
        table,
        trajectory,
        coef,
        hbm=(2, 3, 4),
        scratch=work + (pltpu.VMEM(table.shape, F32), pltpu.SemaphoreType.DMA((3,))),
    )
    fixed = (column, coef, lat_w, lon_w)

    def forcing(s, now):
        kernel = functools.partial(forcing_kernel, s, slots)
        if s == 0:
            return call(kernel, field, snd, now, parts, scratch=work), None
        return call(
            kernel,
            (field, one_step),
            snd,
            now,
            parts,
            trajectory,
            hbm=(3,),
            scratch=work + (pltpu.SemaphoreType.DMA,),
        )

    v = pltpu.VMEM(field.shape, F32)
    moved = (field, lon_edge, lon_edge, lat_edge, lat_edge)
    w, *edges = call(first_step_kernel, moved, force, column, lat_w, lon_w)
    flux = []
    for s in range(steps - 2, -1, -1):
        halos = exchange(*edges)
        force, now = forcing(s, now)
        if s == steps - 2:
            w = call(interior_kernel, field, w, coef)
        *done, flux = call(
            functools.partial(step_kernel, s == steps - 2, s > 0),
            moved + (plane,),
            mask,
            w,
            *halos,
            *flux,
            force,
            *fixed,
            scratch=(v, v) if s > 0 else (v,),
        )
        (w, *edges), flux = done, [flux]
    return call(
        last_kernel,
        (field, plane),
        mask,
        call(interior_kernel, field, w, coef),
        *exchange(*edges),
        *flux,
        hbm_out=(0,),
        scratch=(v, pltpu.SemaphoreType.DMA((3 * tracers,))),
    )


def solution(mesh):
    return jax.shard_map(
        body,
        mesh=mesh,
        in_specs=(
            P(None, None, "lat", "lon"),
            P(None, "lat", "lon"),
            P(None, None, None, "lat", "lon"),
            P(),
            P(None, ("lat", "lon"), None),
            P(None, ("lat", "lon")),
            P(None, ("lat", "lon")),
            P(None, None, ("lat", "lon")),
            P(None, ("lat", "lon")),
        ),
        out_specs=(P(None, None, "lat", "lon"), P(None, "lat", "lon")),
        check_vma=False,
    )
```

```python
import functools

import jax
import jax.numpy as jnp
from jax import lax
from jax.experimental import pallas as pl
from jax.experimental.pallas import tpu as pltpu
from jax.sharding import PartitionSpec as P

CAP = 8
WORDS = 5
F32 = jnp.float32
BF16 = jnp.bfloat16
F8 = jnp.float8_e4m3fn
LOW = 256.0


def split3(x):
    hi = x.astype(BF16)
    rest = x - hi.astype(F32)
    mid = rest.astype(BF16)
    return hi, mid, (rest - mid.astype(F32)).astype(BF16)


def split2(x):
    hi = x.astype(BF16)
    return hi, (x - hi.astype(F32)).astype(BF16)


def dot(a, b):
    return jnp.dot(a, b, preferred_element_type=F32)


def dot_t(a, b):
    return lax.dot_general(a, b, (((1,), (1,)), ((), ())), preferred_element_type=F32)


VMEM = pl.BlockSpec(memory_space=pltpu.VMEM)
HBM = pl.BlockSpec(memory_space=pltpu.HBM)


def call(kernel, outs, *args, scratch=(), vmem=20 << 20, hbm=(), hbm_out=()):
    outs = tuple(outs) if isinstance(outs, (tuple, list)) else (outs,)
    args = [pltpu.with_memory_space_constraint(a, pltpu.HBM) if i in hbm else a for i, a in enumerate(args)]
    done = pl.pallas_call(
        kernel,
        out_shape=tuple(pltpu.HBM(o.shape, o.dtype) if i in hbm_out else o for i, o in enumerate(outs)),
        in_specs=[HBM if i in hbm else VMEM for i in range(len(args))],
        out_specs=tuple(HBM if i in hbm_out else VMEM for i in range(len(outs))),
        scratch_shapes=list(scratch),
        compiler_params=pltpu.CompilerParams(vmem_limit_bytes=vmem),
    )(*args)
    return done if len(outs) > 1 else done[0]


def sds(*shape, dtype=F32):
    return jax.ShapeDtypeStruct(shape, dtype)


def route_kernel(
    tile_in, cell_in, index_in, obs_in, prec_in, out_ref, tile_ref, cell_ref, index_ref, obs_ref, prec_ref, sems
):
    copies = [
        pltpu.make_async_copy(src, dst, sems.at[i])
        for i, (src, dst) in enumerate(
            (
                (tile_in, tile_ref),
                (cell_in, cell_ref),
                (index_in, index_ref),
                (obs_in, obs_ref),
                (prec_in, prec_ref),
            )
        )
    ]
    for copy in copies:
        copy.start()
    steps, count = cell_ref.shape
    ntiles = out_ref.shape[0]
    tile_ids = lax.broadcasted_iota(jnp.int32, (ntiles, count), 0)
    before = (
        lax.broadcasted_iota(jnp.int32, (count, count), 0)
        < lax.broadcasted_iota(jnp.int32, (count, count), 1)
    ).astype(F32).astype(BF16)
    rank_ids = lax.broadcasted_iota(jnp.int32, (CAP, count), 0)
    pad = jnp.zeros((48 - CAP * WORDS, count), F32)
    empty = [jnp.zeros((n, count), BF16) for n in (64, 16)]
    copies[0].wait()
    mine, at_rank = [], []
    for s in range(steps):
        here = tile_ids == tile_ref[s]
        here_f = jnp.where(here, 1.0, 0.0)
        mine.append(here_f.astype(BF16))
        rank = jnp.sum(here_f * dot(mine[s], before), axis=0, keepdims=True).astype(jnp.int32)
        at_rank.append(rank_ids == rank)
    for copy in copies[1:]:
        copy.wait()
    for pair in range(steps // 2):
        total = None
        for side in range(2):
            s = 2 * pair + side
            code = (index_ref[s : s + 1, :] * 4096 + cell_ref[s : s + 1, :]).astype(F32)
            words = [code] + [obs_ref[t, s : s + 1, :] for t in range(3)] + [prec_ref[s : s + 1, :]]
            rows = jnp.concatenate([jnp.where(at_rank[s], w, 0.0) for w in words] + [pad], axis=0)
            for part in split3(rows):
                block = [part, empty[1], empty[0]] if side == 0 else [empty[0], part, empty[1]]
                term = dot_t(mine[s], jnp.concatenate(block, axis=0))
                total = term if total is None else total + term
        out_ref[:, pair, :] = total


def unpack_kernel(got_ref, out_ref):
    ntiles = got_ref.shape[0]
    for pair in range(2):
        turned = got_ref[:, pair, :].T
        for side in range(2):
            s = 2 * pair + side
            base = 64 * side
            code = turned[base : base + CAP, :].astype(jnp.int32)
            kidx = code // 4096
            cell = code - kidx * 4096
            row = cell // 128
            col = cell - row * 128
            hi = row // 16
            fields = [hi * 128 + col, row - hi * 16, kidx]
            fields = [f.astype(F32) for f in fields]
            fields += [turned[base + CAP * w : base + CAP * (w + 1), :] for w in range(1, WORDS)]
            for f, value in enumerate(fields):
                for r in range(CAP):
                    out_ref[s, f : f + 1, r * ntiles : (r + 1) * ntiles] = value[r : r + 1, :]
            out_ref[s, 7:8, :] = jnp.zeros((1, CAP * ntiles), F32)


def forcing_kernel(s, chunk, snd_ref, traj_ref, table_ref, *refs):
    if s == 0:
        out_ref, pick, pick8, weight = refs
    else:
        traj_in, out_ref, next_ref, pick, pick8, weight, sem = refs
        copy = pltpu.make_async_copy(traj_in.at[s - 1], next_ref, sem)
        copy.start()
    forcing_body(s, chunk, snd_ref, traj_ref, table_ref, out_ref, pick, pick8, weight)
    if s > 0:
        copy.wait()


def forcing_body(s, chunk, snd_ref, step_traj, table_ref, out_ref, pick, pick8, weight):
    tracers, layers = out_ref.shape[:2]
    slots = snd_ref.shape[2]
    nker = table_ref.shape[2]
    cell_ids = lax.broadcasted_iota(jnp.int32, (256, chunk), 0).astype(F32)
    low_ids = lax.broadcasted_iota(jnp.int32, (16, chunk), 0).astype(F32)
    ker_ids = lax.broadcasted_iota(jnp.int32, (nker, chunk), 0).astype(F32)
    for c in range(slots // chunk):
        at = pl.ds(c * chunk, chunk)
        here = jnp.where(cell_ids == snd_ref[s, 0:1, at], 1.0, 0.0)
        pick[:, at] = here.astype(BF16)
        pick8[:, at] = here.astype(F8)
        low = jnp.where(low_ids == snd_ref[s, 1:2, at], 1.0, 0.0)
        ker = jnp.where(ker_ids == snd_ref[s, 2:3, at], 1.0, 0.0).astype(BF16)
        w = dot(table_ref[0], ker) + dot(table_ref[1], ker) + dot(table_ref[2], ker)
        for k in range(layers):
            weight[k, :, at] = w[k : k + 1, :] * low
    for t in range(tracers):
        lhs = jnp.concatenate(
            [
                step_traj[t, :, 0:16, :].reshape(layers * 16, 128),
                step_traj[t, :, 16:32, :].reshape(layers * 16, 128),
            ],
            axis=1,
        )
        force = None
        for c in range(slots // chunk):
            at = pl.ds(c * chunk, chunk)
            sampled = dot(lhs, pick[:, at]).reshape(layers, 16, chunk)
            model = jnp.sum(jnp.sum(sampled * weight[:, :, at], axis=0), axis=0, keepdims=True)
            sc = (model - snd_ref[s, 3 + t : 4 + t, at]) * snd_ref[s, 6:7, at]
            value = (weight[:, :, at] * sc).reshape(layers * 16, chunk)
            hi = value.astype(BF16)
            lo = ((value - hi.astype(F32)) * LOW).astype(F8)
            term = dot_t(hi, pick[:, at]) + dot_t(lo, pick8[:, at]) * (1.0 / LOW)
            force = term if force is None else force + term
        out_ref[t, :, 0:16, :] = force[:, 0:128].reshape(layers, 16, 128)
        out_ref[t, :, 16:32, :] = force[:, 128:256].reshape(layers, 16, 128)


def end_rows():
    row = lax.broadcasted_iota(jnp.int32, (8, 256), 0)
    lane = lax.broadcasted_iota(jnp.int32, (8, 256), 1) % 128
    ends = ((row == 0) & (lane == 127)) | ((row == 1) & (lane == 0))
    return jnp.where(ends, 1.0, 0.0).astype(BF16)


def lane_shifts():
    src = lax.broadcasted_iota(jnp.int32, (256, 256), 0) % 128
    dst = lax.broadcasted_iota(jnp.int32, (256, 256), 1)
    dst = jnp.where(dst < 128, dst - 1, dst - 127)
    return jnp.where(src == dst, 1.0, 0.0).astype(BF16)


def columns(column_ref, layers):
    at = [0, layers - 1, 2 * layers - 1]
    sizes = [layers - 1, layers, layers - 1]
    return [column_ref.at[pl.ds(a, n)] for a, n in zip(at, sizes)]


def setup_kernel(
    mask_ref, mix_in, tr_in, traj_in, table_in, coef_out, column_ref, lat_w, lon_w, traj_ref, parts_ref,
    tr_ref, flat_ref, table_ref, in_sems, out_sems,
):
    layers = tr_ref.shape[1]
    mix_ref, inv_ref, up_ref = columns(column_ref, layers)
    copies = [
        pltpu.make_async_copy(src, dst, in_sems.at[i])
        for i, (src, dst) in enumerate(
            (
                (mix_in, mix_ref),
                (tr_in, tr_ref),
                (table_in, table_ref),
                (traj_in.at[traj_in.shape[0] - 1], traj_ref),
            )
        )
    ]
    for copy in copies:
        copy.start()
    sent = []

    def send(src, dst):
        sent.append(pltpu.make_async_copy(src, dst, out_sems.at[len(sent)]))
        sent[-1].start()

    copies[0].wait()
    for k in range(layers):
        diag = jnp.ones_like(mix_ref[0])
        if k > 0:
            diag = diag + mix_ref[k - 1]
        if k < layers - 1:
            diag = diag + mix_ref[k]
        if k > 0:
            diag = diag + mix_ref[k - 1] * up
        inv = 1.0 / diag
        inv_ref[k] = inv
        if k < layers - 1:
            up = -mix_ref[k] * inv
            up_ref[k] = up
    copies[1].wait()
    lane = lax.broadcasted_iota(jnp.int32, (32, 128), 1)
    row = lax.broadcasted_iota(jnp.int32, (32, 128), 0)

    def coefs(k, _):
        te, tw, tn, ts = (tr_ref[i, k] for i in range(4))
        flat_ref[0 * layers + k] = jnp.where(lane == 0, 0.0, pltpu.roll(te, 1, axis=1))
        flat_ref[1 * layers + k] = jnp.where(lane == 127, 0.0, pltpu.roll(tw, 127, axis=1))
        flat_ref[2 * layers + k] = jnp.where(row == 0, 0.0, pltpu.roll(tn, 1, axis=0))
        flat_ref[3 * layers + k] = jnp.where(row == 31, 0.0, pltpu.roll(ts, 31, axis=0))
        flat_ref[4 * layers + k] = 1.0 - te - tw - tn - ts
        return 0

    group = layers // 3
    for g in range(3):
        lax.fori_loop(g * group, (g + 1) * group, coefs, 0, unroll=4)
        for i in range(5):
            at = pl.ds(i * layers + g * group, group)
            send(flat_ref.at[at], coef_out.at[at])
    to_north = tr_ref[3, :, 0, :] * mask_ref[0:1, :]
    to_south = tr_ref[2, :, 31, :] * mask_ref[1:2, :]
    odd = mask_ref[2:3, :]
    lat_w[0] = odd * to_north
    lat_w[1] = (1.0 - odd) * to_south
    lat_w[2] = (1.0 - odd) * to_north
    lat_w[3] = odd * to_south
    odd = mask_ref[3:4, 0:1]
    ends = end_rows()[:, 0:128]
    for side in range(2):
        flat = None
        for part in split3(tr_ref[side].reshape(layers * 32, 128)):
            term = dot_t(ends, part)
            flat = term if flat is None else flat + term
        flat = flat[side : side + 1, :]
        lon_w[side] = flat * (odd if side else 1.0 - odd)
        lon_w[2 + side] = flat * (1.0 - odd if side else odd)
    copies[2].wait()
    for i, part in enumerate(split3(table_ref[...])):
        parts_ref[i] = part
    for copy in copies[3:] + sent:
        copy.wait()


def lon_spots(mask_ref, lon_a, lon_b, first, size, cols):
    row = lax.broadcasted_iota(jnp.int32, (4, cols), 0)
    lane = lax.broadcasted_iota(jnp.int32, (4, cols), 1)
    other = (row % 2).astype(F32)
    lon_odd = jnp.broadcast_to(mask_ref[3:4, :], (4, cols))
    spot = (other * lon_odd + (1.0 - other) * (1.0 - lon_odd)) * (cols - 1)
    place = jnp.where(lane.astype(F32) == spot, 1.0, 0.0).astype(BF16)
    at = slice(first, first + size)
    hi, lo = split2(jnp.concatenate([lon_a[:, at], lon_b[:, at]], axis=0))
    both = jnp.concatenate([hi, lo], axis=0)
    return lax.dot_general(both, place, (((0,), (0,)), ((), ())), preferred_element_type=F32)


def lat_rows(mask_ref, lat_a, lat_b, layers):
    odd = mask_ref[2:3, :] > 0.5
    a, b = lat_a[...].astype(F32), lat_b[...].astype(F32)
    north, south = jnp.where(odd, a, b), jnp.where(odd, b, a)
    return [(x[0:layers], x[layers : 2 * layers], x[2 * layers :]) for x in (north, south)]


def spread(mask_ref, lon_a, lon_b, lat_a, lat_b, halo):
    tracers, layers, rows, cols = halo.shape
    size = layers * rows
    north, south = lat_rows(mask_ref, lat_a, lat_b, layers)
    for t in range(tracers):
        halo[t] = lon_spots(mask_ref, lon_a, lon_b, t * size, size, cols).reshape(layers, rows, cols)
        halo[t, :, 0, :] += north[t]
        halo[t, :, rows - 1, :] += south[t]


def vertical(base, force_ref, column_ref, v):
    tracers, layers = v.shape[:2]
    mix_ref, inv_ref, up_ref = columns(column_ref, layers)
    d = tuple((force_ref[t, 0] + base(t, 0)) * inv_ref[0] for t in range(tracers))
    for t in range(tracers):
        v[t, 0] = d[t]

    def forward(k, d):
        m, inv = mix_ref[k - 1], inv_ref[k]
        d = tuple((force_ref[t, k] + base(t, k) + m * d[t]) * inv for t in range(tracers))
        for t in range(tracers):
            v[t, k] = d[t]
        return d

    d = lax.fori_loop(1, layers, forward, d, unroll=5)

    def backward(i, x):
        k = layers - 2 - i
        u = up_ref[k]
        x = tuple(v[t, k] - u * x[t] for t in range(tracers))
        for t in range(tracers):
            v[t, k] = x[t]
        return x

    lax.fori_loop(0, layers - 1, backward, d, unroll=5)


def horizontal(v, coef_ref=None, w_out=None, weights=None, edges=None):
    tracers, layers, rows, cols = v.shape
    shifts, end_lanes = lane_shifts(), end_rows()
    group = 12
    size = group * rows
    for t in range(tracers):
        for g in range(0, layers, group):
            x = v[t, g : g + group]
            both = jnp.concatenate(split2(x.reshape(size, cols)), axis=1)
            if edges is not None:
                (_, lon_w), (lon_a, lon_b) = weights, edges[:2]
                ends = dot_t(end_lanes, both)
                to = pl.ds((t * layers + g) * rows, size)
                at = pl.ds(g * rows, size)
                lon_a[:, to] = ends[0:1, :] * lon_w[0, :, at] + ends[1:2, :] * lon_w[1, :, at]
                lon_b[:, to] = ends[0:1, :] * lon_w[2, :, at] + ends[1:2, :] * lon_w[3, :, at]
            if w_out is not None:
                moved = dot(both, shifts)
                c = [coef_ref[i * layers + g : i * layers + g + group].reshape(size, cols) for i in range(5)]
                down = jnp.stack([pltpu.roll(x[i], 1, axis=0) for i in range(group)])
                up = jnp.stack([pltpu.roll(x[i], rows - 1, axis=0) for i in range(group)])
                out = c[4] * x.reshape(size, cols) + c[0] * moved[:, :cols] + c[1] * moved[:, cols:]
                out = out + c[2] * down.reshape(size, cols) + c[3] * up.reshape(size, cols)
                w_out[t, g : g + group] = out.reshape(group, rows, cols)
    if edges is not None:
        (lat_w, _), (lat_a, lat_b) = weights, edges[2:]
        ends = [(v[t, :, 0, :], v[t, :, rows - 1, :]) for t in range(tracers)]
        to_a = [top * lat_w[0] + low * lat_w[1] for top, low in ends]
        to_b = [top * lat_w[2] + low * lat_w[3] for top, low in ends]
        lat_a[...] = jnp.concatenate(to_a, axis=0).astype(BF16)
        lat_b[...] = jnp.concatenate(to_b, axis=0).astype(BF16)


def head_kernel(
    s, chunk, got_ref, traj_ref, parts_ref, traj_in, coef_in,
    out_ref, snd_ref, next_ref, coef_ref, pick, pick8, weight, sems,
):
    pairs = ((traj_in.at[s - 1], next_ref), (coef_in, coef_ref))
    copies = [pltpu.make_async_copy(a, b, sems.at[i]) for i, (a, b) in enumerate(pairs)]
    for copy in copies:
        copy.start()
    unpack_kernel(got_ref, snd_ref)
    forcing_body(s, chunk, snd_ref, traj_ref, parts_ref, out_ref, pick, pick8, weight)
    for copy in copies:
        copy.wait()


def first_step_kernel(force_ref, column_ref, coef_ref, lat_w, lon_w, w_out, *refs):
    edges, v = refs[:4], refs[4]
    vertical(lambda t, k: 0.0, force_ref, column_ref, v)
    horizontal(v, coef_ref, w_out, (lat_w, lon_w), edges)


def step_kernel(
    start, whole, mask_ref, w_in, lat_b, lat_a, lon_b, lon_a, *refs
):
    flux_in, refs = (None, refs) if start else (refs[0], refs[1:])
    force_ref, column_ref, coef_ref, lat_w, lon_w, w_out = refs[:6]
    refs = refs[6:]
    edges, flux_out, halo, v = refs[:4], refs[4], refs[5], refs[6] if whole else w_out
    spread(mask_ref, lon_a, lon_b, lat_a, lat_b, halo)

    def base(t, k):
        value = w_in[t, k] + halo[t, k]
        if isinstance(k, int):
            flux_out[t] = value if start else flux_in[t] + value
        return value

    vertical(base, force_ref, column_ref, v)
    horizontal(v, coef_ref if whole else None, w_out if whole else None, (lat_w, lon_w), edges)


def interior_kernel(v, coef_ref, w_out):
    horizontal(v, coef_ref, w_out)


def last_kernel(
    mask_ref, w_in, lat_b, lat_a, lon_b, lon_a, flux_in, adj_out, flux_out, done, sems
):
    tracers, layers, rows, cols = w_in.shape
    north, south = lat_rows(mask_ref, lat_a, lat_b, layers)
    group = layers // 3
    size = group * rows
    copies = []
    for t in range(tracers):
        for g in range(3):
            first = t * layers * rows + g * size
            at = (t, pl.ds(g * group, group))
            spots = lon_spots(mask_ref, lon_a, lon_b, first, size, cols)
            done[at] = w_in[at] + spots.reshape(group, rows, cols)
            done[t, g * group : (g + 1) * group, 0, :] += north[t][g * group : (g + 1) * group]
            done[t, g * group : (g + 1) * group, rows - 1, :] += south[t][g * group : (g + 1) * group]
            copies.append(pltpu.make_async_copy(done.at[at], adj_out.at[at], sems.at[3 * t + g]))
            copies[-1].start()
    flux_out[...] = flux_in[...] + done[:, 0]
    for copy in copies:
        copy.wait()


def swaps(axis):
    peers = lax.axis_size(axis)
    near = [(i, i + 1 - 2 * (i % 2)) for i in range(peers)]
    return near, [((i + 1) % peers, (j + 1) % peers) for i, j in near]


def exchange(lon_a, lon_b, lat_a, lat_b):
    lat_near, lat_far = swaps("lat")
    lon_near, lon_far = swaps("lon")
    lon_b = lax.ppermute(lon_b, "lon", lon_far)
    lat_b = lax.ppermute(lat_b, "lat", lat_far)
    lon_a = lax.ppermute(lon_a, "lon", lon_near)
    lat_a = lax.ppermute(lat_a, "lat", lat_near)
    return lat_b, lat_a, lon_b, lon_a


def body(
    transport, mixing, trajectory, kernel_table, track_tile, sound_cell, kernel_index, observed, precision
):
    ntiles = lax.axis_size(("lat", "lon"))
    steps, tracers, layers, rows, cols = trajectory.shape
    count = sound_cell.shape[1]
    field = sds(tracers, layers, rows, cols)
    plane = sds(tracers, rows, cols)
    lat_edge = sds(tracers * layers, cols, dtype=BF16)
    lon_edge = sds(1, 7168)
    slots = ntiles * CAP
    outgoing = call(
        route_kernel,
        sds(ntiles, 2, 128),
        track_tile.transpose(0, 2, 1),
        sound_cell,
        kernel_index,
        observed.transpose(1, 0, 2),
        precision,
        hbm=range(5),
        scratch=(
            pltpu.VMEM((steps, 1, count), jnp.int32),
            pltpu.VMEM((steps, count), jnp.int32),
            pltpu.VMEM((steps, count), jnp.int32),
            pltpu.VMEM((tracers, steps, count), F32),
            pltpu.VMEM((steps, count), F32),
            pltpu.SemaphoreType.DMA((5,)),
        ),
    )
    got = lax.all_to_all(outgoing, ("lat", "lon"), split_axis=0, concat_axis=0, tiled=True)
    lat, lon = lax.axis_index("lat"), lax.axis_index("lon")
    mask = jnp.stack([lat > 0, lat < lax.axis_size("lat") - 1, lat % 2 > 0, lon % 2 > 0]).astype(F32)
    mask = jnp.broadcast_to(mask[:, None], (4, cols))
    one_step = sds(*trajectory.shape[1:], dtype=BF16)
    table = kernel_table.T
    coef, column, lat_w, lon_w, now, parts = call(
        setup_kernel,
        (
            sds(5 * layers, rows, cols),
            sds(3 * layers - 2, rows, cols),
            sds(4, layers, cols),
            sds(4, 1, layers * rows),
            one_step,
            sds(3, *table.shape, dtype=BF16),
        ),
        mask,
        mixing,
        transport,
        trajectory,
        table,
        hbm=(1, 2, 3, 4),
        hbm_out=(0,),
        scratch=(
            pltpu.VMEM(transport.shape, F32),
            pltpu.VMEM((5 * layers, rows, cols), F32),
            pltpu.VMEM(table.shape, F32),
            pltpu.SemaphoreType.DMA((4,)),
            pltpu.SemaphoreType.DMA((15,)),
        ),
    )
    work = (
        pltpu.VMEM((256, slots), BF16),
        pltpu.VMEM((256, slots), F8),
        pltpu.VMEM((layers, 16, slots), F32),
    )
    force, snd, now, coef = call(
        functools.partial(head_kernel, steps - 1, slots),
        (
            field,
            sds(steps, 8, slots),
            one_step,
            sds(*coef.shape),
        ),
        got,
        now,
        parts,
        trajectory,
        coef,
        hbm=(3, 4),
        scratch=work + (pltpu.SemaphoreType.DMA((2,)),),
    )
    fixed = (column, coef, lat_w, lon_w)

    def forcing(s, now):
        kernel = functools.partial(forcing_kernel, s, slots)
        if s == 0:
            return call(kernel, field, snd, now, parts, scratch=work), None
        return call(
            kernel,
            (field, one_step),
            snd,
            now,
            parts,
            trajectory,
            hbm=(3,),
            scratch=work + (pltpu.SemaphoreType.DMA,),
        )

    v = pltpu.VMEM(field.shape, F32)
    moved = (field, lon_edge, lon_edge, lat_edge, lat_edge)
    w, *edges = call(first_step_kernel, moved, force, *fixed, scratch=(v,))
    flux = []
    for s in range(steps - 2, -1, -1):
        halos = exchange(*edges)
        force, now = forcing(s, now)
        *done, flux = call(
            functools.partial(step_kernel, s == steps - 2, s > 0),
            moved + (plane,),
            mask,
            w,
            *halos,
            *flux,
            force,
            *fixed,
            scratch=(v, v) if s > 0 else (v,),
        )
        (w, *edges), flux = done, [flux]
    return call(
        last_kernel,
        (field, plane),
        mask,
        call(interior_kernel, field, w, coef),
        *exchange(*edges),
        *flux,
        hbm_out=(0,),
        scratch=(v, pltpu.SemaphoreType.DMA((3 * tracers,))),
    )


def solution(mesh):
    return jax.shard_map(
        body,
        mesh=mesh,
        in_specs=(
            P(None, None, "lat", "lon"),
            P(None, "lat", "lon"),
            P(None, None, None, "lat", "lon"),
            P(),
            P(None, ("lat", "lon"), None),
            P(None, ("lat", "lon")),
            P(None, ("lat", "lon")),
            P(None, None, ("lat", "lon")),
            P(None, ("lat", "lon")),
        ),
        out_specs=(P(None, None, "lat", "lon"), P(None, "lat", "lon")),
        check_vma=False,
    )
```

```python
import functools

import jax
import jax.numpy as jnp
from jax import lax
from jax.experimental import pallas as pl
from jax.experimental.pallas import tpu as pltpu
from jax.sharding import PartitionSpec as P

CAP = 8
WORDS = 5
F32 = jnp.float32
BF16 = jnp.bfloat16
F8 = jnp.float8_e4m3fn
LOW = 256.0


def split3(x):
    hi = x.astype(BF16)
    rest = x - hi.astype(F32)
    mid = rest.astype(BF16)
    return hi, mid, (rest - mid.astype(F32)).astype(BF16)


def split2(x):
    hi = x.astype(BF16)
    return hi, (x - hi.astype(F32)).astype(BF16)


def dot(a, b):
    return jnp.dot(a, b, preferred_element_type=F32)


def dot_t(a, b):
    return lax.dot_general(a, b, (((1,), (1,)), ((), ())), preferred_element_type=F32)


VMEM = pl.BlockSpec(memory_space=pltpu.VMEM)
HBM = pl.BlockSpec(memory_space=pltpu.HBM)


def call(kernel, outs, *args, scratch=(), vmem=20 << 20, hbm=(), hbm_out=()):
    outs = tuple(outs) if isinstance(outs, (tuple, list)) else (outs,)
    args = [pltpu.with_memory_space_constraint(a, pltpu.HBM) if i in hbm else a for i, a in enumerate(args)]
    done = pl.pallas_call(
        kernel,
        out_shape=tuple(pltpu.HBM(o.shape, o.dtype) if i in hbm_out else o for i, o in enumerate(outs)),
        in_specs=[HBM if i in hbm else VMEM for i in range(len(args))],
        out_specs=tuple(HBM if i in hbm_out else VMEM for i in range(len(outs))),
        scratch_shapes=list(scratch),
        compiler_params=pltpu.CompilerParams(vmem_limit_bytes=vmem),
    )(*args)
    return done if len(outs) > 1 else done[0]


def sds(*shape, dtype=F32):
    return jax.ShapeDtypeStruct(shape, dtype)


def route_kernel(
    tile_in, cell_in, index_in, obs_in, prec_in, out_ref, tile_ref, cell_ref, index_ref, obs_ref, prec_ref, sems
):
    copies = [
        pltpu.make_async_copy(src, dst, sems.at[i])
        for i, (src, dst) in enumerate(
            (
                (tile_in, tile_ref),
                (cell_in, cell_ref),
                (index_in, index_ref),
                (obs_in, obs_ref),
                (prec_in, prec_ref),
            )
        )
    ]
    for copy in copies:
        copy.start()
    steps, count = cell_ref.shape
    ntiles = out_ref.shape[0]
    tile_ids = lax.broadcasted_iota(jnp.int32, (ntiles, count), 0)
    before = (
        lax.broadcasted_iota(jnp.int32, (count, count), 0)
        < lax.broadcasted_iota(jnp.int32, (count, count), 1)
    ).astype(F32).astype(BF16)
    rank_ids = lax.broadcasted_iota(jnp.int32, (CAP, count), 0)
    pad = jnp.zeros((48 - CAP * WORDS, count), F32)
    empty = [jnp.zeros((n, count), BF16) for n in (64, 16)]
    copies[0].wait()
    mine, at_rank = [], []
    for s in range(steps):
        here = tile_ids == tile_ref[s]
        here_f = jnp.where(here, 1.0, 0.0)
        mine.append(here_f.astype(BF16))
        rank = jnp.sum(here_f * dot(mine[s], before), axis=0, keepdims=True).astype(jnp.int32)
        at_rank.append(rank_ids == rank)
    for copy in copies[1:]:
        copy.wait()
    for pair in range(steps // 2):
        total = None
        for side in range(2):
            s = 2 * pair + side
            code = (index_ref[s : s + 1, :] * 4096 + cell_ref[s : s + 1, :]).astype(F32)
            words = [code] + [obs_ref[t, s : s + 1, :] for t in range(3)] + [prec_ref[s : s + 1, :]]
            rows = jnp.concatenate([jnp.where(at_rank[s], w, 0.0) for w in words] + [pad], axis=0)
            for part in split3(rows):
                block = [part, empty[1], empty[0]] if side == 0 else [empty[0], part, empty[1]]
                term = dot_t(mine[s], jnp.concatenate(block, axis=0))
                total = term if total is None else total + term
        out_ref[:, pair, :] = total


def unpack_kernel(got_ref, out_ref):
    ntiles = got_ref.shape[0]
    for pair in range(2):
        turned = got_ref[:, pair, :].T
        for side in range(2):
            s = 2 * pair + side
            base = 64 * side
            code = turned[base : base + CAP, :].astype(jnp.int32)
            kidx = code // 4096
            cell = code - kidx * 4096
            row = cell // 128
            col = cell - row * 128
            hi = row // 16
            fields = [hi * 128 + col, row - hi * 16, kidx]
            fields = [f.astype(F32) for f in fields]
            fields += [turned[base + CAP * w : base + CAP * (w + 1), :] for w in range(1, WORDS)]
            for f, value in enumerate(fields):
                for r in range(CAP):
                    out_ref[s, f : f + 1, r * ntiles : (r + 1) * ntiles] = value[r : r + 1, :]
            out_ref[s, 7:8, :] = jnp.zeros((1, CAP * ntiles), F32)


def forcing_kernel(s, chunk, snd_ref, traj_ref, table_ref, *refs):
    if s == 0:
        out_ref, pick, pick8, weight = refs
    else:
        traj_in, out_ref, next_ref, pick, pick8, weight, sem = refs
        copy = pltpu.make_async_copy(traj_in.at[s - 1], next_ref, sem)
        copy.start()
    forcing_body(s, chunk, snd_ref, traj_ref, table_ref, out_ref, pick, pick8, weight)
    if s > 0:
        copy.wait()


def forcing_body(s, chunk, snd_ref, step_traj, table_ref, out_ref, pick, pick8, weight):
    tracers, layers = out_ref.shape[:2]
    slots = snd_ref.shape[2]
    nker = table_ref.shape[2]
    cell_ids = lax.broadcasted_iota(jnp.int32, (256, chunk), 0).astype(F32)
    low_ids = lax.broadcasted_iota(jnp.int32, (16, chunk), 0).astype(F32)
    ker_ids = lax.broadcasted_iota(jnp.int32, (nker, chunk), 0).astype(F32)
    for c in range(slots // chunk):
        at = pl.ds(c * chunk, chunk)
        here = jnp.where(cell_ids == snd_ref[s, 0:1, at], 1.0, 0.0)
        pick[:, at] = here.astype(BF16)
        pick8[:, at] = here.astype(F8)
        low = jnp.where(low_ids == snd_ref[s, 1:2, at], 1.0, 0.0)
        ker = jnp.where(ker_ids == snd_ref[s, 2:3, at], 1.0, 0.0).astype(BF16)
        w = dot(table_ref[0], ker) + dot(table_ref[1], ker) + dot(table_ref[2], ker)
        for k in range(layers):
            weight[k, :, at] = w[k : k + 1, :] * low
    for t in range(tracers):
        lhs = jnp.concatenate(
            [
                step_traj[t, :, 0:16, :].reshape(layers * 16, 128),
                step_traj[t, :, 16:32, :].reshape(layers * 16, 128),
            ],
            axis=1,
        )
        force = None
        for c in range(slots // chunk):
            at = pl.ds(c * chunk, chunk)
            sampled = dot(lhs, pick[:, at]).reshape(layers, 16, chunk)
            model = jnp.sum(jnp.sum(sampled * weight[:, :, at], axis=0), axis=0, keepdims=True)
            sc = (model - snd_ref[s, 3 + t : 4 + t, at]) * snd_ref[s, 6:7, at]
            value = (weight[:, :, at] * sc).reshape(layers * 16, chunk)
            hi = value.astype(BF16)
            lo = ((value - hi.astype(F32)) * LOW).astype(F8)
            term = dot_t(hi, pick[:, at]) + dot_t(lo, pick8[:, at]) * (1.0 / LOW)
            force = term if force is None else force + term
        out_ref[t, :, 0:16, :] = force[:, 0:128].reshape(layers, 16, 128)
        out_ref[t, :, 16:32, :] = force[:, 128:256].reshape(layers, 16, 128)


def end_rows():
    row = lax.broadcasted_iota(jnp.int32, (8, 256), 0)
    lane = lax.broadcasted_iota(jnp.int32, (8, 256), 1) % 128
    ends = ((row == 0) & (lane == 127)) | ((row == 1) & (lane == 0))
    return jnp.where(ends, 1.0, 0.0).astype(BF16)


def lane_shifts():
    src = lax.broadcasted_iota(jnp.int32, (256, 256), 0) % 128
    dst = lax.broadcasted_iota(jnp.int32, (256, 256), 1)
    dst = jnp.where(dst < 128, dst - 1, dst - 127)
    return jnp.where(src == dst, 1.0, 0.0).astype(BF16)


def columns(column_ref, layers):
    at = [0, layers - 1, 2 * layers - 1]
    sizes = [layers - 1, layers, layers - 1]
    return [column_ref.at[pl.ds(a, n)] for a, n in zip(at, sizes)]


def setup_kernel(
    mask_ref, mix_in, tr_in, traj_in, coef_out, column_ref, lat_w, lon_w, traj_ref,
    tr_ref, flat_ref, in_sems, out_sems,
):
    layers = tr_ref.shape[1]
    mix_ref, inv_ref, up_ref = columns(column_ref, layers)
    copies = [
        pltpu.make_async_copy(src, dst, in_sems.at[i])
        for i, (src, dst) in enumerate(((mix_in, mix_ref), (tr_in, tr_ref), (traj_in.at[traj_in.shape[0] - 1], traj_ref)))
    ]
    for copy in copies:
        copy.start()
    sent = []

    def send(src, dst):
        sent.append(pltpu.make_async_copy(src, dst, out_sems.at[len(sent)]))
        sent[-1].start()

    copies[0].wait()
    for k in range(layers):
        diag = jnp.ones_like(mix_ref[0])
        if k > 0:
            diag = diag + mix_ref[k - 1]
        if k < layers - 1:
            diag = diag + mix_ref[k]
        if k > 0:
            diag = diag + mix_ref[k - 1] * up
        inv = 1.0 / diag
        inv_ref[k] = inv
        if k < layers - 1:
            up = -mix_ref[k] * inv
            up_ref[k] = up
    copies[1].wait()
    lane = lax.broadcasted_iota(jnp.int32, (32, 128), 1)
    row = lax.broadcasted_iota(jnp.int32, (32, 128), 0)

    def coefs(k, _):
        te, tw, tn, ts = (tr_ref[i, k] for i in range(4))
        flat_ref[0 * layers + k] = jnp.where(lane == 0, 0.0, pltpu.roll(te, 1, axis=1))
        flat_ref[1 * layers + k] = jnp.where(lane == 127, 0.0, pltpu.roll(tw, 127, axis=1))
        flat_ref[2 * layers + k] = jnp.where(row == 0, 0.0, pltpu.roll(tn, 1, axis=0))
        flat_ref[3 * layers + k] = jnp.where(row == 31, 0.0, pltpu.roll(ts, 31, axis=0))
        flat_ref[4 * layers + k] = 1.0 - te - tw - tn - ts
        return 0

    group = layers // 3
    for g in range(3):
        lax.fori_loop(g * group, (g + 1) * group, coefs, 0, unroll=4)
        for i in range(5):
            at = pl.ds(i * layers + g * group, group)
            send(flat_ref.at[at], coef_out.at[at])
    to_north = tr_ref[3, :, 0, :] * mask_ref[0:1, :]
    to_south = tr_ref[2, :, 31, :] * mask_ref[1:2, :]
    odd = mask_ref[2:3, :]
    lat_w[0] = odd * to_north
    lat_w[1] = (1.0 - odd) * to_south
    lat_w[2] = (1.0 - odd) * to_north
    lat_w[3] = odd * to_south
    odd = mask_ref[3:4, 0:1]
    ends = end_rows()[:, 0:128]
    for side in range(2):
        flat = None
        for part in split3(tr_ref[side].reshape(layers * 32, 128)):
            term = dot_t(ends, part)
            flat = term if flat is None else flat + term
        flat = flat[side : side + 1, :]
        lon_w[side] = flat * (odd if side else 1.0 - odd)
        lon_w[2 + side] = flat * (1.0 - odd if side else odd)
    for copy in copies[2:] + sent:
        copy.wait()


def lon_spots(mask_ref, lon_a, lon_b, first, size, cols):
    row = lax.broadcasted_iota(jnp.int32, (4, cols), 0)
    lane = lax.broadcasted_iota(jnp.int32, (4, cols), 1)
    other = (row % 2).astype(F32)
    lon_odd = jnp.broadcast_to(mask_ref[3:4, :], (4, cols))
    spot = (other * lon_odd + (1.0 - other) * (1.0 - lon_odd)) * (cols - 1)
    place = jnp.where(lane.astype(F32) == spot, 1.0, 0.0).astype(BF16)
    at = slice(first, first + size)
    hi, lo = split2(jnp.concatenate([lon_a[:, at], lon_b[:, at]], axis=0))
    both = jnp.concatenate([hi, lo], axis=0)
    return lax.dot_general(both, place, (((0,), (0,)), ((), ())), preferred_element_type=F32)


def lat_rows(mask_ref, lat_a, lat_b, layers):
    odd = mask_ref[2:3, :] > 0.5
    a, b = lat_a[...].astype(F32), lat_b[...].astype(F32)
    north, south = jnp.where(odd, a, b), jnp.where(odd, b, a)
    return [(x[0:layers], x[layers : 2 * layers], x[2 * layers :]) for x in (north, south)]


def spread(mask_ref, lon_a, lon_b, lat_a, lat_b, halo):
    tracers, layers, rows, cols = halo.shape
    size = layers * rows
    north, south = lat_rows(mask_ref, lat_a, lat_b, layers)
    for t in range(tracers):
        halo[t] = lon_spots(mask_ref, lon_a, lon_b, t * size, size, cols).reshape(layers, rows, cols)
        halo[t, :, 0, :] += north[t]
        halo[t, :, rows - 1, :] += south[t]


def vertical(base, force_ref, column_ref, v):
    tracers, layers = v.shape[:2]
    mix_ref, inv_ref, up_ref = columns(column_ref, layers)
    d = tuple((force_ref[t, 0] + base(t, 0)) * inv_ref[0] for t in range(tracers))
    for t in range(tracers):
        v[t, 0] = d[t]

    def forward(k, d):
        m, inv = mix_ref[k - 1], inv_ref[k]
        d = tuple((force_ref[t, k] + base(t, k) + m * d[t]) * inv for t in range(tracers))
        for t in range(tracers):
            v[t, k] = d[t]
        return d

    d = lax.fori_loop(1, layers, forward, d, unroll=35)

    def backward(i, x):
        k = layers - 2 - i
        u = up_ref[k]
        x = tuple(v[t, k] - u * x[t] for t in range(tracers))
        for t in range(tracers):
            v[t, k] = x[t]
        return x

    lax.fori_loop(0, layers - 1, backward, d, unroll=35)


def horizontal(v, coef_ref=None, w_out=None, weights=None, edges=None):
    tracers, layers, rows, cols = v.shape
    shifts, end_lanes = lane_shifts(), end_rows()
    group = 12
    size = group * rows
    for t in range(tracers):
        for g in range(0, layers, group):
            x = v[t, g : g + group]
            both = jnp.concatenate(split2(x.reshape(size, cols)), axis=1)
            if edges is not None:
                (_, lon_w), (lon_a, lon_b) = weights, edges[:2]
                ends = dot_t(end_lanes, both)
                to = pl.ds((t * layers + g) * rows, size)
                at = pl.ds(g * rows, size)
                lon_a[:, to] = ends[0:1, :] * lon_w[0, :, at] + ends[1:2, :] * lon_w[1, :, at]
                lon_b[:, to] = ends[0:1, :] * lon_w[2, :, at] + ends[1:2, :] * lon_w[3, :, at]
            if w_out is not None:
                moved = dot(both, shifts)
                c = [coef_ref[i * layers + g : i * layers + g + group].reshape(size, cols) for i in range(5)]
                down = jnp.stack([pltpu.roll(x[i], 1, axis=0) for i in range(group)])
                up = jnp.stack([pltpu.roll(x[i], rows - 1, axis=0) for i in range(group)])
                out = c[4] * x.reshape(size, cols) + c[0] * moved[:, :cols] + c[1] * moved[:, cols:]
                out = out + c[2] * down.reshape(size, cols) + c[3] * up.reshape(size, cols)
                w_out[t, g : g + group] = out.reshape(group, rows, cols)
    if edges is not None:
        (lat_w, _), (lat_a, lat_b) = weights, edges[2:]
        ends = [(v[t, :, 0, :], v[t, :, rows - 1, :]) for t in range(tracers)]
        to_a = [top * lat_w[0] + low * lat_w[1] for top, low in ends]
        to_b = [top * lat_w[2] + low * lat_w[3] for top, low in ends]
        lat_a[...] = jnp.concatenate(to_a, axis=0).astype(BF16)
        lat_b[...] = jnp.concatenate(to_b, axis=0).astype(BF16)


def head_kernel(
    s, chunk, got_ref, traj_ref, table_in, traj_in, coef_in,
    out_ref, snd_ref, parts_ref, next_ref, coef_ref, pick, pick8, weight, table_ref, sems,
):
    pairs = ((table_in, table_ref), (traj_in.at[s - 1], next_ref), (coef_in, coef_ref))
    copies = [pltpu.make_async_copy(a, b, sems.at[i]) for i, (a, b) in enumerate(pairs)]
    for copy in copies:
        copy.start()
    unpack_kernel(got_ref, snd_ref)
    copies[0].wait()
    for i, part in enumerate(split3(table_ref[...])):
        parts_ref[i] = part
    forcing_body(s, chunk, snd_ref, traj_ref, parts_ref, out_ref, pick, pick8, weight)
    for copy in copies[1:]:
        copy.wait()


def first_step_kernel(force_ref, column_ref, coef_ref, lat_w, lon_w, w_out, *refs):
    edges, v = refs[:4], refs[4]
    vertical(lambda t, k: 0.0, force_ref, column_ref, v)
    horizontal(v, coef_ref, w_out, (lat_w, lon_w), edges)


def step_kernel(
    start, whole, mask_ref, w_in, lat_b, lat_a, lon_b, lon_a, *refs
):
    flux_in, refs = (None, refs) if start else (refs[0], refs[1:])
    force_ref, column_ref, coef_ref, lat_w, lon_w, w_out = refs[:6]
    refs = refs[6:]
    edges, flux_out, halo, v = refs[:4], refs[4], refs[5], refs[6] if whole else w_out
    spread(mask_ref, lon_a, lon_b, lat_a, lat_b, halo)

    def base(t, k):
        value = w_in[t, k] + halo[t, k]
        if isinstance(k, int):
            flux_out[t] = value if start else flux_in[t] + value
        return value

    vertical(base, force_ref, column_ref, v)
    horizontal(v, coef_ref if whole else None, w_out if whole else None, (lat_w, lon_w), edges)


def interior_kernel(v, coef_ref, w_out):
    horizontal(v, coef_ref, w_out)


def last_kernel(
    mask_ref, w_in, lat_b, lat_a, lon_b, lon_a, flux_in, adj_out, flux_out, done, sems
):
    tracers, layers, rows, cols = w_in.shape
    north, south = lat_rows(mask_ref, lat_a, lat_b, layers)
    group = layers // 3
    size = group * rows
    copies = []
    for t in range(tracers):
        for g in range(3):
            first = t * layers * rows + g * size
            at = (t, pl.ds(g * group, group))
            spots = lon_spots(mask_ref, lon_a, lon_b, first, size, cols)
            done[at] = w_in[at] + spots.reshape(group, rows, cols)
            done[t, g * group : (g + 1) * group, 0, :] += north[t][g * group : (g + 1) * group]
            done[t, g * group : (g + 1) * group, rows - 1, :] += south[t][g * group : (g + 1) * group]
            copies.append(pltpu.make_async_copy(done.at[at], adj_out.at[at], sems.at[3 * t + g]))
            copies[-1].start()
    flux_out[...] = flux_in[...] + done[:, 0]
    for copy in copies:
        copy.wait()


def swaps(axis):
    peers = lax.axis_size(axis)
    near = [(i, i + 1 - 2 * (i % 2)) for i in range(peers)]
    return near, [((i + 1) % peers, (j + 1) % peers) for i, j in near]


def exchange(lon_a, lon_b, lat_a, lat_b):
    lat_near, lat_far = swaps("lat")
    lon_near, lon_far = swaps("lon")
    lon_b = lax.ppermute(lon_b, "lon", lon_far)
    lat_b = lax.ppermute(lat_b, "lat", lat_far)
    lon_a = lax.ppermute(lon_a, "lon", lon_near)
    lat_a = lax.ppermute(lat_a, "lat", lat_near)
    return lat_b, lat_a, lon_b, lon_a


def body(
    transport, mixing, trajectory, kernel_table, track_tile, sound_cell, kernel_index, observed, precision
):
    ntiles = lax.axis_size(("lat", "lon"))
    steps, tracers, layers, rows, cols = trajectory.shape
    count = sound_cell.shape[1]
    field = sds(tracers, layers, rows, cols)
    plane = sds(tracers, rows, cols)
    lat_edge = sds(tracers * layers, cols, dtype=BF16)
    lon_edge = sds(1, 7168)
    slots = ntiles * CAP
    outgoing = call(
        route_kernel,
        sds(ntiles, 2, 128),
        track_tile.transpose(0, 2, 1),
        sound_cell,
        kernel_index,
        observed.transpose(1, 0, 2),
        precision,
        hbm=range(5),
        scratch=(
            pltpu.VMEM((steps, 1, count), jnp.int32),
            pltpu.VMEM((steps, count), jnp.int32),
            pltpu.VMEM((steps, count), jnp.int32),
            pltpu.VMEM((tracers, steps, count), F32),
            pltpu.VMEM((steps, count), F32),
            pltpu.SemaphoreType.DMA((5,)),
        ),
    )
    got = lax.all_to_all(outgoing, ("lat", "lon"), split_axis=0, concat_axis=0, tiled=True)
    lat, lon = lax.axis_index("lat"), lax.axis_index("lon")
    mask = jnp.stack([lat > 0, lat < lax.axis_size("lat") - 1, lat % 2 > 0, lon % 2 > 0]).astype(F32)
    mask = jnp.broadcast_to(mask[:, None], (4, cols))
    one_step = sds(*trajectory.shape[1:], dtype=BF16)
    coef, column, lat_w, lon_w, now = call(
        setup_kernel,
        (
            sds(5 * layers, rows, cols),
            sds(3 * layers - 2, rows, cols),
            sds(4, layers, cols),
            sds(4, 1, layers * rows),
            one_step,
        ),
        mask,
        mixing,
        transport,
        trajectory,
        hbm=(1, 2, 3),
        hbm_out=(0,),
        scratch=(
            pltpu.VMEM(transport.shape, F32),
            pltpu.VMEM((5 * layers, rows, cols), F32),
            pltpu.SemaphoreType.DMA((3,)),
            pltpu.SemaphoreType.DMA((15,)),
        ),
    )
    table = kernel_table.T
    work = (
        pltpu.VMEM((256, slots), BF16),
        pltpu.VMEM((256, slots), F8),
        pltpu.VMEM((layers, 16, slots), F32),
    )
    force, snd, parts, now, coef = call(
        functools.partial(head_kernel, steps - 1, slots),
        (
            field,
            sds(steps, 8, slots),
            sds(3, *table.shape, dtype=BF16),
            one_step,
            sds(*coef.shape),
        ),
        got,
        now,
        table,
        trajectory,
        coef,
        hbm=(2, 3, 4),
        scratch=work + (pltpu.VMEM(table.shape, F32), pltpu.SemaphoreType.DMA((3,))),
    )
    fixed = (column, coef, lat_w, lon_w)

    def forcing(s, now):
        kernel = functools.partial(forcing_kernel, s, slots)
        if s == 0:
            return call(kernel, field, snd, now, parts, scratch=work), None
        return call(
            kernel,
            (field, one_step),
            snd,
            now,
            parts,
            trajectory,
            hbm=(3,),
            scratch=work + (pltpu.SemaphoreType.DMA,),
        )

    v = pltpu.VMEM(field.shape, F32)
    moved = (field, lon_edge, lon_edge, lat_edge, lat_edge)
    w, *edges = call(first_step_kernel, moved, force, *fixed, scratch=(v,))
    flux = []
    for s in range(steps - 2, -1, -1):
        halos = exchange(*edges)
        force, now = forcing(s, now)
        *done, flux = call(
            functools.partial(step_kernel, s == steps - 2, s > 0),
            moved + (plane,),
            mask,
            w,
            *halos,
            *flux,
            force,
            *fixed,
            scratch=(v, v) if s > 0 else (v,),
        )
        (w, *edges), flux = done, [flux]
    return call(
        last_kernel,
        (field, plane),
        mask,
        call(interior_kernel, field, w, coef),
        *exchange(*edges),
        *flux,
        hbm_out=(0,),
        scratch=(v, pltpu.SemaphoreType.DMA((3 * tracers,))),
    )


def solution(mesh):
    return jax.shard_map(
        body,
        mesh=mesh,
        in_specs=(
            P(None, None, "lat", "lon"),
            P(None, "lat", "lon"),
            P(None, None, None, "lat", "lon"),
            P(),
            P(None, ("lat", "lon"), None),
            P(None, ("lat", "lon")),
            P(None, ("lat", "lon")),
            P(None, None, ("lat", "lon")),
            P(None, ("lat", "lon")),
        ),
        out_specs=(P(None, None, "lat", "lon"), P(None, "lat", "lon")),
        check_vma=False,
    )
```
